32 devices in a mesh: head: 2 (over core), batch: 16 (over z, y, x).
Axes of the slice: x: 2, y: 2, z: 4, core: 2. Of those that a mesh axis runs over, the one named last changes fastest.
Arguments:
- inputs: bfloat16 [32, 512, 1024], P('batch', 'head'), may hold values from -6 to 6
- prior_scores: bfloat16 [32, 16, 512, 512], P('batch', 'head'), may hold values from -6 to 6
- lengths: int32 [32], P('batch'), may hold values from 65 to 512, as said below
- w_query: bfloat16 [1024, 1024], P(None, 'head'), may hold values from -0.1875 to 0.1875
- w_key: bfloat16 [1024, 1024], P(None, 'head'), may hold values from -0.1875 to 0.1875
- w_value: bfloat16 [1024, 1024], P(None, 'head'), may hold values from -0.1875 to 0.1875
- b_query: bfloat16 [1024], P('head'), may hold values from -3 to 3
- b_value: bfloat16 [1024], P('head'), may hold values from -2 to 2
- w_output: bfloat16 [1024, 1024], P('head'), may hold values from -1.5 to 1.5
- b_output: bfloat16 [1024], replicated, may hold values from -2 to 2
- gain_attn: bfloat16 [1024], replicated, may hold values from 0.5 to 1.5
- shift_attn: bfloat16 [1024], replicated, may hold values from -2 to 2
- w_inner: bfloat16 [1024, 4096], P(None, 'head'), may hold values from -0.1875 to 0.1875
- b_inner: bfloat16 [4096], P('head'), may hold values from -3 to 3
- w_outer: bfloat16 [4096, 1024], P('head'), may hold values from -0.09375 to 0.09375
- b_outer: bfloat16 [1024], replicated, may hold values from -2 to 2
- gain_ffn: bfloat16 [1024], replicated, may hold values from 0.5 to 1.5
- shift_ffn: bfloat16 [1024], replicated, may hold values from -2 to 2
- grad_out: bfloat16 [32, 512, 1024], P('batch', 'head'), may hold values from -6 to 6
- grad_scores: bfloat16 [32, 16, 512, 512], P('batch', 'head'), may hold values from -1.5 to 1.5
Outputs:
- outputs: bfloat16 [32, 512, 1024], P('batch', 'head')
- new_scores: bfloat16 [32, 16, 512, 512], P('batch', 'head')
- grad_inputs: bfloat16 [32, 512, 1024], P('batch', 'head')
- grad_prior: bfloat16 [32, 16, 512, 512], P('batch', 'head')
- grad_w_query: float32 [1024, 1024], P(None, 'head')
- grad_w_key: float32 [1024, 1024], P(None, 'head')
- grad_w_value: float32 [1024, 1024], P(None, 'head')
- grad_b_query: float32 [1024], P('head')
- grad_b_value: float32 [1024], P('head')
- grad_w_output: float32 [1024, 1024], P('head')
- grad_b_output: float32 [1024], replicated
- grad_gain_attn: float32 [1024], replicated
- grad_shift_attn: float32 [1024], replicated
- grad_w_inner: float32 [1024, 4096], P(None, 'head')
- grad_b_inner: float32 [4096], P('head')
- grad_w_outer: float32 [4096, 1024], P('head')
- grad_b_outer: float32 [1024], replicated
- grad_gain_ffn: float32 [1024], replicated
- grad_shift_ffn: float32 [1024], replicated
The draws below stay inside these ranges and needn't reach their ends.
Inputs may be any that keep to these rules, and one draw needn't show every extreme that they name: The 2 sequences of one index of batch all lie in one bucket B, one of 128, 256 and 512, with lengths from B/2 + 1 to B; some sequence has length 512.
All inputs are finite; a program needn't handle non-finite values.
Results may differ from the reference program's by a relative error of at most 0.018.
Values may be sent and summed in bfloat16 or wider, within the bound.
A program may use at most 256 MiB of HBM per device.

```python
import jax
import jax.numpy as jnp
from jax import lax

D = 1024
H = 16
HD = 64
FF = 4096
L = 512
SEQ_DEV = 2
SEQS = 32
N_HEAD = 2


def draw_lengths(key, part):
    groups = SEQS // SEQ_DEV
    key_level, key_group, key_pick, key_len = jax.random.split(jax.random.fold_in(key, 17), 4)
    level = jax.random.randint(key_level, (groups,), 0, 3)
    chosen = jax.random.randint(key_group, (), 0, groups)
    level = jnp.where(jnp.arange(groups) == chosen, 2, level)
    bucket_table = jnp.array([L // 4, L // 2, L], jnp.int32)
    bucket = jnp.sum(jnp.where(level[:, None] == jnp.arange(3)[None, :], bucket_table[None, :], 0), axis=1)
    per_seq = jnp.repeat(bucket, SEQ_DEV)
    low_end = per_seq // 2 + 1
    lengths = jax.random.randint(key_len, (SEQS,), low_end, per_seq + 1)
    longest = chosen * SEQ_DEV + jax.random.randint(key_pick, (), 0, SEQ_DEV)
    lengths = jnp.where(jnp.arange(SEQS) == longest, L, lengths)
    return lengths.astype(jnp.int32)


def level_of(key, dims, cuts, smallest, high):
    level, own = 1.0, jax.random.fold_in(key, 6)
    for axis_at, shards_of in cuts:
        draws = jnp.exp(jax.random.uniform(jax.random.fold_in(own, axis_at), (shards_of,), jnp.float32, smallest / len(cuts), high / len(cuts)))
        level = level * jnp.repeat(draws, dims[axis_at] // shards_of).reshape([-1 if axis == axis_at else 1 for axis in range(len(dims))])
    return level


def gaussian(key, shape, spread, bound, shards=(), held_as=jnp.bfloat16):
    factor_of = level_of(key, shape, shards, -0.22, 0.18) if shards else 1.0
    result = jax.random.normal(key, shape, jnp.float32) * spread * factor_of
    return jnp.minimum(jnp.maximum(result, -bound), bound).astype(held_as)


def setup_inputs(seed: int = 0) -> dict:
    streams_of = jax.random.split(jax.random.key(seed), 21)
    inputs = gaussian(streams_of[0], (SEQS, L, D), 1.0, 6.0, ((0, 16), (1, 2)))
    prior_scores = gaussian(streams_of[1], (SEQS, H, L, L), 1.0, 6.0, ((0, 16), (1, 2)))
    lengths = draw_lengths(jax.random.fold_in(streams_of[20], 71), 0)
    w_query = gaussian(streams_of[3], (D, D), D ** -0.5, 0.1875, ((1, 2),))
    w_key = gaussian(streams_of[4], (D, D), D ** -0.5, 0.1875, ((1, 2),))
    w_value = gaussian(streams_of[5], (D, D), D ** -0.5, 0.1875, ((1, 2),))
    b_query = gaussian(streams_of[6], (D,), 0.5, 3.0, ((0, 2),))
    b_value = gaussian(streams_of[7], (D,), 0.3, 2.0, ((0, 2),))
    w_output = gaussian(streams_of[8], (D, D), (D // 64) ** -0.5, 1.5, ((0, 2),))
    b_output = gaussian(streams_of[9], (D,), 0.3, 2.0)
    gain_attn = jnp.clip(1.0 + 0.1 * jax.random.normal(streams_of[10], (D,), jnp.float32), 0.5, 1.5).astype(jnp.bfloat16)
    shift_attn = gaussian(streams_of[11], (D,), 0.3, 2.0)
    w_inner = gaussian(streams_of[12], (D, FF), D ** -0.5, 0.1875, ((1, 2),))
    b_inner = gaussian(streams_of[13], (FF,), 0.5, 3.0, ((0, 2),))
    w_outer = gaussian(streams_of[14], (FF, D), FF ** -0.5, 0.09375, ((0, 2),))
    b_outer = gaussian(streams_of[15], (D,), 0.3, 2.0)
    gain_ffn = jnp.clip(1.0 + 0.1 * jax.random.normal(streams_of[16], (D,), jnp.float32), 0.5, 1.5).astype(jnp.bfloat16)
    shift_ffn = gaussian(streams_of[17], (D,), 0.3, 2.0)
    grad_out = gaussian(streams_of[18], (SEQS, L, D), 1.0, 6.0, ((0, 16), (1, 2)))
    grad_scores = gaussian(streams_of[19], (SEQS, H, L, L), 0.25, 1.5, ((0, 16), (1, 2)))
    return {"inputs": inputs, "prior_scores": prior_scores, "lengths": lengths, "w_query": w_query, "w_key": w_key, "w_value": w_value, "b_query": b_query, "b_value": b_value, "w_output": w_output, "b_output": b_output, "gain_attn": gain_attn, "shift_attn": shift_attn, "w_inner": w_inner, "b_inner": b_inner, "w_outer": w_outer, "b_outer": b_outer, "gain_ffn": gain_ffn, "shift_ffn": shift_ffn, "grad_out": grad_out, "grad_scores": grad_scores}


EPS = 1e-12
NEG = -1e+30
HIGH = lax.Precision.HIGHEST

@jax.custom_vjp
def low(v):
    return lax.optimization_barrier(v.astype(jnp.bfloat16)).astype(jnp.float32)

@jax.custom_vjp
def low_back(v):
    return v

def low_keep(v):
    return (low(v), None)

def low_pass(kept, grad):
    return (grad,)

def back_keep(v):
    return (v, None)

def back_low(kept, grad):
    return (low(grad),)
low.defvjp(low_keep, low_pass)
low_back.defvjp(back_keep, back_low)

def layer_norm(values, norm_gain, norm_shift):
    row_mean = lax.optimization_barrier(jnp.mean(values, axis=-1, keepdims=True))
    centred = values - row_mean
    row_var = lax.optimization_barrier(jnp.mean(centred * centred, axis=-1, keepdims=True))
    return centred * lax.rsqrt(row_var + EPS) * norm_gain + norm_shift

def product(left_side, right_side):
    return jnp.dot(left_side, right_side, precision=HIGH)

def grouped_sum(left_side, right_side):
    left_groups = left_side.reshape(left_side.shape[0], N_HEAD, left_side.shape[1] // N_HEAD)
    right_groups = right_side.reshape(N_HEAD, right_side.shape[0] // N_HEAD, right_side.shape[1])
    partials = jnp.einsum('lgc,gcd->gld', left_groups, right_groups, precision=HIGH)
    return lax.optimization_barrier(jnp.sum(low(low_back(partials)), axis=0))

def sequence_forward(params, inputs_seq, prior_seq, length):
    w_query, w_key, w_value, b_query, b_value, w_output, b_output, gain_attn, shift_attn, w_inner, b_inner, w_outer, b_outer, gain_ffn, shift_ffn = params
    query_rows = low(low_back(product(inputs_seq, w_query) + b_query))
    key_rows = low(low_back(product(inputs_seq, w_key)))
    value_rows = low(low_back(product(inputs_seq, w_value) + b_value))
    query_heads = query_rows.reshape(L, H, HD)
    key_heads = key_rows.reshape(L, H, HD)
    value_heads = value_rows.reshape(L, H, HD)
    raw_scores = jnp.einsum('qhe,khe->hqk', query_heads, key_heads, precision=HIGH)
    scores = low_back(raw_scores * HD ** (-0.5) + prior_seq)
    live_keys = jnp.arange(L) < length
    masked = jnp.where(live_keys[None, None, :], scores, NEG)
    attn_probs = low(jax.nn.softmax(masked, axis=-1))
    context = low(low_back(jnp.einsum('hqk,khe->qhe', attn_probs, value_heads, precision=HIGH))).reshape(L, D)
    pre_attn = grouped_sum(context, w_output) + b_output + inputs_seq
    hidden = layer_norm(pre_attn, gain_attn, shift_attn)
    inner_pre = low_back(product(low(hidden), w_inner) + b_inner)
    inner_act = low(low_back(jax.nn.gelu(inner_pre, approximate=False)))
    pre_ffn = grouped_sum(inner_act, w_outer) + b_outer + hidden
    return (layer_norm(pre_ffn, gain_ffn, shift_ffn), scores)

def reference(inputs, prior_scores, lengths, w_query, w_key, w_value, b_query, b_value, w_output, b_output, gain_attn, shift_attn, w_inner, b_inner, w_outer, b_outer, gain_ffn, shift_ffn, grad_out, grad_scores):
    params = tuple((weight.astype(jnp.float32) for weight in (w_query, w_key, w_value, b_query, b_value, w_output, b_output, gain_attn, shift_attn, w_inner, b_inner, w_outer, b_outer, gain_ffn, shift_ffn)))

    def seq_step(running, seq_item):
        inputs_seq, prior_seq, length, grad_seq_out, grad_seq_scores = seq_item

        def forward(param_set, inputs_rows, prior_rows):
            return sequence_forward(param_set, inputs_rows, prior_rows, length)
        (out_rows, score_rows), pull_back = jax.vjp(forward, params, inputs_seq.astype(jnp.float32), prior_seq.astype(jnp.float32))
        param_grads, grad_seq, grad_prior_seq = pull_back((grad_seq_out.astype(jnp.float32), grad_seq_scores.astype(jnp.float32)))
        running = jax.tree.map(jnp.add, running, param_grads)
        return (running, (out_rows.astype(jnp.bfloat16), score_rows.astype(jnp.bfloat16), grad_seq.astype(jnp.bfloat16), grad_prior_seq.astype(jnp.bfloat16)))
    zero_grads = tuple((jnp.zeros(weight.shape, jnp.float32) for weight in params))
    totals, (outputs, new_scores, grad_inputs, grad_prior) = lax.scan(seq_step, zero_grads, (inputs, prior_scores, lengths, grad_out, grad_scores))
    return (outputs, new_scores, grad_inputs, grad_prior) + tuple(totals)
```

```python
import functools

import jax
import jax.numpy as jnp
from jax import lax
from jax.sharding import PartitionSpec as P

from jax.experimental import pallas as pl
from jax.experimental.pallas import tpu as pltpu

MESH = pl.DeviceIdType.MESH
F32, BF16 = jnp.float32, jnp.bfloat16


def grid_bits(n):
    bits = n.bit_length() - 1
    side = bits // 3
    return (0, side, 2 * side), bits


def chunk_plan(n, color):
    (bx, by, bz), bits = grid_bits(n)
    order = ((bx, by, bz), (by, bx, bz), (bz, bx, by), (bz, by, bx))[color]
    rest = [b for b in range(bits) if b not in order]
    stages = [("scatter", b) for b in order] + [("double", b) for b in rest]
    stages += [("gather", b) for b in reversed(order)]
    return stages


def event_order(n, colors, rows):
    (bx, by, bz), bits = grid_bits(n)
    axis = lambda b: 0 if b < by else 1 if b < bz else 2
    hop = lambda b: 1 << (b - (bx, by, bz)[axis(b)])
    free = [0.0, 0.0, 0.0]
    ready = [0.0] * len(colors)
    plans = [chunk_plan(n, c) for c in colors]
    step = [0] * len(colors)
    length = [1.0] * len(colors)
    events = []
    total = sum(len(p) for p in plans)
    while len(events) < total:
        best = None
        for c, plan in enumerate(plans):
            if step[c] == len(plan):
                continue
            kind, b = plan[step[c]]
            start = max(ready[c], free[axis(b)])
            key = (start, -step[c], c)
            if best is None or key < best[0]:
                best = (key, c)
        (start, _, _), c = best
        kind, b = plans[c][step[c]]
        if kind == "scatter":
            length[c] /= 2
        span = length[c] * (min(hop(b), 2))
        if kind == "gather":
            length[c] *= 2
        free[axis(b)] = start + span
        ready[c] = start + span + 0.08
        events.append((start, c, step[c]))
        step[c] += 1
    events.sort()
    return [(c, s) for _, c, s in events], max(ready)


def flip(index, bit):
    return index + (1 - 2 * ((index // (1 << bit)) % 2)) * (1 << bit)


def reduce_kernel(n, colors, rows, g_hbm, out_hbm, work, got, full, load_sem, save_sem, send_sem, recv_sem):
    nc = len(colors)
    me = lax.axis_index("batch")
    (bx, by, bz), bits = grid_bits(n)
    for c in range(nc):
        pltpu.make_async_copy(g_hbm.at[c], work.at[c], load_sem.at[c]).start()
    barrier = pltpu.get_barrier_semaphore()
    for b in range(bits):
        pl.semaphore_signal(barrier, inc=1, device_id={"batch": flip(me, b)}, device_id_type=MESH)
    pl.semaphore_wait(barrier, bits)

    plans = [chunk_plan(n, c) for c in colors]
    events, _ = event_order(n, colors, rows)
    bit_of = [(me // (1 << b)) % 2 for b in range(bits)]
    spans = []
    for c in range(nc):
        off, length, at = 0, rows, 0
        row = []
        for kind, b in plans[c]:
            if kind == "scatter":
                half = length // 2
                keep = off + bit_of[b] * half
                give = off + (1 - bit_of[b]) * half
                row.append((keep, give, half, at))
                off, length, at = keep, half, at + half
            elif kind == "double":
                row.append((off, off, length, at))
                at += length
            else:
                row.append((off, off, length, None))
                off = off - bit_of[b] * length
                length = 2 * length
        spans.append(row)

    def copy_of(c, s):
        kind, b = plans[c][s]
        keep, give, length, at = spans[c][s]
        place = (c, pl.ds(pl.multiple_of(give, 16), length))
        if kind == "gather":
            src, dst = full.at[place], full.at[place]
        else:
            src, dst = work.at[place], got.at[c, pl.ds(at, length)]
        return pltpu.make_async_remote_copy(
            src_ref=src, dst_ref=dst, send_sem=send_sem.at[c, s], recv_sem=recv_sem.at[c, s],
            device_id={"batch": flip(me, b)}, device_id_type=MESH)

    def finish(c, s):
        kind, b = plans[c][s]
        keep, give, length, at = spans[c][s]
        copy_of(c, s).wait()
        if kind != "gather":
            target = full if plans[c][s + 1][0] == "gather" else work

            def add(i, _):
                r = pl.multiple_of(keep + i * 16, 16)
                q = pl.multiple_of(at + i * 16, 16)
                target[c, pl.ds(r, 16), :] = (work[c, pl.ds(r, 16), :].astype(F32) + got[c, pl.ds(q, 16), :].astype(F32)).astype(BF16)
                return 0
            lax.fori_loop(0, length // 16, add, 0)

    for c, s in events:
        if s == 0:
            pltpu.make_async_copy(g_hbm.at[c], work.at[c], load_sem.at[c]).wait()
        else:
            finish(c, s - 1)
        copy_of(c, s).start()
    for c in range(nc):
        finish(c, len(plans[c]) - 1)
        pltpu.make_async_copy(full.at[c], out_hbm.at[c], save_sem.at[c]).start()
    for c in range(nc):
        pltpu.make_async_copy(full.at[c], out_hbm.at[c], save_sem.at[c]).wait()


def all_reduce(g, n, colors):
    nc, rows, cols = g.shape
    stages = len(chunk_plan(n, 0))
    _, bits = grid_bits(n)
    got_rows = rows - rows // 8 + (bits - 3) * rows // 8
    return pl.pallas_call(
        functools.partial(reduce_kernel, n, colors, rows),
        out_shape=jax.ShapeDtypeStruct(g.shape, g.dtype),
        in_specs=[pl.BlockSpec(memory_space=pl.ANY)],
        out_specs=pl.BlockSpec(memory_space=pl.ANY),
        scratch_shapes=[
            pltpu.VMEM(g.shape, BF16), pltpu.VMEM((nc, got_rows, cols), BF16), pltpu.VMEM(g.shape, BF16),
            pltpu.SemaphoreType.DMA((nc,)), pltpu.SemaphoreType.DMA((nc,)),
            pltpu.SemaphoreType.DMA((nc, stages)), pltpu.SemaphoreType.DMA((nc, stages)),
        ],
        compiler_params=pltpu.CompilerParams(collective_id=0, has_side_effects=True, vmem_limit_bytes=60 << 20),
        name="reduce_gradients",
    )(g)


MB = 1


EPS = 1e-12
NEG = -1e30


def layer_norm(values, norm_gain, norm_shift):
    row_mean = jnp.mean(values, axis=-1, keepdims=True)
    centred = values - row_mean
    row_var = jnp.mean(centred * centred, axis=-1, keepdims=True)
    return centred * lax.rsqrt(row_var + EPS) * norm_gain + norm_shift


def project(left_side, right_side):
    return jnp.dot(left_side, right_side, preferred_element_type=jnp.float32)


def project_back(left_side, right_side):
    return jnp.einsum("sla,ba->slb", left_side, right_side, preferred_element_type=jnp.float32)


def outer_sum(left_side, right_side):
    return jnp.einsum("sla,slb->ab", left_side, right_side, preferred_element_type=jnp.float32)


def gelu_slope(inner_pre):
    cdf_part = 0.5 * (1.0 + lax.erf(inner_pre * 0.7071067811865476))
    density = jnp.exp(-0.5 * inner_pre * inner_pre) * 0.3989422804014327
    return cdf_part + inner_pre * density


def masked_scores(query_heads, key_heads, prior_block, live_keys, score_scale):
    raw_scores = jnp.einsum(
        "sqhe,skhe->shqk", query_heads, key_heads, preferred_element_type=jnp.float32
    )
    scores = raw_scores * score_scale + prior_block.astype(jnp.float32)
    masked = jnp.where(live_keys[:, None, None, :], scores, NEG)
    return (scores, masked)


def on_device(
    n_batch,
    inputs,
    prior_scores,
    lengths,
    w_query,
    w_key,
    w_value,
    b_query,
    b_value,
    w_output,
    b_output,
    gain_attn,
    shift_attn,
    w_inner,
    b_inner,
    w_outer,
    b_outer,
    gain_ffn,
    shift_ffn,
    grad_out,
    grad_scores,
):
    micro_seqs = inputs.shape[0] // MB
    full_len = prior_scores.shape[-1]
    heads_local = prior_scores.shape[1]
    head_size = w_query.shape[1] // heads_local
    score_scale = head_size ** (-0.5)
    positions = jnp.arange(full_len)
    head_shape = (micro_seqs, full_len, heads_local, head_size)
    bias_query = b_query.astype(jnp.float32)
    bias_value = b_value.astype(jnp.float32)
    bias_output = b_output.astype(jnp.float32)
    bias_inner = b_inner.astype(jnp.float32)
    bias_outer = b_outer.astype(jnp.float32)
    norm_gain_a = gain_attn.astype(jnp.float32)
    norm_shift_a = shift_attn.astype(jnp.float32)
    norm_gain_f = gain_ffn.astype(jnp.float32)
    norm_shift_f = shift_ffn.astype(jnp.float32)
    weight_totals = tuple(
        (
            jnp.zeros(weight.shape, jnp.float32)
            for weight in (
                w_query,
                w_key,
                w_value,
                b_query,
                b_value,
                w_output,
                w_inner,
                b_inner,
                w_outer,
            )
        )
    )
    small_totals = tuple(
        (
            jnp.zeros(weight.shape, jnp.float32)
            for weight in (b_output, gain_attn, shift_attn, b_outer, gain_ffn, shift_ffn)
        )
    )
    out_list, score_list, grad_in_list, grad_prior_list = ([], [], [], [])
    for micro_index in range(MB):
        first_seq = micro_index * micro_seqs
        inputs_mb = inputs[first_seq : first_seq + micro_seqs]
        prior_mb = prior_scores[first_seq : first_seq + micro_seqs]
        live_keys = positions[None, :] < lengths[first_seq : first_seq + micro_seqs][:, None]
        gathered = lax.all_gather(inputs_mb, "head", axis=1, tiled=True)
        query_rows = (project(gathered, w_query) + bias_query).astype(jnp.bfloat16)
        key_rows = project(gathered, w_key).astype(jnp.bfloat16)
        value_rows = (project(gathered, w_value) + bias_value).astype(jnp.bfloat16)
        query_heads = query_rows.reshape(head_shape)
        key_heads = key_rows.reshape(head_shape)
        value_heads = value_rows.reshape(head_shape)
        scores, masked = masked_scores(query_heads, key_heads, prior_mb, live_keys, score_scale)
        row_max = jnp.max(masked, axis=-1, keepdims=True)
        exp_terms = jnp.exp(masked - row_max)
        row_total = jnp.sum(exp_terms, axis=-1, keepdims=True)
        attn_probs = (exp_terms / row_total).astype(jnp.bfloat16)
        log_total = row_max + jnp.log(row_total)
        context = jnp.einsum(
            "shqk,skhe->sqhe", attn_probs, value_heads, preferred_element_type=jnp.float32
        ).astype(jnp.bfloat16)
        context = context.reshape(micro_seqs, full_len, heads_local * head_size)
        attn_sum = lax.psum_scatter(
            project(context, w_output).astype(jnp.bfloat16), "head", scatter_dimension=1, tiled=True
        ).astype(jnp.float32)
        pre_attn = attn_sum + bias_output + inputs_mb.astype(jnp.float32)
        hidden = layer_norm(pre_attn, norm_gain_a, norm_shift_a)
        hidden_rows = lax.all_gather(hidden.astype(jnp.bfloat16), "head", axis=1, tiled=True)
        inner_pre = project(hidden_rows, w_inner) + bias_inner
        inner_act = jax.nn.gelu(inner_pre, approximate=False).astype(jnp.bfloat16)
        ffn_sum = lax.psum_scatter(
            project(inner_act, w_outer).astype(jnp.bfloat16),
            "head",
            scatter_dimension=1,
            tiled=True,
        ).astype(jnp.float32)
        pre_ffn = ffn_sum + bias_outer + hidden
        out_list.append(layer_norm(pre_ffn, norm_gain_f, norm_shift_f).astype(jnp.bfloat16))
        score_list.append(scores.astype(jnp.bfloat16))
        grad_mb = grad_out[first_seq : first_seq + micro_seqs].astype(jnp.float32)
        unused_ffn, pull_ffn = jax.vjp(layer_norm, pre_ffn, norm_gain_f, norm_shift_f)
        grad_pre_ffn, grad_gain_f, grad_shift_f = pull_ffn(grad_mb)
        grad_ffn_rows = lax.all_gather(
            grad_pre_ffn.astype(jnp.bfloat16), "head", axis=1, tiled=True
        )
        grad_act = project_back(grad_ffn_rows, w_outer).astype(jnp.bfloat16)
        grad_inner = (grad_act.astype(jnp.float32) * gelu_slope(inner_pre)).astype(jnp.bfloat16)
        grad_hidden = grad_pre_ffn + lax.psum_scatter(
            project_back(grad_inner, w_inner).astype(jnp.bfloat16),
            "head",
            scatter_dimension=1,
            tiled=True,
        ).astype(jnp.float32)
        unused_attn, pull_attn = jax.vjp(layer_norm, pre_attn, norm_gain_a, norm_shift_a)
        grad_pre_attn, grad_gain_a, grad_shift_a = pull_attn(grad_hidden)
        grad_attn_rows = lax.all_gather(
            grad_pre_attn.astype(jnp.bfloat16), "head", axis=1, tiled=True
        )
        grad_context = (
            project_back(grad_attn_rows, w_output).astype(jnp.bfloat16).reshape(head_shape)
        )
        unused_scores, masked_again = masked_scores(
            query_heads, key_heads, prior_mb, live_keys, score_scale
        )
        probs_again = jnp.exp(masked_again - log_total)
        grad_probs = jnp.einsum(
            "sqhe,skhe->shqk", grad_context, value_heads, preferred_element_type=jnp.float32
        )
        row_delta = jnp.sum(probs_again * grad_probs, axis=-1, keepdims=True)
        grad_raw = probs_again * (grad_probs - row_delta) + grad_scores[
            first_seq : first_seq + micro_seqs
        ].astype(jnp.float32)
        grad_raw_low = grad_raw.astype(jnp.bfloat16)
        grad_prior_list.append(grad_raw_low)
        grad_query = (
            jnp.einsum(
                "shqk,skhe->sqhe", grad_raw_low, key_heads, preferred_element_type=jnp.float32
            )
            * score_scale
        ).astype(jnp.bfloat16)
        grad_key = (
            jnp.einsum(
                "shqk,sqhe->skhe", grad_raw_low, query_heads, preferred_element_type=jnp.float32
            )
            * score_scale
        ).astype(jnp.bfloat16)
        grad_value = jnp.einsum(
            "shqk,sqhe->skhe", attn_probs, grad_context, preferred_element_type=jnp.float32
        ).astype(jnp.bfloat16)
        flat_shape = (micro_seqs, full_len, heads_local * head_size)
        grad_query = grad_query.reshape(flat_shape)
        grad_key = grad_key.reshape(flat_shape)
        grad_value = grad_value.reshape(flat_shape)
        grad_gathered = (
            project_back(grad_query, w_query)
            + project_back(grad_key, w_key)
            + project_back(grad_value, w_value)
        )
        grad_rows = grad_pre_attn + lax.psum_scatter(
            grad_gathered.astype(jnp.bfloat16), "head", scatter_dimension=1, tiled=True
        ).astype(jnp.float32)
        grad_in_list.append(grad_rows.astype(jnp.bfloat16))
        micro_grads = (
            outer_sum(gathered, grad_query),
            outer_sum(gathered, grad_key),
            outer_sum(gathered, grad_value),
            jnp.sum(grad_query.astype(jnp.float32), axis=(0, 1)),
            jnp.sum(grad_value.astype(jnp.float32), axis=(0, 1)),
            outer_sum(context, grad_attn_rows),
            outer_sum(hidden_rows, grad_inner),
            jnp.sum(grad_inner.astype(jnp.float32), axis=(0, 1)),
            outer_sum(inner_act, grad_ffn_rows),
        )
        micro_small = (
            jnp.sum(grad_pre_attn, axis=(0, 1)),
            grad_gain_a,
            grad_shift_a,
            jnp.sum(grad_pre_ffn, axis=(0, 1)),
            grad_gain_f,
            grad_shift_f,
        )
        weight_totals = jax.tree.map(jnp.add, weight_totals, micro_grads)
        small_totals = jax.tree.map(jnp.add, small_totals, micro_small)
    low = [total.astype(jnp.bfloat16) for total in weight_totals]
    width = inputs.shape[2]
    packed = jnp.concatenate([
        jnp.concatenate([low[0], low[1]], axis=1),
        low[2].reshape(-1, width), low[5],
        low[6].reshape(-1, width), low[8]], axis=0)
    colors = (0, 1) * 12
    done = all_reduce(packed.reshape(len(colors), -1, width), n_batch, colors)
    done = done.reshape(-1, width).astype(jnp.float32)
    sizes = [low[0].shape[0], low[2].size // width, low[5].shape[0], low[6].size // width, low[8].shape[0]]
    starts = [sum(sizes[:i]) for i in range(6)]
    part = [done[starts[i]:starts[i + 1]] for i in range(5)]
    half = low[0].shape[1]
    final_b = lax.psum((weight_totals[3], weight_totals[4], weight_totals[7]), "batch")
    final_grads = (part[0][:, :half], part[0][:, half:], part[1].reshape(low[2].shape),
                   final_b[0], final_b[1], part[2], part[3].reshape(low[6].shape), final_b[2], part[4])
    final_small = lax.psum(small_totals, ("head", "batch"))
    (
        grad_w_query,
        grad_w_key,
        grad_w_value,
        grad_b_query,
        grad_b_value,
        grad_w_output,
        grad_w_inner,
        grad_b_inner,
        grad_w_outer,
    ) = final_grads
    grad_b_output, grad_gain_attn, grad_shift_attn, grad_b_outer, grad_gain_ffn, grad_shift_ffn = (
        final_small
    )
    return (
        jnp.concatenate(out_list, axis=0),
        jnp.concatenate(score_list, axis=0),
        jnp.concatenate(grad_in_list, axis=0),
        jnp.concatenate(grad_prior_list, axis=0),
        grad_w_query,
        grad_w_key,
        grad_w_value,
        grad_b_query,
        grad_b_value,
        grad_w_output,
        grad_b_output,
        grad_gain_attn,
        grad_shift_attn,
        grad_w_inner,
        grad_b_inner,
        grad_w_outer,
        grad_b_outer,
        grad_gain_ffn,
        grad_shift_ffn,
    )


def solution(mesh):
    in_specs = (
        P("batch", "head", None),
        P("batch", "head", None, None),
        P("batch"),
        P(None, "head"),
        P(None, "head"),
        P(None, "head"),
        P("head"),
        P("head"),
        P("head", None),
        P(),
        P(),
        P(),
        P(None, "head"),
        P("head"),
        P("head", None),
        P(),
        P(),
        P(),
        P("batch", "head", None),
        P("batch", "head", None, None),
    )
    out_specs = (
        P("batch", "head", None),
        P("batch", "head", None, None),
        P("batch", "head", None),
        P("batch", "head", None, None),
        P(None, "head"),
        P(None, "head"),
        P(None, "head"),
        P("head"),
        P("head"),
        P("head", None),
        P(),
        P(),
        P(),
        P(None, "head"),
        P("head"),
        P("head", None),
        P(),
        P(),
        P(),
    )
    return jax.shard_map(
        functools.partial(on_device, mesh.shape["batch"]), mesh=mesh, in_specs=in_specs, out_specs=out_specs, check_vma=False
    )
```

```python
import functools
import jax, jax.numpy as jnp
from jax import lax
from jax.experimental import pallas as pl
from jax.experimental.pallas import tpu as pltpu
from jax.sharding import PartitionSpec as P

MESH = pl.DeviceIdType.MESH
F32, BF16 = jnp.float32, jnp.bfloat16
EPS = 1e-12
NEG = -1e30
LIMIT = 64 * 1000 * 1000


def dot(a, b):
    return jnp.dot(a, b, preferred_element_type=F32)


def dot_t(a, b):
    return lax.dot_general(a, b, (((1,), (1,)), ((), ())), preferred_element_type=F32)


def t_dot(a, b):
    return lax.dot_general(a, b, (((0,), (0,)), ((), ())), preferred_element_type=F32)


def meet(partner):
    barrier = pltpu.get_barrier_semaphore()
    pl.semaphore_signal(barrier, inc=1, device_id={"head": partner}, device_id_type=MESH)
    pl.semaphore_wait(barrier, 1)


def to_partner(src, dst, sems, i, partner):
    return pltpu.make_async_remote_copy(
        src_ref=src, dst_ref=dst, send_sem=sems.at[0, i], recv_sem=sems.at[1, i],
        device_id={"head": partner}, device_id_type=MESH)


def vmem(count):
    return [pl.BlockSpec(memory_space=pltpu.VMEM)] * count


def project_kernel(seqs, part, x, wq, wk, wv, bias, rows, q, k, v, got, sems):
    me = lax.axis_index("head")
    other = 1 - me
    meet(other)
    for s in range(seqs):
        to_partner(x.at[s], got.at[s], sems, s, other).start()

    def emit(block, s, p):
        at = pl.ds(pl.multiple_of((2 * s + p) * part, part), part)
        rows[at, :] = block
        q[at, :] = (dot(block, wq[...]) + bias[0:1, :]).astype(BF16)
        k[at, :] = dot(block, wk[...]).astype(BF16)
        v[at, :] = (dot(block, wv[...]) + bias[1:2, :]).astype(BF16)

    def own(s, _):
        emit(x[s], s, me)
        return 0

    lax.fori_loop(0, seqs, own, 0)
    for s in range(seqs):
        to_partner(x.at[s], got.at[s], sems, s, other).wait()

    def theirs(s, _):
        emit(got[s], s, other)
        return 0

    lax.fori_loop(0, seqs, theirs, 0)


def project_rows(x, wq, wk, wv, bias):
    seqs, part, width = x.shape
    total, cols = 2 * seqs * part, wq.shape[1]
    out = jax.ShapeDtypeStruct((total, cols), BF16)
    return pl.pallas_call(
        functools.partial(project_kernel, seqs, part),
        out_shape=(jax.ShapeDtypeStruct((total, width), BF16), out, out, out),
        in_specs=vmem(5), out_specs=tuple(vmem(4)),
        scratch_shapes=[pltpu.VMEM(x.shape, BF16), pltpu.SemaphoreType.DMA((2, seqs))],
        compiler_params=pltpu.CompilerParams(collective_id=1, has_side_effects=True, vmem_limit_bytes=LIMIT),
        name="project_rows",
    )(x, wq, wk, wv, bias)


def attend_kernel(block, head, lengths, q, k, v, prior, score, c, norm):
    full = k.shape[0]
    live = lax.broadcasted_iota(jnp.int32, (1, full), 1) < lengths[pl.program_id(0)]
    first = lax.broadcasted_iota(jnp.int32, (1, 2 * head), 1) < head
    scale = head ** -0.5
    for r in range(0, full, block):
        rows = pl.ds(r, block)
        queries = q[rows, :]
        parts, norms = [], []
        for h in range(2):
            mine = jnp.where(first == (h == 0), queries, jnp.zeros_like(queries))
            scores = dot_t(mine, k[...]) * scale + prior[0, h, rows, :].astype(F32)
            score[0, h, rows, :] = scores.astype(BF16)
            masked = jnp.where(live, scores, NEG)
            top = jnp.max(masked, axis=-1, keepdims=True)
            terms = jnp.exp(masked - top)
            total = jnp.sum(terms, axis=-1, keepdims=True)
            probs = (terms * (1.0 / total)).astype(BF16)
            parts.append(dot(probs, v[...]))
            norms.append(top + jnp.log(total))
        c[rows, :] = jnp.where(first, parts[0], parts[1]).astype(BF16)
        norm[0, 0, rows, :] = jnp.where(first, norms[0], norms[1])


def attend(lengths, q, k, v, prior):
    seqs, heads, full, _ = prior.shape
    pair = q.shape[1] // heads * 2
    rows = pl.BlockSpec((full, pair), lambda s, h, n: (s, h))
    big = pl.BlockSpec((1, 2, full, full), lambda s, h, n: (s, h, 0, 0))
    norm = pl.BlockSpec((1, 1, full, pair), lambda s, h, n: (s, h, 0, 0))
    return pl.pallas_call(
        functools.partial(attend_kernel, 256, pair // 2),
        grid_spec=pltpu.PrefetchScalarGridSpec(
            num_scalar_prefetch=1, grid=(seqs, heads // 2),
            in_specs=[rows, rows, rows, big], out_specs=(big, rows, norm)),
        out_shape=(jax.ShapeDtypeStruct(prior.shape, BF16), jax.ShapeDtypeStruct(q.shape, BF16),
                   jax.ShapeDtypeStruct((seqs, heads // 2, full, pair), F32)),
        compiler_params=pltpu.CompilerParams(vmem_limit_bytes=40 << 20),
        name="attend",
    )(lengths, q, k, v, prior)


def attend_back_kernel(block, head, lengths, q, k, v, dc, prior, norm, given, grad, dq, dk, dv):
    full = k.shape[0]
    live = lax.broadcasted_iota(jnp.int32, (1, full), 1) < lengths[pl.program_id(0)]
    first = lax.broadcasted_iota(jnp.int32, (1, 2 * head), 1) < head
    scale = head ** -0.5
    q_t, dc_t = q[...].T, dc[...].T
    dk_t, dv_t = [0.0, 0.0], [0.0, 0.0]
    for r in range(0, full, block):
        rows = pl.ds(r, block)
        queries, cots = q[rows, :], dc[rows, :]
        parts = []
        for h in range(2):
            mine = first == (h == 0)
            scores = dot_t(jnp.where(mine, queries, jnp.zeros_like(queries)), k[...]) * scale
            scores = scores + prior[0, h, rows, :].astype(F32)
            probs = jnp.exp(jnp.where(live, scores, NEG) - norm[0, 0, rows, h * head:h * head + 1])
            dp = dot_t(jnp.where(mine, cots, jnp.zeros_like(cots)), v[...])
            delta = jnp.sum(probs * dp, axis=-1, keepdims=True)
            ds = (probs * (dp - delta) + given[0, h, rows, :].astype(F32)).astype(BF16)
            grad[0, h, rows, :] = ds
            parts.append(dot(ds, k[...]))
            lanes = slice(h * head, (h + 1) * head)
            dk_t[h] = dk_t[h] + dot(q_t[lanes, r:r + block], ds)
            dv_t[h] = dv_t[h] + dot(dc_t[lanes, r:r + block], probs.astype(BF16))
        dq[rows, :] = (jnp.where(first, parts[0], parts[1]) * scale).astype(BF16)
    dk[...] = (jnp.concatenate(dk_t, axis=0) * scale).T.astype(BF16)
    dv[...] = jnp.concatenate(dv_t, axis=0).T.astype(BF16)


def attend_back(lengths, q, k, v, dc, prior, norm, given):
    seqs, heads, full, _ = prior.shape
    pair = q.shape[1] // heads * 2
    rows = pl.BlockSpec((full, pair), lambda s, h, n: (s, h))
    big = pl.BlockSpec((1, 2, full, full), lambda s, h, n: (s, h, 0, 0))
    norms = pl.BlockSpec((1, 1, full, pair), lambda s, h, n: (s, h, 0, 0))
    flat = jax.ShapeDtypeStruct(q.shape, BF16)
    return pl.pallas_call(
        functools.partial(attend_back_kernel, 256, pair // 2),
        grid_spec=pltpu.PrefetchScalarGridSpec(
            num_scalar_prefetch=1, grid=(seqs, heads // 2),
            in_specs=[rows, rows, rows, rows, big, norms, big], out_specs=(big, rows, rows, rows)),
        out_shape=(jax.ShapeDtypeStruct(prior.shape, BF16), flat, flat, flat),
        compiler_params=pltpu.CompilerParams(vmem_limit_bytes=40 << 20),
        name="attend_back",
    )(lengths, q, k, v, dc, prior, norm, given)


def fold(value):
    return jnp.sum(value.reshape(value.shape[0] // 8, 8, value.shape[1]), axis=0)


def norm_stats(z):
    mean = jnp.mean(z, axis=-1, keepdims=True)
    centred = z - mean
    r = lax.rsqrt(jnp.mean(centred * centred, axis=-1, keepdims=True) + EPS)
    return centred * r, r


def norm_back(cot, gain, unit, r):
    e = cot * gain
    return r * (e - jnp.mean(e, axis=-1, keepdims=True) - unit * jnp.mean(e * unit, axis=-1, keepdims=True))


def middle_kernel(seqs, part, c, x, wo, wi, wf, vec, b_inner, gout,
                  out, dz1, dc, g_wo, g_wi, g_wf, small, g_bi,
                  unit1, r1, dz2, hn, act, slope, df, du, da, give, got, own, sums, bsum, sems):
    me = lax.axis_index("head")
    other = 1 - me
    width = x.shape[2]
    hidden = wi.shape[1]
    tile = 512
    sub = 64
    meet(other)
    b_output, gain1, shift1, b_outer, gain2, shift2 = [vec[i:i + 1, :] for i in range(6)]
    sums[...] = jnp.zeros_like(sums)
    bsum[...] = jnp.zeros_like(bsum)

    def rows_of(s, p):
        return pl.ds(pl.multiple_of((2 * s + p) * part, part), part)

    def at(start, size):
        return pl.ds(pl.multiple_of(start, size), size)

    def attn_part(s, _):
        give[s] = dot(c[rows_of(s, other), :], wo[...]).astype(BF16)
        return 0
    for s in range(seqs):
        attn_part(s, 0)
        to_partner(give.at[s], got.at[0, s], sems, s, other).start()

    def attn_own(s, _):
        own[s] = dot(c[rows_of(s, me), :], wo[...]).astype(BF16)
        return 0
    lax.fori_loop(0, seqs, attn_own, 0)
    for s in range(seqs):
        to_partner(give.at[s], got.at[0, s], sems, s, other).wait()

        def first_norm(i, _):
            rows = at(i * sub, sub)
            z = x[s, rows, :].astype(F32) + (own[s, rows, :].astype(F32) + got[0, s, rows, :].astype(F32)) + b_output
            unit, r = norm_stats(z)
            unit1[s, rows, :] = unit
            r1[s, rows, :] = jnp.broadcast_to(r, (sub, 128))
            hn[at((2 * s + me) * part + i * sub, sub), :] = (unit * gain1 + shift1).astype(BF16)
            return 0
        lax.fori_loop(0, part // sub, first_norm, 0)
        block = hn.at[rows_of(s, me)]
        to_partner(block, block, sems, seqs + s, other).start()

    order = [(0, me)] + [(s, other) for s in range(seqs)] + [(s, me) for s in range(1, seqs)]

    def inner(s, p):
        rows = rows_of(s, p)

        def columns(j, _):
            cols = at(j * tile, tile)
            u = dot(hn[rows, :], wi[:, cols]) + b_inner[:, cols]
            cdf = 0.5 * (1.0 + lax.erf(u * 0.7071067811865476))
            act[rows, cols] = (u * cdf).astype(BF16)
            slope[rows, cols] = cdf + u * (jnp.exp(-0.5 * u * u) * 0.3989422804014327)
            return 0
        lax.fori_loop(0, hidden // tile, columns, 0)

    def outer(s, p, place):
        rows = rows_of(s, p)

        def columns(j, _):
            cols = at(j * tile, tile)
            place[s, :, cols] = dot(act[rows, :], wf[:, cols]).astype(BF16)
            return 0
        lax.fori_loop(0, width // tile, columns, 0)

    for n, (s, p) in enumerate(order):
        if n == 1:
            for q in range(seqs):
                block = hn.at[rows_of(q, me)]
                to_partner(block, block, sems, seqs + q, other).wait()
        inner(s, p)
        if p is other:
            outer(s, p, give.at[pl.ds(seqs, seqs)])
            to_partner(give.at[seqs + s], got.at[1, s], sems, 2 * seqs + s, other).start()
        else:
            outer(s, p, own)

    for s in range(seqs):
        to_partner(give.at[seqs + s], got.at[1, s], sems, 2 * seqs + s, other).wait()

        def second_norm(i, _):
            rows = at(i * sub, sub)
            h = unit1[s, rows, :] * gain1 + shift1
            z = (own[s, rows, :].astype(F32) + got[1, s, rows, :].astype(F32)) + b_outer + h
            unit, r = norm_stats(z)
            out[s, rows, :] = (unit * gain2 + shift2).astype(BF16)
            g = gout[s, rows, :].astype(F32)
            d = norm_back(g, gain2, unit, r)
            dz2[s, rows, :] = d
            df[at((2 * s + me) * part + i * sub, sub), :] = d.astype(BF16)
            sums[3] += fold(d)
            sums[4] += fold(g * unit)
            sums[5] += fold(g)
            return 0
        lax.fori_loop(0, part // sub, second_norm, 0)
        block = df.at[rows_of(s, me)]
        to_partner(block, block, sems, 3 * seqs + s, other).start()

    def inner_back(s, p):
        rows = rows_of(s, p)

        def columns(j, _):
            cols = at(j * tile, tile)
            dg = dot_t(df[rows, :], wf[cols, :]).astype(BF16).astype(F32)
            low = (dg * slope[rows, cols]).astype(BF16)
            du[rows, cols] = low
            bsum[:, cols] += fold(low.astype(F32))
            return 0
        lax.fori_loop(0, hidden // tile, columns, 0)

    def outer_back(s, p, place):
        rows = rows_of(s, p)

        def columns(j, _):
            cols = at(j * tile, tile)
            place[s, :, cols] = dot_t(du[rows, :], wi[cols, :]).astype(BF16)
            return 0
        lax.fori_loop(0, width // tile, columns, 0)

    for n, (s, p) in enumerate(order):
        if n == 1:
            for q in range(seqs):
                block = df.at[rows_of(q, me)]
                to_partner(block, block, sems, 3 * seqs + q, other).wait()
        inner_back(s, p)
        if p is other:
            outer_back(s, p, give.at[pl.ds(2 * seqs, seqs)])
            to_partner(give.at[2 * seqs + s], got.at[2, s], sems, 4 * seqs + s, other).start()
        else:
            outer_back(s, p, own)

    for s in range(seqs):
        to_partner(give.at[2 * seqs + s], got.at[2, s], sems, 4 * seqs + s, other).wait()

        def first_back(i, _):
            rows = at(i * sub, sub)
            cot = dz2[s, rows, :] + (own[s, rows, :].astype(F32) + got[2, s, rows, :].astype(F32))
            unit = unit1[s, rows, :]
            d = norm_back(cot, gain1, unit, r1[s, rows, 0:1])
            dz1[s, rows, :] = d
            da[at((2 * s + me) * part + i * sub, sub), :] = d.astype(BF16)
            sums[0] += fold(d)
            sums[1] += fold(cot * unit)
            sums[2] += fold(cot)
            return 0
        lax.fori_loop(0, part // sub, first_back, 0)
        block = da.at[rows_of(s, me)]
        to_partner(block, block, sems, 5 * seqs + s, other).start()

    def grad_inner(j, _):
        cols = at(j * tile, tile)
        g_wi[:, cols] = t_dot(hn[...], du[:, cols]).astype(BF16)
        return 0
    lax.fori_loop(0, hidden // tile, grad_inner, 0)

    def grad_outer(j, _):
        cols = at(j * tile, tile)
        g_wf[cols, :] = t_dot(act[:, cols], df[...]).astype(BF16)
        return 0
    lax.fori_loop(0, hidden // tile, grad_outer, 0)

    for s in range(seqs):
        block = da.at[rows_of(s, me)]
        to_partner(block, block, sems, 5 * seqs + s, other).wait()
    dc[...] = dot_t(da[...], wo[...]).astype(BF16)
    g_wo[...] = t_dot(c[...], da[...]).astype(BF16)
    small[...] = jnp.sum(sums[...], axis=1)
    g_bi[...] = jnp.sum(bsum[...], axis=0, keepdims=True)


def middle(c, x, wo, wi, wf, vec, b_inner, gout):
    seqs, part, width = x.shape
    total, cols = c.shape
    hidden = wi.shape[1]
    sds = jax.ShapeDtypeStruct
    return pl.pallas_call(
        functools.partial(middle_kernel, seqs, part),
        out_shape=(sds(x.shape, BF16), sds(x.shape, F32), sds(c.shape, BF16), sds(wo.shape, BF16),
                   sds(wi.shape, BF16), sds(wf.shape, BF16), sds((6, width), F32), sds((1, hidden), F32)),
        in_specs=vmem(8), out_specs=tuple(vmem(8)),
        scratch_shapes=[
            pltpu.VMEM(x.shape, F32), pltpu.VMEM((seqs, part, 128), F32), pltpu.VMEM(x.shape, F32),
            pltpu.VMEM((total, width), BF16), pltpu.VMEM((total, hidden), BF16), pltpu.VMEM((total, hidden), F32),
            pltpu.VMEM((total, width), BF16), pltpu.VMEM((total, hidden), BF16), pltpu.VMEM((total, width), BF16),
            pltpu.VMEM((3 * seqs, part, width), BF16), pltpu.VMEM((3, seqs, part, width), BF16),
            pltpu.VMEM(x.shape, BF16), pltpu.VMEM((6, 8, width), F32), pltpu.VMEM((8, hidden), F32),
            pltpu.SemaphoreType.DMA((2, 6 * seqs)),
        ],
        compiler_params=pltpu.CompilerParams(collective_id=2, has_side_effects=True, vmem_limit_bytes=LIMIT),
        name="middle",
    )(c, x, wo, wi, wf, vec, b_inner, gout)


def project_back_kernel(seqs, part, rows, dq, dk, dv, wq, wk, wv, dz1,
                        gin, g_q, g_k, g_v, g_b, give, got, sems):
    me = lax.axis_index("head")
    other = 1 - me
    meet(other)

    def total_of(s, p):
        at = pl.ds(pl.multiple_of((2 * s + p) * part, part), part)
        return dot_t(dq[at, :], wq[...]) + dot_t(dk[at, :], wk[...]) + dot_t(dv[at, :], wv[...])

    for s in range(seqs):
        give[s] = total_of(s, other).astype(BF16)
        to_partner(give.at[s], got.at[s], sems, s, other).start()
    g_q[...] = t_dot(rows[...], dq[...]).astype(BF16)
    g_k[...] = t_dot(rows[...], dk[...]).astype(BF16)
    g_v[...] = t_dot(rows[...], dv[...]).astype(BF16)
    g_b[0:1, :] = jnp.sum(fold(dq[...].astype(F32)), axis=0, keepdims=True)
    g_b[1:2, :] = jnp.sum(fold(dv[...].astype(F32)), axis=0, keepdims=True)
    for s in range(seqs):
        own = total_of(s, me).astype(BF16)
        to_partner(give.at[s], got.at[s], sems, s, other).wait()
        gin[s] = (dz1[s] + (own.astype(F32) + got[s].astype(F32))).astype(BF16)


def project_back(rows, dq, dk, dv, wq, wk, wv, dz1):
    seqs, part, width = dz1.shape
    sds = jax.ShapeDtypeStruct
    grad = sds(wq.shape, BF16)
    return pl.pallas_call(
        functools.partial(project_back_kernel, seqs, part),
        out_shape=(sds(dz1.shape, BF16), grad, grad, grad, sds((2, wq.shape[1]), F32)),
        in_specs=vmem(8), out_specs=tuple(vmem(5)),
        scratch_shapes=[pltpu.VMEM(dz1.shape, BF16), pltpu.VMEM(dz1.shape, BF16), pltpu.SemaphoreType.DMA((2, seqs))],
        compiler_params=pltpu.CompilerParams(collective_id=3, has_side_effects=True, vmem_limit_bytes=LIMIT),
        name="project_back",
    )(rows, dq, dk, dv, wq, wk, wv, dz1)
def grid_bits(n):
    bits = n.bit_length() - 1
    side = bits // 3
    return (0, side, 2 * side), bits


def chunk_plan(n, color):
    (bx, by, bz), bits = grid_bits(n)
    order = ((bx, by, bz), (by, bx, bz), (bz, bx, by), (bz, by, bx))[color]
    rest = [b for b in range(bits) if b not in order]
    stages = [("scatter", b) for b in order] + [("double", b) for b in rest]
    return stages + [("gather", b) for b in reversed(order)]


def event_order(n, colors):
    (bx, by, bz), _ = grid_bits(n)
    plans = [chunk_plan(n, c) for c in colors]
    free, ready = [0.0] * 3, [0.0] * len(colors)
    step, length = [0] * len(colors), [1.0] * len(colors)
    events = []
    for _ in range(sum(len(p) for p in plans)):
        best = None
        for c, plan in enumerate(plans):
            if step[c] < len(plan):
                axis = (plan[step[c]][1] >= by) + (plan[step[c]][1] >= bz)
                key = (max(ready[c], free[axis]), -step[c], c, axis)
                best = key if best is None or key < best else best
        start, _, c, axis = best
        kind, b = plans[c][step[c]]
        length[c] *= 0.5 if kind == "scatter" else 1.0
        free[axis] = start + length[c] * (2 if b != (bx, by, bz)[axis] else 1)
        length[c] *= 2.0 if kind == "gather" else 1.0
        ready[c] = free[axis] + 0.08
        events.append((start, c, step[c]))
        step[c] += 1
    return [(c, s) for _, c, s in sorted(events)]


def flip(index, bit):
    return index + (1 - 2 * ((index // (1 << bit)) % 2)) * (1 << bit)


def chunk_pieces(shapes, rows, width):
    chunks = []
    for i, (height, cols) in enumerate(shapes):
        per = max(1, width // cols)
        for r in range(0, height, rows * per):
            for col in range(0, cols, width):
                span = min(cols, width)
                chunks.append([(i, r + j * rows, col, span, j * span) for j in range(per)])
    return chunks


def reduce_kernel(n, colors, rows, pieces, count, *refs):
    grads, tiny = refs[:count], refs[count]
    sums, tiny_out = refs[count + 1:2 * count + 1], refs[2 * count + 1]
    work, got, full, hold, tiny_got, load_sem, save_sem, send_sem, recv_sem, tiny_sem = refs[2 * count + 2:]
    nc = len(colors)
    me, head = lax.axis_index("batch"), lax.axis_index("head")
    _, bits = grid_bits(n)

    def moves(c, out):
        for k, (i, r, col, span, at) in enumerate(pieces[c]):
            outside = (sums if out else grads)[i].at[pl.ds(r, rows), pl.ds(col, span)]
            inside = (full if out else work).at[c, :, pl.ds(at, span)]
            if out:
                yield pltpu.make_async_copy(inside, outside, save_sem.at[c, k])
            else:
                yield pltpu.make_async_copy(outside, inside, load_sem.at[c, k])

    for c in range(nc):
        for move in moves(c, False):
            move.start()
    hold[...] = tiny[...]
    barrier = pltpu.get_barrier_semaphore()
    for b in range(bits):
        pl.semaphore_signal(barrier, inc=1, device_id={"batch": flip(me, b)}, device_id_type=MESH)
    pl.semaphore_signal(barrier, inc=1, device_id={"head": 1 - head}, device_id_type=MESH)
    pl.semaphore_wait(barrier, bits + 1)

    plans = [chunk_plan(n, c) for c in colors]
    bit_of = [(me // (1 << b)) % 2 for b in range(bits)]
    spans = []
    for c in range(nc):
        off, length, at, row = 0, rows, 0, []
        for kind, b in plans[c]:
            if kind == "scatter":
                length //= 2
                row.append((off + bit_of[b] * length, off + (1 - bit_of[b]) * length, length, at))
                off, at = row[-1][0], at + length
            elif kind == "double":
                row.append((off, off, length, at))
                at += length
            else:
                row.append((off, off, length, 0))
                off, length = off - bit_of[b] * length, 2 * length
        spans.append(row)

    def copy_of(c, s):
        kind, b = plans[c][s]
        _, start, length, at = spans[c][s]
        place = (c, pl.ds(pl.multiple_of(start, 16), length))
        if kind == "gather":
            src, dst = full.at[place], full.at[place]
        else:
            src, dst = work.at[place], got.at[c, pl.ds(at, length)]
        return pltpu.make_async_remote_copy(
            src_ref=src, dst_ref=dst, send_sem=send_sem.at[c, s], recv_sem=recv_sem.at[c, s],
            device_id={"batch": flip(me, b)}, device_id_type=MESH)

    def finish(c, s):
        keep, _, length, at = spans[c][s]
        copy_of(c, s).wait()
        if plans[c][s][0] != "gather":
            target = full if plans[c][s + 1][0] == "gather" else work

            def add(i, _):
                here = pl.ds(pl.multiple_of(keep + i * 16, 16), 16)
                there = pl.ds(pl.multiple_of(at + i * 16, 16), 16)
                target[c, here, :] = (work[c, here, :].astype(F32) + got[c, there, :].astype(F32)).astype(BF16)
                return 0
            lax.fori_loop(0, length // 16, add, 0)

    def tiny_copy(k):
        rest = hold.at[pl.ds(0, 8)] if k == 0 else hold
        there = tiny_got.at[k, pl.ds(0, 8)] if k == 0 else tiny_got.at[k]
        target = {"head": 1 - head} if k == 0 else {"batch": flip(me, k - 1)}
        return pltpu.make_async_remote_copy(
            src_ref=rest, dst_ref=there, send_sem=tiny_sem.at[0, k], recv_sem=tiny_sem.at[1, k],
            device_id=target, device_id_type=MESH)

    def tiny_finish(k):
        tiny_copy(k).wait()
        if k == 0:
            hold[0:8, :] += tiny_got[0, 0:8, :]
        else:
            hold[...] += tiny_got[k]

    events = event_order(n, colors)
    gap = len(events) // (bits + 2)
    for e, (c, s) in enumerate(events):
        if s == 0:
            for move in moves(c, False):
                move.wait()
        else:
            finish(c, s - 1)
        copy_of(c, s).start()
        if e % gap == 0 and e // gap <= bits:
            k = e // gap
            if k > 0:
                tiny_finish(k - 1)
            tiny_copy(k).start()
    tiny_finish(bits)
    tiny_out[...] = hold[...]
    for c in range(nc):
        finish(c, len(plans[c]) - 1)
        for move in moves(c, True):
            move.start()
    for c in range(nc):
        for move in moves(c, True):
            move.wait()


def reduce_gradients(grads, tiny, n, rows=256):
    width = tiny.shape[1]
    pieces = chunk_pieces([g.shape for g in grads], rows, width)
    nc = len(pieces)
    colors = [c % 2 for c in range(nc)]
    stages = len(chunk_plan(n, 0))
    _, bits = grid_bits(n)
    got_rows = rows - rows // 8 + (bits - 3) * rows // 8
    hbm = [pl.BlockSpec(memory_space=pl.ANY)] * len(grads)
    done = pl.pallas_call(
        functools.partial(reduce_kernel, n, colors, rows, pieces, len(grads)),
        out_shape=tuple(jax.ShapeDtypeStruct(g.shape, g.dtype) for g in (*grads, tiny)),
        in_specs=hbm + vmem(1), out_specs=tuple(hbm + vmem(1)),
        scratch_shapes=[
            pltpu.VMEM((nc, rows, width), BF16), pltpu.VMEM((nc, got_rows, width), BF16),
            pltpu.VMEM((nc, rows, width), BF16), pltpu.VMEM(tiny.shape, F32),
            pltpu.VMEM((bits + 1,) + tiny.shape, F32),
            pltpu.SemaphoreType.DMA((nc, 2)), pltpu.SemaphoreType.DMA((nc, 2)),
            pltpu.SemaphoreType.DMA((nc, stages)), pltpu.SemaphoreType.DMA((nc, stages)),
            pltpu.SemaphoreType.DMA((2, bits + 1)),
        ],
        compiler_params=pltpu.CompilerParams(collective_id=0, has_side_effects=True, vmem_limit_bytes=LIMIT),
        name="reduce_gradients",
    )(*grads, tiny)
    return done[:-1], done[-1]
def on_device(n_batch, inputs, prior_scores, lengths, w_query, w_key, w_value, b_query, b_value, w_output, b_output,
              gain_attn, shift_attn, w_inner, b_inner, w_outer, b_outer, gain_ffn, shift_ffn, grad_out, grad_scores):
    width = inputs.shape[2]
    bias = jnp.stack([b_query, b_value]).astype(F32)
    vec = jnp.stack([b_output, gain_attn, shift_attn, b_outer, gain_ffn, shift_ffn]).astype(F32)
    rows, q, k, v = project_rows(inputs, w_query, w_key, w_value, bias)
    new_scores, context, norm = attend(lengths, q, k, v, prior_scores)
    outputs, dz1, dc, g_wo, g_wi, g_wf, small, g_bi = middle(
        context, inputs, w_output, w_inner, w_outer, vec, b_inner.astype(F32)[None], grad_out)
    grad_prior, dq, dk, dv = attend_back(lengths, q, k, v, dc, prior_scores, norm, grad_scores)
    grad_inputs, g_wq, g_wk, g_wv, g_b = project_back(rows, dq, dk, dv, w_query, w_key, w_value, dz1)
    pad = lambda a, to: jnp.pad(a, ((0, to - a.shape[0]), (0, 0)))
    mine = jnp.concatenate([g_bi.reshape(-1, width), g_b.reshape(-1, width)])
    tiny = jnp.concatenate([pad(small, 8), pad(mine, 8)])
    grads, tiny = reduce_gradients((g_wi, g_wf, g_wo, g_wq, g_wk, g_wv), tiny, n_batch)
    g_wi, g_wf, g_wo, g_wq, g_wk, g_wv = [g.astype(F32) for g in grads]
    g_bi = tiny[8:8 + g_bi.size // width].reshape(-1)
    g_b = tiny[8 + g_bi.size // width:8 + mine.shape[0]].reshape(g_b.shape)
    return (outputs, new_scores, grad_inputs, grad_prior, g_wq, g_wk, g_wv, g_b[0], g_b[1], g_wo,
            tiny[0], tiny[1], tiny[2], g_wi, g_bi, g_wf, tiny[3], tiny[4], tiny[5])


def solution(mesh):
    seq, scores, whole = P("batch", "head", None), P("batch", "head", None, None), P()
    down, across, vector = P("head", None), P(None, "head"), P("head")
    in_specs = (seq, scores, P("batch"), across, across, across, vector, vector, down, whole, whole, whole,
                across, vector, down, whole, whole, whole, seq, scores)
    out_specs = (seq, scores, seq, scores, across, across, across, vector, vector, down, whole, whole, whole,
                 across, vector, down, whole, whole, whole)
    layer = functools.partial(on_device, mesh.shape["batch"])
    return jax.shard_map(layer, mesh=mesh, in_specs=in_specs, out_specs=out_specs, check_vma=False)
```

```python
import functools
import jax, jax.numpy as jnp
from jax import lax
from jax.experimental import pallas as pl
from jax.experimental.pallas import tpu as pltpu
from jax.sharding import PartitionSpec as P

MESH = pl.DeviceIdType.MESH
F32, BF16 = jnp.float32, jnp.bfloat16
EPS = 1e-12
NEG = -1e30
LIMIT = 64 * 1000 * 1000


def dot(a, b):
    return jnp.dot(a, b, preferred_element_type=F32)


def dot_t(a, b):
    return lax.dot_general(a, b, (((1,), (1,)), ((), ())), preferred_element_type=F32)


def t_dot(a, b):
    return lax.dot_general(a, b, (((0,), (0,)), ((), ())), preferred_element_type=F32)


def meet(partner):
    barrier = pltpu.get_barrier_semaphore()
    pl.semaphore_signal(barrier, inc=1, device_id={"head": partner}, device_id_type=MESH)
    pl.semaphore_wait(barrier, 1)


def to_partner(src, dst, sems, i, partner):
    return pltpu.make_async_remote_copy(
        src_ref=src, dst_ref=dst, send_sem=sems.at[0, i], recv_sem=sems.at[1, i],
        device_id={"head": partner}, device_id_type=MESH)


def vmem(count):
    return [pl.BlockSpec(memory_space=pltpu.VMEM)] * count


def project_kernel(seqs, part, x, wq, wk, wv, bias, rows, q, k, v, got, sems):
    me = lax.axis_index("head")
    other = 1 - me
    meet(other)
    for s in range(seqs):
        to_partner(x.at[s], got.at[s], sems, s, other).start()

    def emit(block, s, p):
        at = pl.ds(pl.multiple_of((2 * s + p) * part, part), part)
        rows[at, :] = block
        q[at, :] = (dot(block, wq[...]) + bias[0:1, :]).astype(BF16)
        k[at, :] = dot(block, wk[...]).astype(BF16)
        v[at, :] = (dot(block, wv[...]) + bias[1:2, :]).astype(BF16)

    def own(s, _):
        emit(x[s], s, me)
        return 0

    lax.fori_loop(0, seqs, own, 0)
    for s in range(seqs):
        to_partner(x.at[s], got.at[s], sems, s, other).wait()

    def theirs(s, _):
        emit(got[s], s, other)
        return 0

    lax.fori_loop(0, seqs, theirs, 0)


def project_rows(x, wq, wk, wv, bias):
    seqs, part, width = x.shape
    total, cols = 2 * seqs * part, wq.shape[1]
    out = jax.ShapeDtypeStruct((total, cols), BF16)
    return pl.pallas_call(
        functools.partial(project_kernel, seqs, part),
        out_shape=(jax.ShapeDtypeStruct((total, width), BF16), out, out, out),
        in_specs=vmem(5), out_specs=tuple(vmem(4)),
        scratch_shapes=[pltpu.VMEM(x.shape, BF16), pltpu.SemaphoreType.DMA((2, seqs))],
        compiler_params=pltpu.CompilerParams(collective_id=1, has_side_effects=True, vmem_limit_bytes=LIMIT),
        name="project_rows",
    )(x, wq, wk, wv, bias)


def attend_kernel(block, head, lengths, q, k, v, prior, score, c, norm):
    full = k.shape[0]
    live = lax.broadcasted_iota(jnp.int32, (1, full), 1) < lengths[pl.program_id(0)]
    first = lax.broadcasted_iota(jnp.int32, (1, 2 * head), 1) < head
    scale = head ** -0.5
    for r in range(0, full, block):
        rows = pl.ds(r, block)
        queries = q[rows, :]
        parts, norms = [], []
        for h in range(2):
            mine = jnp.where(first == (h == 0), queries, jnp.zeros_like(queries))
            scores = dot_t(mine, k[...]) * scale + prior[0, h, rows, :].astype(F32)
            score[0, h, rows, :] = scores.astype(BF16)
            masked = jnp.where(live, scores, NEG)
            top = jnp.max(masked, axis=-1, keepdims=True)
            terms = jnp.exp(masked - top)
            total = jnp.sum(terms, axis=-1, keepdims=True)
            probs = (terms * (1.0 / total)).astype(BF16)
            parts.append(dot(probs, v[...]))
            norms.append(top + jnp.log(total))
        c[rows, :] = jnp.where(first, parts[0], parts[1]).astype(BF16)
        norm[0, 0, rows, :] = jnp.where(first, norms[0], norms[1])


def attend(lengths, q, k, v, prior):
    seqs, heads, full, _ = prior.shape
    pair = q.shape[1] // heads * 2
    rows = pl.BlockSpec((full, pair), lambda s, h, n: (s, h))
    big = pl.BlockSpec((1, 2, full, full), lambda s, h, n: (s, h, 0, 0))
    norm = pl.BlockSpec((1, 1, full, pair), lambda s, h, n: (s, h, 0, 0))
    return pl.pallas_call(
        functools.partial(attend_kernel, 256, pair // 2),
        grid_spec=pltpu.PrefetchScalarGridSpec(
            num_scalar_prefetch=1, grid=(seqs, heads // 2),
            in_specs=[rows, rows, rows, big], out_specs=(big, rows, norm)),
        out_shape=(jax.ShapeDtypeStruct(prior.shape, BF16), jax.ShapeDtypeStruct(q.shape, BF16),
                   jax.ShapeDtypeStruct((seqs, heads // 2, full, pair), F32)),
        compiler_params=pltpu.CompilerParams(vmem_limit_bytes=40 << 20),
        name="attend",
    )(lengths, q, k, v, prior)


def attend_back_kernel(block, head, lengths, q, k, v, dc, prior, norm, given, grad, dq, dk, dv):
    full = k.shape[0]
    live = lax.broadcasted_iota(jnp.int32, (1, full), 1) < lengths[pl.program_id(0)]
    first = lax.broadcasted_iota(jnp.int32, (1, 2 * head), 1) < head
    scale = head ** -0.5
    q_t, dc_t = q[...].T, dc[...].T
    dk_t, dv_t = [0.0, 0.0], [0.0, 0.0]
    for r in range(0, full, block):
        rows = pl.ds(r, block)
        queries, cots = q[rows, :], dc[rows, :]
        parts = []
        for h in range(2):
            mine = first == (h == 0)
            scores = dot_t(jnp.where(mine, queries, jnp.zeros_like(queries)), k[...]) * scale
            scores = scores + prior[0, h, rows, :].astype(F32)
            probs = jnp.exp(jnp.where(live, scores, NEG) - norm[0, 0, rows, h * head:h * head + 1])
            dp = dot_t(jnp.where(mine, cots, jnp.zeros_like(cots)), v[...])
            delta = jnp.sum(probs * dp, axis=-1, keepdims=True)
            ds = (probs * (dp - delta) + given[0, h, rows, :].astype(F32)).astype(BF16)
            grad[0, h, rows, :] = ds
            parts.append(dot(ds, k[...]))
            lanes = slice(h * head, (h + 1) * head)
            dk_t[h] = dk_t[h] + dot(q_t[lanes, r:r + block], ds)
            dv_t[h] = dv_t[h] + dot(dc_t[lanes, r:r + block], probs.astype(BF16))
        dq[rows, :] = (jnp.where(first, parts[0], parts[1]) * scale).astype(BF16)
    dk[...] = (jnp.concatenate(dk_t, axis=0) * scale).T.astype(BF16)
    dv[...] = jnp.concatenate(dv_t, axis=0).T.astype(BF16)


def attend_back(lengths, q, k, v, dc, prior, norm, given):
    seqs, heads, full, _ = prior.shape
    pair = q.shape[1] // heads * 2
    rows = pl.BlockSpec((full, pair), lambda s, h, n: (s, h))
    big = pl.BlockSpec((1, 2, full, full), lambda s, h, n: (s, h, 0, 0))
    norms = pl.BlockSpec((1, 1, full, pair), lambda s, h, n: (s, h, 0, 0))
    flat = jax.ShapeDtypeStruct(q.shape, BF16)
    return pl.pallas_call(
        functools.partial(attend_back_kernel, 256, pair // 2),
        grid_spec=pltpu.PrefetchScalarGridSpec(
            num_scalar_prefetch=1, grid=(seqs, heads // 2),
            in_specs=[rows, rows, rows, rows, big, norms, big], out_specs=(big, rows, rows, rows)),
        out_shape=(jax.ShapeDtypeStruct(prior.shape, BF16), flat, flat, flat),
        compiler_params=pltpu.CompilerParams(vmem_limit_bytes=40 << 20),
        cost_estimate=pl.CostEstimate(flops=40 * full * full * seqs * heads * pair // 2, transcendentals=prior.size,
                                      bytes_accessed=6 * prior.size),
        name="attend_back",
    )(lengths, q, k, v, dc, prior, norm, given)


def fold(value):
    return jnp.sum(value.reshape(value.shape[0] // 8, 8, value.shape[1]), axis=0)


def norm_stats(z):
    mean = jnp.mean(z, axis=-1, keepdims=True)
    centred = z - mean
    r = lax.rsqrt(jnp.mean(centred * centred, axis=-1, keepdims=True) + EPS)
    return centred * r, r


def norm_back(cot, gain, unit, r):
    e = cot * gain
    return r * (e - jnp.mean(e, axis=-1, keepdims=True) - unit * jnp.mean(e * unit, axis=-1, keepdims=True))


def middle_kernel(seqs, part, firsts, c, x, wo, wi, wf, vec, b_inner, gout,
                  out, dz1, dc, g_wo, keep, give_x, give_y, give_z, small, g_bi,
                  unit1, r1, dz2, hn, act, slope, df, du, da, give, got, own, sums, bsum, sems):
    me = lax.axis_index("head")
    other = 1 - me
    width = x.shape[2]
    hidden = wi.shape[1]
    tile = 512
    sub = 64
    meet(other)
    b_output, gain1, shift1, b_outer, gain2, shift2 = [vec[i:i + 1, :] for i in range(6)]
    sums[...] = jnp.zeros_like(sums)
    bsum[...] = jnp.zeros_like(bsum)

    def rows_of(s, p):
        return pl.ds(pl.multiple_of((2 * s + p) * part, part), part)

    def at(start, size):
        return pl.ds(pl.multiple_of(start, size), size)

    def attn_part(s, _):
        give[s] = dot(c[rows_of(s, other), :], wo[...]).astype(BF16)
        return 0
    for s in range(seqs):
        attn_part(s, 0)
        to_partner(give.at[s], got.at[0, s], sems, s, other).start()

    def attn_own(s, _):
        own[s] = dot(c[rows_of(s, me), :], wo[...]).astype(BF16)
        return 0
    lax.fori_loop(0, seqs, attn_own, 0)
    for s in range(seqs):
        to_partner(give.at[s], got.at[0, s], sems, s, other).wait()

        def first_norm(i, _):
            rows = at(i * sub, sub)
            z = x[s, rows, :].astype(F32) + (own[s, rows, :].astype(F32) + got[0, s, rows, :].astype(F32)) + b_output
            unit, r = norm_stats(z)
            unit1[s, rows, :] = unit
            r1[s, rows, :] = jnp.broadcast_to(r, (sub, 128))
            hn[at((2 * s + me) * part + i * sub, sub), :] = (unit * gain1 + shift1).astype(BF16)
            return 0
        lax.fori_loop(0, part // sub, first_norm, 0)
        block = hn.at[rows_of(s, me)]
        to_partner(block, block, sems, seqs + s, other).start()

    order = [(0, me)] + [(s, other) for s in range(seqs)] + [(s, me) for s in range(1, seqs)]

    def inner(s, p):
        rows = rows_of(s, p)

        def columns(j, _):
            cols = at(j * tile, tile)
            u = dot(hn[rows, :], wi[:, cols]) + b_inner[:, cols]
            cdf = 0.5 * (1.0 + lax.erf(u * 0.7071067811865476))
            act[rows, cols] = (u * cdf).astype(BF16)
            slope[rows, cols] = cdf + u * (jnp.exp(-0.5 * u * u) * 0.3989422804014327)
            return 0
        lax.fori_loop(0, hidden // tile, columns, 0)

    def outer(s, p, place):
        rows = rows_of(s, p)

        def columns(j, _):
            cols = at(j * tile, tile)
            place[s, :, cols] = dot(act[rows, :], wf[:, cols]).astype(BF16)
            return 0
        lax.fori_loop(0, width // tile, columns, 0)

    for n, (s, p) in enumerate(order):
        if n == 1:
            for q in range(seqs):
                block = hn.at[rows_of(q, me)]
                to_partner(block, block, sems, seqs + q, other).wait()
        inner(s, p)
        if p is other:
            outer(s, p, give.at[pl.ds(seqs, seqs)])
            to_partner(give.at[seqs + s], got.at[1, s], sems, 2 * seqs + s, other).start()
        else:
            outer(s, p, own)

    for s in range(seqs):
        to_partner(give.at[seqs + s], got.at[1, s], sems, 2 * seqs + s, other).wait()

        def second_norm(i, _):
            rows = at(i * sub, sub)
            h = unit1[s, rows, :] * gain1 + shift1
            z = (own[s, rows, :].astype(F32) + got[1, s, rows, :].astype(F32)) + b_outer + h
            unit, r = norm_stats(z)
            out[s, rows, :] = (unit * gain2 + shift2).astype(BF16)
            g = gout[s, rows, :].astype(F32)
            d = norm_back(g, gain2, unit, r)
            dz2[s, rows, :] = d
            df[at((2 * s + me) * part + i * sub, sub), :] = d.astype(BF16)
            sums[3] += fold(d)
            sums[4] += fold(g * unit)
            sums[5] += fold(g)
            return 0
        lax.fori_loop(0, part // sub, second_norm, 0)
        block = df.at[rows_of(s, me)]
        to_partner(block, block, sems, 3 * seqs + s, other).start()

    def inner_back(s, p):
        rows = rows_of(s, p)

        def columns(j, _):
            cols = at(j * tile, tile)
            dg = dot_t(df[rows, :], wf[cols, :]).astype(BF16).astype(F32)
            low = (dg * slope[rows, cols]).astype(BF16)
            du[rows, cols] = low
            bsum[:, cols] += fold(low.astype(F32))
            return 0
        lax.fori_loop(0, hidden // tile, columns, 0)

    def outer_back(s, p, place):
        rows = rows_of(s, p)

        def columns(j, _):
            cols = at(j * tile, tile)
            place[s, :, cols] = dot_t(du[rows, :], wi[cols, :]).astype(BF16)
            return 0
        lax.fori_loop(0, width // tile, columns, 0)

    for n, (s, p) in enumerate(order):
        if n == 1:
            for q in range(seqs):
                block = df.at[rows_of(q, me)]
                to_partner(block, block, sems, 3 * seqs + q, other).wait()
        inner_back(s, p)
        if p is other:
            outer_back(s, p, give.at[pl.ds(2 * seqs, seqs)])
            to_partner(give.at[2 * seqs + s], got.at[2, s], sems, 4 * seqs + s, other).start()
        else:
            outer_back(s, p, own)

    for s in range(seqs):
        to_partner(give.at[2 * seqs + s], got.at[2, s], sems, 4 * seqs + s, other).wait()

        def first_back(i, _):
            rows = at(i * sub, sub)
            cot = dz2[s, rows, :] + (own[s, rows, :].astype(F32) + got[2, s, rows, :].astype(F32))
            unit = unit1[s, rows, :]
            d = norm_back(cot, gain1, unit, r1[s, rows, 0:1])
            dz1[s, rows, :] = d
            da[at((2 * s + me) * part + i * sub, sub), :] = d.astype(BF16)
            sums[0] += fold(d)
            sums[1] += fold(cot * unit)
            sums[2] += fold(cot)
            return 0
        lax.fori_loop(0, part // sub, first_back, 0)
        block = da.at[rows_of(s, me)]
        to_partner(block, block, sems, 5 * seqs + s, other).start()

    mine = lax.axis_index("batch")
    gives = (give_x, give_y, give_z)
    half = keep.shape[1]
    per = hidden // width

    def put(value, kept, axis, given):
        bit = (mine // (1 << firsts[axis])) % 2

        @pl.when(bit == 0)
        def _():
            keep[kept] = value[:half].astype(BF16)
            gives[axis][given] = value[half:].astype(BF16)

        @pl.when(bit == 1)
        def _():
            keep[kept] = value[half:].astype(BF16)
            gives[axis][given] = value[:half].astype(BF16)

    def grads_of(axis, start, count):
        def grad_outer(i, _):
            at_act = at((start + i) * 2 * half, 2 * half)
            put(t_dot(act[:, at_act], df[...]), early + start + i, axis, count + i)
            return 0

        def grad_inner(i, _):
            at_hn, at_du = at((start + i) // per * 2 * half, 2 * half), at((start + i) % per * width, width)
            put(t_dot(hn[:, at_hn], du[:, at_du]), start + i, axis, i)
            return 0

        lax.fori_loop(0, count, grad_inner, 0)
        lax.fori_loop(0, count, grad_outer, 0)

    early = keep.shape[0] // 2
    begin = 0
    for axis in range(3):
        grads_of(axis, begin, gives[axis].shape[0] // 2)
        begin += gives[axis].shape[0] // 2

    for s in range(seqs):
        block = da.at[rows_of(s, me)]
        to_partner(block, block, sems, 5 * seqs + s, other).wait()
    dc[...] = dot_t(da[...], wo[...]).astype(BF16)
    g_wo[...] = t_dot(c[...], da[...]).astype(BF16)
    small[...] = jnp.sum(sums[...], axis=1)
    g_bi[...] = jnp.sum(bsum[...], axis=0, keepdims=True)


def middle(c, x, wo, wi, wf, vec, b_inner, gout, firsts, counts, rows):
    seqs, part, width = x.shape
    total, cols = c.shape
    hidden = wi.shape[1]
    sds = jax.ShapeDtypeStruct
    halves = [sds((2 * count, rows // 2, width), BF16) for count in (sum(counts), *counts)]
    return pl.pallas_call(
        functools.partial(middle_kernel, seqs, part, firsts),
        out_shape=(sds(x.shape, BF16), sds(x.shape, F32), sds(c.shape, BF16), sds(wo.shape, BF16),
                   *halves, sds((6, width), F32), sds((1, hidden), F32)),
        in_specs=vmem(8), out_specs=tuple(vmem(10)),
        scratch_shapes=[
            pltpu.VMEM(x.shape, F32), pltpu.VMEM((seqs, part, 128), F32), pltpu.VMEM(x.shape, F32),
            pltpu.VMEM((total, width), BF16), pltpu.VMEM((total, hidden), BF16), pltpu.VMEM((total, hidden), F32),
            pltpu.VMEM((total, width), BF16), pltpu.VMEM((total, hidden), BF16), pltpu.VMEM((total, width), BF16),
            pltpu.VMEM((3 * seqs, part, width), BF16), pltpu.VMEM((3, seqs, part, width), BF16),
            pltpu.VMEM(x.shape, BF16), pltpu.VMEM((6, 8, width), F32), pltpu.VMEM((8, hidden), F32),
            pltpu.SemaphoreType.DMA((2, 6 * seqs)),
        ],
        compiler_params=pltpu.CompilerParams(collective_id=2, has_side_effects=True, vmem_limit_bytes=LIMIT),
        cost_estimate=pl.CostEstimate(flops=14 * total * width * hidden, transcendentals=total * hidden,
                                      bytes_accessed=30 << 20),
        name="middle",
    )(c, x, wo, wi, wf, vec, b_inner, gout)


def project_back_kernel(seqs, part, rows, dq, dk, dv, wq, wk, wv, dz1,
                        gin, g_q, g_k, g_v, g_b, give, got, sems):
    me = lax.axis_index("head")
    other = 1 - me
    meet(other)

    def total_of(s, p):
        at = pl.ds(pl.multiple_of((2 * s + p) * part, part), part)
        return dot_t(dq[at, :], wq[...]) + dot_t(dk[at, :], wk[...]) + dot_t(dv[at, :], wv[...])

    for s in range(seqs):
        give[s] = total_of(s, other).astype(BF16)
        to_partner(give.at[s], got.at[s], sems, s, other).start()
    g_q[...] = t_dot(rows[...], dq[...]).astype(BF16)
    g_k[...] = t_dot(rows[...], dk[...]).astype(BF16)
    g_v[...] = t_dot(rows[...], dv[...]).astype(BF16)
    g_b[0:1, :] = jnp.sum(fold(dq[...].astype(F32)), axis=0, keepdims=True)
    g_b[1:2, :] = jnp.sum(fold(dv[...].astype(F32)), axis=0, keepdims=True)
    for s in range(seqs):
        own = total_of(s, me).astype(BF16)
        to_partner(give.at[s], got.at[s], sems, s, other).wait()
        gin[s] = (dz1[s] + (own.astype(F32) + got[s].astype(F32))).astype(BF16)


def project_back(rows, dq, dk, dv, wq, wk, wv, dz1):
    seqs, part, width = dz1.shape
    sds = jax.ShapeDtypeStruct
    grad = sds(wq.shape, BF16)
    return pl.pallas_call(
        functools.partial(project_back_kernel, seqs, part),
        out_shape=(sds(dz1.shape, BF16), grad, grad, grad, sds((2, wq.shape[1]), F32)),
        in_specs=vmem(8), out_specs=tuple(vmem(5)),
        scratch_shapes=[pltpu.VMEM(dz1.shape, BF16), pltpu.VMEM(dz1.shape, BF16), pltpu.SemaphoreType.DMA((2, seqs))],
        compiler_params=pltpu.CompilerParams(collective_id=3, has_side_effects=True, vmem_limit_bytes=LIMIT),
        cost_estimate=pl.CostEstimate(flops=12 * rows.size * wq.shape[1], transcendentals=0, bytes_accessed=16 << 20),
        name="project_back",
    )(rows, dq, dk, dv, wq, wk, wv, dz1)
def grid_bits(n):
    bits = n.bit_length() - 1
    side = bits // 3
    return (0, side, 2 * side), bits


def chunk_plan(n, color):
    (bx, by, bz), bits = grid_bits(n)
    order = ((bx, by, bz), (by, bx, bz), (bz, bx, by), (bz, by, bx))[color]
    rest = [b for b in range(bits) if b not in order]
    stages = [("scatter", b) for b in order] + [("double", b) for b in rest]
    return stages + [("gather", b) for b in reversed(order)]


def event_order(n, plans, halved):
    first, _ = grid_bits(n)
    lag = 0.1

    def path(b):
        axis = (b >= first[1]) + (b >= first[2])
        return ((axis, 1),) if b == first[axis] else ((axis, 1), (axis + 3, 2))

    work = []
    for plan, half in zip(plans, halved):
        length, row = 0.5 if half else 1.0, []
        for kind, b in plan:
            length *= 0.5 if kind == "scatter" else 1.0
            row.append((path(b), length))
            length *= 2.0 if kind == "gather" else 1.0
        work.append(row)
    left = [sum(w * p[-1][1] + lag for p, w in row) for row in work]
    free, ready, step, events = [0.0] * 6, [0.0] * len(plans), [0] * len(plans), []
    for _ in range(sum(len(p) for p in plans)):
        best = None
        for c, row in enumerate(work):
            if step[c] < len(row):
                start = max([ready[c]] + [free[link] for link, _ in row[step[c]][0]])
                key = (start, left[c] + step[c], c)
                best = key if best is None or key < best else best
        start, _, c = best
        links, span = work[c][step[c]]
        for link, times in links:
            free[link] = start + times * span
        ready[c] = start + links[-1][1] * span + lag
        left[c] -= links[-1][1] * span + lag
        events.append((start, c, step[c]))
        step[c] += 1
    return [(c, s) for _, c, s in sorted(events)]


def flip(index, bit):
    return index + (1 - 2 * ((index // (1 << bit)) % 2)) * (1 << bit)


def chunk_pieces(shapes, rows, width):
    chunks = []
    for i, (height, cols) in enumerate(shapes):
        per = max(1, width // cols)
        for r in range(0, height, rows * per):
            for col in range(0, cols, width):
                span = min(cols, width)
                chunks.append([(i, r + j * rows, col, span, j * span) for j in range(per)])
    return chunks


def reduce_kernel(n, colors, rows, loads, saves, count, results, *refs):
    grads, tiny = refs[:count], refs[count]
    sums, tiny_out = refs[count + 1:count + results + 1], refs[count + results + 1]
    work, got, full, hold, tiny_got, load_sem, save_sem, send_sem, recv_sem, tiny_sem = refs[count + results + 2:]
    nc = len(colors)
    me, head = lax.axis_index("batch"), lax.axis_index("head")
    _, bits = grid_bits(n)

    def moves(c, out):
        if out:
            for k, (i, r, col, span, at) in enumerate(saves[c]):
                outside = sums[i].at[pl.ds(r, rows), pl.ds(col, span)]
                yield pltpu.make_async_copy(full.at[c, :, pl.ds(at, span)], outside, save_sem.at[c, k])
        elif loads[c] is None:
            for k, (i, r, col, span, at) in enumerate(saves[c]):
                outside = grads[i + count - results].at[pl.ds(r, rows), pl.ds(col, span)]
                yield pltpu.make_async_copy(outside, work.at[c, :, pl.ds(at, span)], load_sem.at[c, k])
        else:
            kept, kept_at, given, given_at = loads[c]
            keep, _, length, at = spans[c][0]
            inside = work.at[c, pl.ds(pl.multiple_of(keep, 16), length)]
            yield pltpu.make_async_copy(grads[kept].at[kept_at], inside, load_sem.at[c, 0])
            yield pltpu.make_async_copy(grads[given].at[given_at], got.at[c, pl.ds(at, length)], load_sem.at[c, 1])

    plans = [chunk_plan(n, c) for c in colors]
    bit_of = [(me // (1 << b)) % 2 for b in range(bits)]
    spans = []
    for c in range(nc):
        off, length, at, row = 0, rows, 0, []
        for kind, b in plans[c]:
            if kind == "scatter":
                length //= 2
                row.append((off + bit_of[b] * length, off + (1 - bit_of[b]) * length, length, at))
                off, at = row[-1][0], at + length
            elif kind == "double":
                row.append((off, off, length, at))
                at += length
            else:
                row.append((off, off, length, 0))
                off, length = off - bit_of[b] * length, 2 * length
        spans.append(row)

    for c in range(nc):
        for move in moves(c, False):
            move.start()
    hold[...] = tiny[...]
    barrier = pltpu.get_barrier_semaphore()
    for b in range(bits):
        pl.semaphore_signal(barrier, inc=1, device_id={"batch": flip(me, b)}, device_id_type=MESH)
    pl.semaphore_signal(barrier, inc=1, device_id={"head": 1 - head}, device_id_type=MESH)
    pl.semaphore_wait(barrier, bits + 1)

    def copy_of(c, s):
        kind, b = plans[c][s]
        _, start, length, at = spans[c][s]
        place = (c, pl.ds(pl.multiple_of(start, 16), length))
        if kind == "gather":
            src, dst = full.at[place], full.at[place]
        else:
            src, dst = work.at[place], got.at[c, pl.ds(at, length)]
        return pltpu.make_async_remote_copy(
            src_ref=src, dst_ref=dst, send_sem=send_sem.at[c, s], recv_sem=recv_sem.at[c, s],
            device_id={"batch": flip(me, b)}, device_id_type=MESH)

    def finish(c, s):
        keep, _, length, at = spans[c][s]
        if s == 0 and loads[c] is not None:
            for move in moves(c, False):
                move.wait()
        else:
            copy_of(c, s).wait()
        if plans[c][s][0] != "gather":
            target = full if plans[c][s + 1][0] == "gather" else work

            def add(i, _):
                here = pl.ds(pl.multiple_of(keep + i * 16, 16), 16)
                there = pl.ds(pl.multiple_of(at + i * 16, 16), 16)
                target[c, here, :] = (work[c, here, :].astype(F32) + got[c, there, :].astype(F32)).astype(BF16)
                return 0
            lax.fori_loop(0, length // 16, add, 0)

    def tiny_copy(k):
        rest = hold.at[pl.ds(0, 8)] if k == 0 else hold
        there = tiny_got.at[k, pl.ds(0, 8)] if k == 0 else tiny_got.at[k]
        target = {"head": 1 - head} if k == 0 else {"batch": flip(me, k - 1)}
        return pltpu.make_async_remote_copy(
            src_ref=rest, dst_ref=there, send_sem=tiny_sem.at[0, k], recv_sem=tiny_sem.at[1, k],
            device_id=target, device_id_type=MESH)

    def tiny_finish(k):
        tiny_copy(k).wait()
        if k == 0:
            hold[0:8, :] += tiny_got[0, 0:8, :]
        else:
            hold[...] += tiny_got[k]

    done = [load is not None for load in loads]
    events = [(c, s + done[c]) for c, s in event_order(n, [p[d:] for p, d in zip(plans, done)], done)]
    gap = len(events) // (bits + 2)
    for e, (c, s) in enumerate(events):
        if s == 0:
            for move in moves(c, False):
                move.wait()
        else:
            finish(c, s - 1)
        copy_of(c, s).start()
        if e % gap == 0 and e // gap <= bits:
            k = e // gap
            if k > 0:
                tiny_finish(k - 1)
            tiny_copy(k).start()
    tiny_finish(bits)
    tiny_out[...] = hold[...]
    for c in range(nc):
        finish(c, len(plans[c]) - 1)
        for move in moves(c, True):
            move.start()
    for c in range(nc):
        for move in moves(c, True):
            move.wait()


EARLY_MIX = (0, 0, 0, 1, 1, 1, 2, 3)
LATE_MIX = (0, 1, 2, 0, 1, 3, 0, 1)
ROWS = 256


def reduce_gradients(early, late, shapes, tiny, n):
    width = tiny.shape[1]
    saves = chunk_pieces(shapes, ROWS, width)
    count = early[0].shape[0] // 2
    slots, colors, loads = [0, 0, 0], [], []
    for which in range(2):
        for c in range(count):
            color = EARLY_MIX[c * len(EARLY_MIX) // count]
            axis = min(color, 2)
            loads.append((0, which * count + c, 1 + axis, slots[axis]))
            slots[axis] += 1
            colors.append(color)
    for c in range(len(saves) - 2 * count):
        colors.append(LATE_MIX[c % len(LATE_MIX)])
        loads.append(None)
    rank = [(c % count, c // count) if c < 2 * count else (c - 2 * count, 2) for c in range(len(saves))]
    order = sorted(range(len(saves)), key=lambda c: rank[c])
    saves, colors, loads = ([array[c] for c in order] for array in (saves, colors, loads))
    nc = len(saves)
    stages = len(chunk_plan(n, 0))
    _, bits = grid_bits(n)
    got_rows = ROWS - ROWS // 8 + (bits - 3) * ROWS // 8
    grads = (*early, *late)
    hbm = lambda k: [pl.BlockSpec(memory_space=pl.ANY)] * k
    done = pl.pallas_call(
        functools.partial(reduce_kernel, n, colors, ROWS, loads, saves, len(grads), len(shapes)),
        out_shape=(*(jax.ShapeDtypeStruct(shape, BF16) for shape in shapes), jax.ShapeDtypeStruct(tiny.shape, F32)),
        in_specs=hbm(len(grads)) + vmem(1), out_specs=tuple(hbm(len(shapes)) + vmem(1)),
        scratch_shapes=[
            pltpu.VMEM((nc, ROWS, width), BF16), pltpu.VMEM((nc, got_rows, width), BF16),
            pltpu.VMEM((nc, ROWS, width), BF16), pltpu.VMEM(tiny.shape, F32),
            pltpu.VMEM((bits + 1,) + tiny.shape, F32),
            pltpu.SemaphoreType.DMA((nc, 2)), pltpu.SemaphoreType.DMA((nc, 2)),
            pltpu.SemaphoreType.DMA((nc, stages)), pltpu.SemaphoreType.DMA((nc, stages)),
            pltpu.SemaphoreType.DMA((2, bits + 1)),
        ],
        compiler_params=pltpu.CompilerParams(collective_id=0, has_side_effects=True, vmem_limit_bytes=LIMIT),
        name="reduce_gradients",
    )(*grads, tiny)
    return done[:-1], done[-1]
def on_device(n_batch, inputs, prior_scores, lengths, w_query, w_key, w_value, b_query, b_value, w_output, b_output,
              gain_attn, shift_attn, w_inner, b_inner, w_outer, b_outer, gain_ffn, shift_ffn, grad_out, grad_scores):
    width = inputs.shape[2]
    bias = jnp.stack([b_query, b_value]).astype(F32)
    vec = jnp.stack([b_output, gain_attn, shift_attn, b_outer, gain_ffn, shift_ffn]).astype(F32)
    rows, q, k, v = project_rows(inputs, w_query, w_key, w_value, bias)
    new_scores, context, norm = attend(lengths, q, k, v, prior_scores)
    firsts, _ = grid_bits(n_batch)
    chunks = w_inner.size // (ROWS * width)
    counts = [chunks * sum(min(color, 2) == axis for color in EARLY_MIX) // len(EARLY_MIX) for axis in range(3)]
    outputs, dz1, dc, g_wo, keep, *gives, small, g_bi = middle(
        context, inputs, w_output, w_inner, w_outer, vec, b_inner.astype(F32)[None], grad_out, firsts, counts, ROWS)
    taken = [lax.ppermute(give, "batch", [(i, flip(i, first)) for i in range(n_batch)])
             for give, first in zip(gives, firsts)]
    grad_prior, dq, dk, dv = attend_back(lengths, q, k, v, dc, prior_scores, norm, grad_scores)
    grad_inputs, g_wq, g_wk, g_wv, g_b = project_back(rows, dq, dk, dv, w_query, w_key, w_value, dz1)
    pad = lambda a, to: jnp.pad(a, ((0, to - a.shape[0]), (0, 0)))
    mine = jnp.concatenate([g_bi.reshape(-1, width), g_b.reshape(-1, width)])
    tiny = jnp.concatenate([pad(small, 8), pad(mine, 8)])
    late = (g_wo, g_wq, g_wk, g_wv)
    shapes = [w_inner.shape, w_outer.shape] + [g.shape for g in late]
    grads, tiny = reduce_gradients((keep, *taken), late, shapes, tiny, n_batch)
    g_wi, g_wf, g_wo, g_wq, g_wk, g_wv = [g.astype(F32) for g in grads]
    g_bi = tiny[8:8 + g_bi.size // width].reshape(-1)
    g_b = tiny[8 + g_bi.size // width:8 + mine.shape[0]].reshape(g_b.shape)
    return (outputs, new_scores, grad_inputs, grad_prior, g_wq, g_wk, g_wv, g_b[0], g_b[1], g_wo,
            tiny[0], tiny[1], tiny[2], g_wi, g_bi, g_wf, tiny[3], tiny[4], tiny[5])


def solution(mesh):
    seq, scores, whole = P("batch", "head", None), P("batch", "head", None, None), P()
    down, across, vector = P("head", None), P(None, "head"), P("head")
    in_specs = (seq, scores, P("batch"), across, across, across, vector, vector, down, whole, whole, whole,
                across, vector, down, whole, whole, whole, seq, scores)
    out_specs = (seq, scores, seq, scores, across, across, across, vector, vector, down, whole, whole, whole,
                 across, vector, down, whole, whole, whole)
    layer = functools.partial(on_device, mesh.shape["batch"])
    return jax.shard_map(layer, mesh=mesh, in_specs=in_specs, out_specs=out_specs, check_vma=False)
```

```python
import functools
import jax, jax.numpy as jnp
from jax import lax
from jax.experimental import pallas as pl
from jax.experimental.pallas import tpu as pltpu
from jax.sharding import PartitionSpec as P

MESH = pl.DeviceIdType.MESH
F32, BF16 = jnp.float32, jnp.bfloat16
EPS = 1e-12
NEG = -1e30
LIMIT = 64 * 1000 * 1000


def dot(a, b):
    return jnp.dot(a, b, preferred_element_type=F32)


def dot_t(a, b):
    return lax.dot_general(a, b, (((1,), (1,)), ((), ())), preferred_element_type=F32)


def t_dot(a, b):
    return lax.dot_general(a, b, (((0,), (0,)), ((), ())), preferred_element_type=F32)


def meet(partner):
    barrier = pltpu.get_barrier_semaphore()
    pl.semaphore_signal(barrier, inc=1, device_id={"head": partner}, device_id_type=MESH)
    pl.semaphore_wait(barrier, 1)


def to_partner(src, dst, sems, i, partner):
    return pltpu.make_async_remote_copy(
        src_ref=src, dst_ref=dst, send_sem=sems.at[0, i], recv_sem=sems.at[1, i],
        device_id={"head": partner}, device_id_type=MESH)


def vmem(count):
    return [pl.BlockSpec(memory_space=pltpu.VMEM)] * count


def as_row(vector):
    return vector[...].astype(F32).reshape(1, vector.shape[0])


def project_kernel(seqs, part, x, wq, wk, wv, b_query, b_value, rows, q, k, v, got, sems):
    me = lax.axis_index("head")
    other = 1 - me
    meet(other)
    for s in range(seqs):
        to_partner(x.at[s], got.at[s], sems, s, other).start()

    bias_q, bias_v = as_row(b_query), as_row(b_value)

    def emit(block, s, p):
        at = pl.ds(pl.multiple_of((2 * s + p) * part, part), part)
        rows[at, :] = block
        q[at, :] = (dot(block, wq[...]) + bias_q).astype(BF16)
        k[at, :] = dot(block, wk[...]).astype(BF16)
        v[at, :] = (dot(block, wv[...]) + bias_v).astype(BF16)

    def own(s, _):
        emit(x[s], s, me)
        return 0

    lax.fori_loop(0, seqs, own, 0)
    for s in range(seqs):
        to_partner(x.at[s], got.at[s], sems, s, other).wait()

    def theirs(s, _):
        emit(got[s], s, other)
        return 0

    lax.fori_loop(0, seqs, theirs, 0)


def project_rows(x, wq, wk, wv, b_query, b_value):
    seqs, part, width = x.shape
    total, cols = 2 * seqs * part, wq.shape[1]
    out = jax.ShapeDtypeStruct((total, cols), BF16)
    return pl.pallas_call(
        functools.partial(project_kernel, seqs, part),
        out_shape=(jax.ShapeDtypeStruct((total, width), BF16), out, out, out),
        in_specs=vmem(6), out_specs=tuple(vmem(4)),
        scratch_shapes=[pltpu.VMEM(x.shape, BF16), pltpu.SemaphoreType.DMA((2, seqs))],
        compiler_params=pltpu.CompilerParams(collective_id=1, has_side_effects=True, vmem_limit_bytes=LIMIT),
        name="project_rows",
    )(x, wq, wk, wv, b_query, b_value)


def attend_kernel(block, head, lengths, q, k, v, prior, score, c, norm):
    full = k.shape[0]
    live = lax.broadcasted_iota(jnp.int32, (1, full), 1) < lengths[pl.program_id(0)]
    first = lax.broadcasted_iota(jnp.int32, (1, 2 * head), 1) < head
    scale = head ** -0.5
    for r in range(0, full, block):
        rows = pl.ds(r, block)
        queries = q[rows, :]
        parts, norms = [], []
        for h in range(2):
            mine = jnp.where(first == (h == 0), queries, jnp.zeros_like(queries))
            scores = dot_t(mine, k[...]) * scale + prior[0, h, rows, :].astype(F32)
            score[0, h, rows, :] = scores.astype(BF16)
            masked = jnp.where(live, scores, NEG)
            top = jnp.max(masked, axis=-1, keepdims=True)
            terms = jnp.exp(masked - top)
            total = jnp.sum(terms, axis=-1, keepdims=True)
            probs = (terms * (1.0 / total)).astype(BF16)
            parts.append(dot(probs, v[...]))
            norms.append(top + jnp.log(total))
        c[rows, :] = jnp.where(first, parts[0], parts[1]).astype(BF16)
        norm[0, 0, rows, :] = jnp.where(first, norms[0], norms[1])


def attend(lengths, q, k, v, prior):
    seqs, heads, full, _ = prior.shape
    pair = q.shape[1] // heads * 2
    rows = pl.BlockSpec((full, pair), lambda s, h, n: (s, h))
    big = pl.BlockSpec((1, 2, full, full), lambda s, h, n: (s, h, 0, 0))
    norm = pl.BlockSpec((1, 1, full, pair), lambda s, h, n: (s, h, 0, 0))
    return pl.pallas_call(
        functools.partial(attend_kernel, 256, pair // 2),
        grid_spec=pltpu.PrefetchScalarGridSpec(
            num_scalar_prefetch=1, grid=(seqs, heads // 2),
            in_specs=[rows, rows, rows, big], out_specs=(big, rows, norm)),
        out_shape=(jax.ShapeDtypeStruct(prior.shape, BF16), jax.ShapeDtypeStruct(q.shape, BF16),
                   jax.ShapeDtypeStruct((seqs, heads // 2, full, pair), F32)),
        compiler_params=pltpu.CompilerParams(vmem_limit_bytes=LIMIT),
        name="attend",
    )(lengths, q, k, v, prior)


def attend_back_kernel(block, head, lengths, q, k, v, dc, prior, norm, given, grad, dq, dk, dv):
    full = k.shape[0]
    live = lax.broadcasted_iota(jnp.int32, (1, full), 1) < lengths[pl.program_id(0)]
    first = lax.broadcasted_iota(jnp.int32, (1, 2 * head), 1) < head
    scale = head ** -0.5
    q_t, dc_t = q[...].T, dc[...].T
    dk_t, dv_t = [0.0, 0.0], [0.0, 0.0]
    for r in range(0, full, block):
        rows = pl.ds(r, block)
        queries, cots = q[rows, :], dc[rows, :]
        parts = []
        for h in range(2):
            mine = first == (h == 0)
            scores = dot_t(jnp.where(mine, queries, jnp.zeros_like(queries)), k[...]) * scale
            scores = scores + prior[0, h, rows, :].astype(F32)
            probs = jnp.exp(jnp.where(live, scores, NEG) - norm[0, 0, rows, h * head:h * head + 1])
            dp = dot_t(jnp.where(mine, cots, jnp.zeros_like(cots)), v[...])
            delta = jnp.sum(probs * dp, axis=-1, keepdims=True)
            ds = (probs * (dp - delta) + given[0, h, rows, :].astype(F32)).astype(BF16)
            grad[0, h, rows, :] = ds
            parts.append(dot(ds, k[...]))
            lanes = slice(h * head, (h + 1) * head)
            dk_t[h] = dk_t[h] + dot(q_t[lanes, r:r + block], ds)
            dv_t[h] = dv_t[h] + dot(dc_t[lanes, r:r + block], probs.astype(BF16))
        dq[rows, :] = (jnp.where(first, parts[0], parts[1]) * scale).astype(BF16)
    dk[...] = (jnp.concatenate(dk_t, axis=0) * scale).T.astype(BF16)
    dv[...] = jnp.concatenate(dv_t, axis=0).T.astype(BF16)


def attend_back(lengths, q, k, v, dc, prior, norm, given):
    seqs, heads, full, _ = prior.shape
    pair = q.shape[1] // heads * 2
    rows = pl.BlockSpec((full, pair), lambda s, h, n: (s, h))
    big = pl.BlockSpec((1, 2, full, full), lambda s, h, n: (s, h, 0, 0))
    norms = pl.BlockSpec((1, 1, full, pair), lambda s, h, n: (s, h, 0, 0))
    flat = jax.ShapeDtypeStruct(q.shape, BF16)
    return pl.pallas_call(
        functools.partial(attend_back_kernel, 256, pair // 2),
        grid_spec=pltpu.PrefetchScalarGridSpec(
            num_scalar_prefetch=1, grid=(seqs, heads // 2),
            in_specs=[rows, rows, rows, rows, big, norms, big], out_specs=(big, rows, rows, rows)),
        out_shape=(jax.ShapeDtypeStruct(prior.shape, BF16), flat, flat, flat),
        compiler_params=pltpu.CompilerParams(vmem_limit_bytes=LIMIT),
        cost_estimate=pl.CostEstimate(flops=40 * full * full * seqs * heads * pair // 2, transcendentals=prior.size,
                                      bytes_accessed=6 * prior.size),
        name="attend_back",
    )(lengths, q, k, v, dc, prior, norm, given)


def fold(value):
    return jnp.sum(value.reshape(value.shape[0] // 8, 8, value.shape[1]), axis=0)


def norm_stats(z):
    mean = jnp.mean(z, axis=-1, keepdims=True)
    centred = z - mean
    r = lax.rsqrt(jnp.mean(centred * centred, axis=-1, keepdims=True) + EPS)
    return centred * r, r


def norm_back(cot, gain, unit, r):
    e = cot * gain
    return r * (e - jnp.mean(e, axis=-1, keepdims=True) - unit * jnp.mean(e * unit, axis=-1, keepdims=True))


def middle_kernel(seqs, part, firsts, c, x, wo, wi, wf, b_output, gain1, shift1, b_outer, gain2, shift2, b_inner, gout,
                  out, dz1, dc, g_wo, keep, give_x, give_y, small, g_bi,
                  unit1, r1, dz2, hn, act, slope, df, du, da, give, got, own, sums, bsum, bi, sems):
    me = lax.axis_index("head")
    other = 1 - me
    width = x.shape[2]
    hidden = wi.shape[1]
    tile = 512
    sub = 64
    meet(other)
    b_output, gain1, shift1, b_outer, gain2, shift2 = map(as_row, (b_output, gain1, shift1, b_outer, gain2, shift2))
    sums[...] = jnp.zeros_like(sums)
    bsum[...] = jnp.zeros_like(bsum)
    bi[...] = as_row(b_inner)

    def rows_of(s, p):
        return pl.ds(pl.multiple_of((2 * s + p) * part, part), part)

    def at(start, size):
        return pl.ds(pl.multiple_of(start, size), size)

    def attn_part(s, _):
        give[s] = dot(c[rows_of(s, other), :], wo[...]).astype(BF16)
        return 0
    for s in range(seqs):
        attn_part(s, 0)
        to_partner(give.at[s], got.at[0, s], sems, s, other).start()

    def attn_own(s, _):
        own[s] = dot(c[rows_of(s, me), :], wo[...]).astype(BF16)
        return 0
    lax.fori_loop(0, seqs, attn_own, 0)
    for s in range(seqs):
        to_partner(give.at[s], got.at[0, s], sems, s, other).wait()

        def first_norm(i, _):
            rows = at(i * sub, sub)
            z = x[s, rows, :].astype(F32) + (own[s, rows, :].astype(F32) + got[0, s, rows, :].astype(F32)) + b_output
            unit, r = norm_stats(z)
            unit1[s, rows, :] = unit
            r1[s, rows, :] = jnp.broadcast_to(r, (sub, 128))
            hn[at((2 * s + me) * part + i * sub, sub), :] = (unit * gain1 + shift1).astype(BF16)
            return 0
        lax.fori_loop(0, part // sub, first_norm, 0)
        block = hn.at[rows_of(s, me)]
        to_partner(block, block, sems, seqs + s, other).start()

    order = [(0, me)] + [(s, other) for s in range(seqs)] + [(s, me) for s in range(1, seqs)]

    def inner(s, p):
        rows = rows_of(s, p)

        def columns(j, _):
            cols = at(j * tile, tile)
            u = dot(hn[rows, :], wi[:, cols]) + bi[:, cols]
            cdf = 0.5 * (1.0 + lax.erf(u * 0.7071067811865476))
            act[rows, cols] = (u * cdf).astype(BF16)
            slope[rows, cols] = cdf + u * (jnp.exp(-0.5 * u * u) * 0.3989422804014327)
            return 0
        lax.fori_loop(0, hidden // tile, columns, 0)

    def outer(s, p, place):
        rows = rows_of(s, p)

        def columns(j, _):
            cols = at(j * tile, tile)
            place[s, :, cols] = dot(act[rows, :], wf[:, cols]).astype(BF16)
            return 0
        lax.fori_loop(0, width // tile, columns, 0)

    for n, (s, p) in enumerate(order):
        if n == 1:
            for q in range(seqs):
                block = hn.at[rows_of(q, me)]
                to_partner(block, block, sems, seqs + q, other).wait()
        inner(s, p)
        if p is other:
            outer(s, p, give.at[pl.ds(seqs, seqs)])
            to_partner(give.at[seqs + s], got.at[1, s], sems, 2 * seqs + s, other).start()
        else:
            outer(s, p, own)

    for s in range(seqs):
        to_partner(give.at[seqs + s], got.at[1, s], sems, 2 * seqs + s, other).wait()

        def second_norm(i, _):
            rows = at(i * sub, sub)
            h = unit1[s, rows, :] * gain1 + shift1
            z = (own[s, rows, :].astype(F32) + got[1, s, rows, :].astype(F32)) + b_outer + h
            unit, r = norm_stats(z)
            out[s, rows, :] = (unit * gain2 + shift2).astype(BF16)
            g = gout[s, rows, :].astype(F32)
            d = norm_back(g, gain2, unit, r)
            dz2[s, rows, :] = d
            df[at((2 * s + me) * part + i * sub, sub), :] = d.astype(BF16)
            sums[3] += fold(d)
            sums[4] += fold(g * unit)
            sums[5] += fold(g)
            return 0
        lax.fori_loop(0, part // sub, second_norm, 0)
        block = df.at[rows_of(s, me)]
        to_partner(block, block, sems, 3 * seqs + s, other).start()

    def inner_back(s, p):
        rows = rows_of(s, p)

        def columns(j, _):
            cols = at(j * tile, tile)
            dg = dot_t(df[rows, :], wf[cols, :]).astype(BF16).astype(F32)
            low = (dg * slope[rows, cols]).astype(BF16)
            du[rows, cols] = low
            bsum[:, cols] += fold(low.astype(F32))
            return 0
        lax.fori_loop(0, hidden // tile, columns, 0)

    def outer_back(s, p, place):
        rows = rows_of(s, p)

        def columns(j, _):
            cols = at(j * tile, tile)
            place[s, :, cols] = dot_t(du[rows, :], wi[cols, :]).astype(BF16)
            return 0
        lax.fori_loop(0, width // tile, columns, 0)

    for n, (s, p) in enumerate(order):
        if n == 1:
            for q in range(seqs):
                block = df.at[rows_of(q, me)]
                to_partner(block, block, sems, 3 * seqs + q, other).wait()
        inner_back(s, p)
        if p is other:
            outer_back(s, p, give.at[pl.ds(2 * seqs, seqs)])
            to_partner(give.at[2 * seqs + s], got.at[2, s], sems, 4 * seqs + s, other).start()
        else:
            outer_back(s, p, own)

    for s in range(seqs):
        to_partner(give.at[2 * seqs + s], got.at[2, s], sems, 4 * seqs + s, other).wait()

        def first_back(i, _):
            rows = at(i * sub, sub)
            cot = dz2[s, rows, :] + (own[s, rows, :].astype(F32) + got[2, s, rows, :].astype(F32))
            unit = unit1[s, rows, :]
            d = norm_back(cot, gain1, unit, r1[s, rows, 0:1])
            dz1[s, rows, :] = d
            da[at((2 * s + me) * part + i * sub, sub), :] = d.astype(BF16)
            sums[0] += fold(d)
            sums[1] += fold(cot * unit)
            sums[2] += fold(cot)
            return 0
        lax.fori_loop(0, part // sub, first_back, 0)
        block = da.at[rows_of(s, me)]
        to_partner(block, block, sems, 5 * seqs + s, other).start()

    mine = lax.axis_index("batch")
    gives = (give_x, give_y)
    half = keep.shape[1]
    per = hidden // width

    def put(value, kept, axis, given):
        bit = (mine // (1 << firsts[axis])) % 2

        @pl.when(bit == 0)
        def _():
            keep[kept] = value[:half].astype(BF16)
            gives[axis][given] = value[half:].astype(BF16)

        @pl.when(bit == 1)
        def _():
            keep[kept] = value[half:].astype(BF16)
            gives[axis][given] = value[:half].astype(BF16)

    def grads_of(axis, start, count):
        def grad_outer(i, _):
            at_act = at((start + i) * 2 * half, 2 * half)
            put(t_dot(act[:, at_act], df[...]), early + start + i, axis, count + i)
            return 0

        def grad_inner(i, _):
            at_hn, at_du = at((start + i) // per * 2 * half, 2 * half), at((start + i) % per * width, width)
            put(t_dot(hn[:, at_hn], du[:, at_du]), start + i, axis, i)
            return 0

        lax.fori_loop(0, count, grad_inner, 0)
        lax.fori_loop(0, count, grad_outer, 0)

    early = keep.shape[0] // 2
    begin = 0
    for axis in range(2):
        grads_of(axis, begin, gives[axis].shape[0] // 2)
        begin += gives[axis].shape[0] // 2

    for s in range(seqs):
        block = da.at[rows_of(s, me)]
        to_partner(block, block, sems, 5 * seqs + s, other).wait()
    dc[...] = dot_t(da[...], wo[...]).astype(BF16)
    g_wo[...] = t_dot(c[...], da[...]).astype(BF16)
    small[...] = jnp.sum(sums[...], axis=1)
    g_bi[...] = jnp.sum(bsum[...], axis=0, keepdims=True)


def middle(c, x, wo, wi, wf, vectors, gout, firsts, counts, rows):
    seqs, part, width = x.shape
    total, cols = c.shape
    hidden = wi.shape[1]
    sds = jax.ShapeDtypeStruct
    halves = [sds((2 * count, rows // 2, width), BF16) for count in (sum(counts), *counts)]
    return pl.pallas_call(
        functools.partial(middle_kernel, seqs, part, firsts),
        out_shape=(sds(x.shape, BF16), sds(x.shape, F32), sds(c.shape, BF16), sds(wo.shape, BF16),
                   *halves, sds((6, width), F32), sds((1, hidden), F32)),
        in_specs=vmem(6 + len(vectors)), out_specs=tuple(vmem(9)),
        scratch_shapes=[
            pltpu.VMEM(x.shape, F32), pltpu.VMEM((seqs, part, 128), F32), pltpu.VMEM(x.shape, F32),
            pltpu.VMEM((total, width), BF16), pltpu.VMEM((total, hidden), BF16), pltpu.VMEM((total, hidden), F32),
            pltpu.VMEM((total, width), BF16), pltpu.VMEM((total, hidden), BF16), pltpu.VMEM((total, width), BF16),
            pltpu.VMEM((3 * seqs, part, width), BF16), pltpu.VMEM((3, seqs, part, width), BF16),
            pltpu.VMEM(x.shape, BF16), pltpu.VMEM((6, 8, width), F32), pltpu.VMEM((8, hidden), F32),
            pltpu.VMEM((1, hidden), F32),
            pltpu.SemaphoreType.DMA((2, 6 * seqs)),
        ],
        compiler_params=pltpu.CompilerParams(collective_id=2, has_side_effects=True, vmem_limit_bytes=LIMIT),
        cost_estimate=pl.CostEstimate(flops=14 * total * width * hidden, transcendentals=total * hidden,
                                      bytes_accessed=30 << 20),
        name="middle",
    )(c, x, wo, wi, wf, *vectors, gout)


def project_back_kernel(seqs, part, rows, dq, dk, dv, wq, wk, wv, dz1,
                        gin, g_q, g_k, g_v, g_b, give, got, sems):
    me = lax.axis_index("head")
    other = 1 - me
    meet(other)

    def total_of(s, p):
        at = pl.ds(pl.multiple_of((2 * s + p) * part, part), part)
        return dot_t(dq[at, :], wq[...]) + dot_t(dk[at, :], wk[...]) + dot_t(dv[at, :], wv[...])

    for s in range(seqs):
        give[s] = total_of(s, other).astype(BF16)
        to_partner(give.at[s], got.at[s], sems, s, other).start()
    g_q[...] = t_dot(rows[...], dq[...]).astype(BF16)
    g_k[...] = t_dot(rows[...], dk[...]).astype(BF16)
    g_v[...] = t_dot(rows[...], dv[...]).astype(BF16)
    g_b[0:1, :] = jnp.sum(fold(dq[...].astype(F32)), axis=0, keepdims=True)
    g_b[1:2, :] = jnp.sum(fold(dv[...].astype(F32)), axis=0, keepdims=True)
    for s in range(seqs):
        own = total_of(s, me).astype(BF16)
        to_partner(give.at[s], got.at[s], sems, s, other).wait()
        gin[s] = (dz1[s] + (own.astype(F32) + got[s].astype(F32))).astype(BF16)


def project_back(rows, dq, dk, dv, wq, wk, wv, dz1):
    seqs, part, width = dz1.shape
    sds = jax.ShapeDtypeStruct
    grad = sds(wq.shape, BF16)
    return pl.pallas_call(
        functools.partial(project_back_kernel, seqs, part),
        out_shape=(sds(dz1.shape, BF16), grad, grad, grad, sds((2, wq.shape[1]), F32)),
        in_specs=vmem(8), out_specs=tuple(vmem(5)),
        scratch_shapes=[pltpu.VMEM(dz1.shape, BF16), pltpu.VMEM(dz1.shape, BF16), pltpu.SemaphoreType.DMA((2, seqs))],
        compiler_params=pltpu.CompilerParams(collective_id=3, has_side_effects=True, vmem_limit_bytes=LIMIT),
        cost_estimate=pl.CostEstimate(flops=12 * rows.size * wq.shape[1], transcendentals=0, bytes_accessed=16 << 20),
        name="project_back",
    )(rows, dq, dk, dv, wq, wk, wv, dz1)
LINE = 16
ROWS = 256
LATE_COLORS = (0, 1, 2, 3, 0, 1, 2, 3)
PRECEDENCE = (29, 13, 18, 0, 6, 13, 11, 17, 6, 9, 1, 15, 15, 6, 22, 21, 13, 2, 9, 12, 8, 7, 35, 19)
LANDS = ("gather", "out", "back_in", "back_mid", "back_out")


def grid_bits(n):
    bits = n.bit_length() - 1
    side = bits // 3
    return (0, side, 2 * side), bits


def chunk_plan(n, color, rows):
    (bx, by, bz), bits = grid_bits(n)
    order = (by, bx) if color % 2 else (bx, by)
    line = n == LINE
    plan, length = [], rows
    if line and color >= 2:
        plan = [("far_in", bz, 3 * rows // 4), ("far_mid", bz, rows // 2), ("far_out", bz, rows // 4)]
        length = rows // 4
    if not line:
        order = (*order, bz)
    for b in order:
        length //= 2
        plan.append(("scatter", b, length))
    if line and color < 2:
        plan += [(kind, bz, length) for kind in ("in", "mid", "out")]
    plan += [("double", b, length) for b in range(bits) if not line and b not in order]
    for b in reversed(order):
        plan.append(("gather", b, length))
        length *= 2
    if line and color >= 2:
        plan += [("back_in", bz, rows // 4), ("back_mid", bz, rows // 2), ("back_out", bz, 3 * rows // 4)]
    return plan


def event_order(n, plans, rows):
    first, _ = grid_bits(n)
    lag = 0.16

    def path(kind, b):
        place = kind.split("_")[-1]
        if place in ("in", "mid", "out"):
            return ("in", "mid", "out").index(place) + 2
        return (b >= first[1]) + (b >= first[2])

    work = [[(path(kind, b), size / rows) for kind, b, size in plan] for plan in plans]
    free, ready, step, events = [0.0] * 5, [0.0] * len(plans), [0] * len(plans), []
    for _ in range(sum(map(len, work))):
        start, _, c = min((max(ready[c], free[row[step[c]][0]]), -PRECEDENCE[c % len(PRECEDENCE)], c)
                          for c, row in enumerate(work) if step[c] < len(row))
        link, span = work[c][step[c]]
        free[link] = start + span
        ready[c] = free[link] + lag
        events.append((start, c, step[c]))
        step[c] += 1
    events += [(r, c, len(work[c])) for c, r in enumerate(ready)]
    return [(c, s) for _, c, s in sorted(events)]


def flip(index, bit):
    return index + (1 - 2 * ((index // (1 << bit)) % 2)) * (1 << bit)


def chunk_pieces(shapes, rows, width):
    chunks = []
    for i, (height, cols) in enumerate(shapes):
        per = max(1, width // cols)
        for r in range(0, height, rows * per):
            for col in range(0, cols, width):
                span = min(cols, width)
                chunks.append([(i, r + j * rows, col, span, j * span) for j in range(per)])
    return chunks


def only(cond, body):
    if cond is None:
        body()
    else:
        pl.when(cond)(body)


def reduce_kernel(n, plans, rows, loads, saves, count, results, *refs):
    grads, (small, g_bi, g_b) = refs[:count], refs[count:count + 3]
    refs = refs[count + 3:]
    sums, tiny_out = refs[:results], refs[results]
    work, got, full, hold, tiny_got, load_sem, save_sem, send_sem, recv_sem, tiny_sem = refs[results + 1:]
    nc = len(plans)
    me, head = lax.axis_index("batch"), lax.axis_index("head")
    first, bits = grid_bits(n)
    bit_of = [(me // (1 << b)) % 2 for b in range(bits)]
    z = me // (1 << first[2])
    side = z // 2
    end = z % 3 == 0
    middle = z % 3 != 0
    mirror = me + (3 - 2 * z) * (1 << first[2])

    spans = []
    for plan in plans:
        off, length, at, row = 0, rows, 0, []
        quarter = rows // 4
        for kind, b, size in plan:
            where = None if kind in LANDS else at
            at += 0 if kind in LANDS else size
            if kind == "scatter":
                row.append((off + bit_of[b] * size, off + (1 - bit_of[b]) * size, size, where))
                off = row[-1][0]
            elif kind == "gather":
                row.append((off, off, size, where))
                off = off - bit_of[b] * size
            elif kind in ("far_in", "back_out"):
                row.append(((1 - side) * quarter, (1 - side) * quarter, size, where))
            elif kind == "far_mid":
                row.append((side * 2 * quarter, (1 - side) * 2 * quarter, size, where))
            elif kind == "back_mid":
                row.append((side * 2 * quarter, side * 2 * quarter, size, where))
            elif kind in ("far_out", "back_in"):
                row.append((side * 3 * quarter, side * 3 * quarter, size, where))
                off = z * quarter
            else:
                row.append((off, off, size, where))
        spans.append(row)

    def roles(kind):
        place = kind.split("_")[-1]
        return {"in": (end, middle), "mid": (middle, middle), "out": (middle, end)}.get(place, (None, None))

    def moves(c, out):
        if out:
            for k, (i, r, col, span, at) in enumerate(saves[c]):
                outside = sums[i].at[pl.ds(r, rows), pl.ds(col, span)]
                yield pltpu.make_async_copy(full.at[c, :, pl.ds(at, span)], outside, save_sem.at[c, k])
        elif loads[c] is None:
            for k, (i, r, col, span, at) in enumerate(saves[c]):
                outside = grads[i + count - results].at[pl.ds(r, rows), pl.ds(col, span)]
                yield pltpu.make_async_copy(outside, work.at[c, :, pl.ds(at, span)], load_sem.at[c, k])
        else:
            kept, kept_at, given, given_at = loads[c]
            keep, _, length, at = spans[c][0]
            inside = work.at[c, pl.ds(pl.multiple_of(keep, 16), length)]
            yield pltpu.make_async_copy(grads[kept].at[kept_at], inside, load_sem.at[c, 0])
            yield pltpu.make_async_copy(grads[given].at[given_at], got.at[c, pl.ds(at, length)], load_sem.at[c, 1])

    for c in range(nc):
        for move in moves(c, False):
            move.start()
    hold[...] = jnp.zeros_like(hold)
    hold[0:6, :] = small[...]
    width, row = hold.shape[1], 8
    for j in range(g_bi.shape[1] // width):
        hold[row:row + 1, :] = g_bi[:, j * width:(j + 1) * width]
        row += 1
    cols = g_b.shape[1]
    for j in range(2):
        hold[row + j * cols // width:row + j * cols // width + 1, pl.ds(j * cols % width, cols)] = g_b[j:j + 1, :]
    barrier = pltpu.get_barrier_semaphore()
    friends = [flip(me, b) for b in range(bits)] + ([mirror] if n == LINE else [])
    for friend in friends:
        pl.semaphore_signal(barrier, inc=1, device_id={"batch": friend}, device_id_type=MESH)
    pl.semaphore_signal(barrier, inc=1, device_id={"head": 1 - head}, device_id_type=MESH)
    pl.semaphore_wait(barrier, len(friends) + 1)

    def copy_of(c, s):
        kind, b, _ = plans[c][s]
        _, start, length, at = spans[c][s]
        place = (c, pl.ds(pl.multiple_of(start, 16), length))
        src = full.at[place] if kind in LANDS else work.at[place]
        dst = full.at[place] if kind in LANDS else got.at[c, pl.ds(at, length)]
        return pltpu.make_async_remote_copy(
            src_ref=src, dst_ref=dst, send_sem=send_sem.at[c, s], recv_sem=recv_sem.at[c, s],
            device_id={"batch": mirror if kind.endswith("mid") else flip(me, b)}, device_id_type=MESH)

    def finish(c, s):
        kind = plans[c][s][0]
        keep, _, length, at = spans[c][s]
        sender, receiver = roles(kind)
        if s == 0 and loads[c] is not None:
            for move in moves(c, False):
                move.wait()
        else:
            only(sender, lambda: copy_of(c, s).wait_send())

        def take():
            if s > 0 or loads[c] is None:
                copy_of(c, s).wait_recv()
            if kind in LANDS:
                return
            target = full if plans[c][s + 1][0] in LANDS else work

            def add(i, _):
                here = pl.ds(pl.multiple_of(keep + i * 16, 16), 16)
                there = pl.ds(pl.multiple_of(at + i * 16, 16), 16)
                target[c, here, :] = (work[c, here, :].astype(F32) + got[c, there, :].astype(F32)).astype(BF16)
                return 0
            lax.fori_loop(0, length // 16, add, 0)
        only(receiver, take)

    def tiny_copy(k):
        rest = hold.at[pl.ds(0, 8)] if k == 0 else hold
        there = tiny_got.at[k, pl.ds(0, 8)] if k == 0 else tiny_got.at[k]
        target = {"head": 1 - head} if k == 0 else {"batch": flip(me, k - 1)}
        return pltpu.make_async_remote_copy(
            src_ref=rest, dst_ref=there, send_sem=tiny_sem.at[0, k], recv_sem=tiny_sem.at[1, k],
            device_id=target, device_id_type=MESH)

    def tiny_finish(k):
        tiny_copy(k).wait()
        if k == 0:
            hold[0:8, :] += tiny_got[0, 0:8, :]
        else:
            hold[...] += tiny_got[k]

    done = [load is not None for load in loads]
    events = [(c, s + done[c]) for c, s in event_order(n, [p[d:] for p, d in zip(plans, done)], rows)]
    gap = len(events) // (bits + 2)
    for e, (c, s) in enumerate(events):
        if s == 0:
            for move in moves(c, False):
                move.wait()
        else:
            finish(c, s - 1)
        if s == len(plans[c]):
            for move in moves(c, True):
                move.start()
        else:
            only(roles(plans[c][s][0])[0], lambda: copy_of(c, s).start())
        if e % gap == 0 and e // gap <= bits:
            k = e // gap
            if k > 0:
                tiny_finish(k - 1)
            tiny_copy(k).start()
    tiny_finish(bits)
    tiny_out[...] = hold[...]
    for c in range(nc):
        for move in moves(c, True):
            move.wait()


def reduce_gradients(early, late, shapes, tiny, n):
    width = tiny[0].shape[1]
    tiny_shape = (16, width)
    saves = chunk_pieces(shapes, ROWS, width)
    count = early[0].shape[0] // 2
    slots, plans, loads = [0, 0], [], []
    for which in range(2):
        for c in range(count):
            color = c * 2 // count
            loads.append((0, which * count + c, 1 + color, slots[color]))
            slots[color] += 1
            plans.append(chunk_plan(n, color, ROWS))
    for c in range(len(saves) - 2 * count):
        plans.append(chunk_plan(n, LATE_COLORS[c % len(LATE_COLORS)], ROWS))
        loads.append(None)
    nc = len(saves)
    stages = max(len(plan) for plan in plans)
    _, bits = grid_bits(n)
    got_rows = max(sum(size for kind, _, size in plan if kind not in LANDS) for plan in plans)
    grads = (*early, *late)
    hbm = lambda k: [pl.BlockSpec(memory_space=pl.ANY)] * k
    done = pl.pallas_call(
        functools.partial(reduce_kernel, n, plans, ROWS, loads, saves, len(grads), len(shapes)),
        out_shape=(*(jax.ShapeDtypeStruct(shape, BF16) for shape in shapes), jax.ShapeDtypeStruct(tiny_shape, F32)),
        in_specs=hbm(len(grads)) + vmem(3), out_specs=tuple(hbm(len(shapes)) + vmem(1)),
        scratch_shapes=[
            pltpu.VMEM((nc, ROWS, width), BF16), pltpu.VMEM((nc, got_rows, width), BF16),
            pltpu.VMEM((nc, ROWS, width), BF16), pltpu.VMEM(tiny_shape, F32),
            pltpu.VMEM((bits + 1,) + tiny_shape, F32),
            pltpu.SemaphoreType.DMA((nc, 2)), pltpu.SemaphoreType.DMA((nc, 2)),
            pltpu.SemaphoreType.DMA((nc, stages)), pltpu.SemaphoreType.DMA((nc, stages)),
            pltpu.SemaphoreType.DMA((2, bits + 1)),
        ],
        compiler_params=pltpu.CompilerParams(collective_id=0, has_side_effects=True, vmem_limit_bytes=LIMIT),
        name="reduce_gradients",
    )(*grads, *tiny)
    return done[:-1], done[-1]


def on_device(n_batch, inputs, prior_scores, lengths, w_query, w_key, w_value, b_query, b_value, w_output, b_output,
              gain_attn, shift_attn, w_inner, b_inner, w_outer, b_outer, gain_ffn, shift_ffn, grad_out, grad_scores):
    width = inputs.shape[2]
    vectors = (b_output, gain_attn, shift_attn, b_outer, gain_ffn, shift_ffn, b_inner)
    rows, q, k, v = project_rows(inputs, w_query, w_key, w_value, b_query, b_value)
    new_scores, context, norm = attend(lengths, q, k, v, prior_scores)
    firsts = grid_bits(n_batch)[0][:2]
    chunks = w_inner.size // (ROWS * width)
    counts = [chunks // 2] * 2
    outputs, dz1, dc, g_wo, keep, *gives, small, g_bi = middle(
        context, inputs, w_output, w_inner, w_outer, vectors, grad_out, firsts, counts, ROWS)
    taken = [lax.ppermute(give, "batch", [(i, flip(i, first)) for i in range(n_batch)])
             for give, first in zip(gives, firsts)]
    grad_prior, dq, dk, dv = attend_back(lengths, q, k, v, dc, prior_scores, norm, grad_scores)
    grad_inputs, g_wq, g_wk, g_wv, g_b = project_back(rows, dq, dk, dv, w_query, w_key, w_value, dz1)
    late = (g_wo, g_wq, g_wk, g_wv)
    shapes = [w_inner.shape, w_outer.shape] + [g.shape for g in late]
    grads, tiny = reduce_gradients((keep, *taken), late, shapes, (small, g_bi, g_b), n_batch)
    g_wi, g_wf, g_wo, g_wq, g_wk, g_wv = [g.astype(F32) for g in grads]
    g_bi = tiny[8:8 + g_bi.size // width].reshape(-1)
    g_b = tiny[8 + g_bi.size // width:][:g_b.size // width].reshape(g_b.shape)
    return (outputs, new_scores, grad_inputs, grad_prior, g_wq, g_wk, g_wv, g_b[0], g_b[1], g_wo,
            tiny[0], tiny[1], tiny[2], g_wi, g_bi, g_wf, tiny[3], tiny[4], tiny[5])


def solution(mesh):
    seq, scores, whole = P("batch", "head", None), P("batch", "head", None, None), P()
    down, across, vector = P("head", None), P(None, "head"), P("head")
    in_specs = (seq, scores, P("batch"), across, across, across, vector, vector, down, whole, whole, whole,
                across, vector, down, whole, whole, whole, seq, scores)
    out_specs = (seq, scores, seq, scores, across, across, across, vector, vector, down, whole, whole, whole,
                 across, vector, down, whole, whole, whole)
    layer = functools.partial(on_device, mesh.shape["batch"])
    return jax.shard_map(layer, mesh=mesh, in_specs=in_specs, out_specs=out_specs, check_vma=False)
```

```python
import functools
import jax, jax.numpy as jnp
from jax import lax
from jax.experimental import pallas as pl
from jax.experimental.pallas import tpu as pltpu
from jax.sharding import PartitionSpec as P

MESH = pl.DeviceIdType.MESH
F32, BF16 = jnp.float32, jnp.bfloat16
EPS = 1e-12
NEG = -1e30
LIMIT = 64 * 1000 * 1000


def dot(a, b):
    return jnp.dot(a, b, preferred_element_type=F32)


def dot_t(a, b):
    return lax.dot_general(a, b, (((1,), (1,)), ((), ())), preferred_element_type=F32)


def t_dot(a, b):
    return lax.dot_general(a, b, (((0,), (0,)), ((), ())), preferred_element_type=F32)


def meet(partner):
    barrier = pltpu.get_barrier_semaphore()
    pl.semaphore_signal(barrier, inc=1, device_id={"head": partner}, device_id_type=MESH)
    pl.semaphore_wait(barrier, 1)


def to_partner(src, dst, sems, i, partner):
    return pltpu.make_async_remote_copy(
        src_ref=src, dst_ref=dst, send_sem=sems.at[0, i], recv_sem=sems.at[1, i],
        device_id={"head": partner}, device_id_type=MESH)


def vmem(count):
    return [pl.BlockSpec(memory_space=pltpu.VMEM)] * count


def as_row(vector):
    return vector[...].astype(F32).reshape(1, vector.shape[0])


def project_kernel(seqs, part, x, wq, wk, wv, b_query, b_value, rows, q, k, v, got, sems):
    me = lax.axis_index("head")
    other = 1 - me
    meet(other)
    for s in range(seqs):
        to_partner(x.at[s], got.at[s], sems, s, other).start()

    bias_q, bias_v = as_row(b_query), as_row(b_value)

    def emit(block, s, p):
        at = pl.ds(pl.multiple_of((2 * s + p) * part, part), part)
        rows[at, :] = block
        q[at, :] = (dot(block, wq[...]) + bias_q).astype(BF16)
        k[at, :] = dot(block, wk[...]).astype(BF16)
        v[at, :] = (dot(block, wv[...]) + bias_v).astype(BF16)

    def own(s, _):
        emit(x[s], s, me)
        return 0

    lax.fori_loop(0, seqs, own, 0)
    for s in range(seqs):
        to_partner(x.at[s], got.at[s], sems, s, other).wait()

    def theirs(s, _):
        emit(got[s], s, other)
        return 0

    lax.fori_loop(0, seqs, theirs, 0)


def project_rows(x, wq, wk, wv, b_query, b_value):
    seqs, part, width = x.shape
    total, cols = 2 * seqs * part, wq.shape[1]
    out = jax.ShapeDtypeStruct((total, cols), BF16)
    return pl.pallas_call(
        functools.partial(project_kernel, seqs, part),
        out_shape=(jax.ShapeDtypeStruct((total, width), BF16), out, out, out),
        in_specs=vmem(6), out_specs=tuple(vmem(4)),
        scratch_shapes=[pltpu.VMEM(x.shape, BF16), pltpu.SemaphoreType.DMA((2, seqs))],
        compiler_params=pltpu.CompilerParams(collective_id=1, has_side_effects=True, vmem_limit_bytes=LIMIT),
        name="project_rows",
    )(x, wq, wk, wv, b_query, b_value)


def attend_kernel(block, head, lengths, q, k, v, prior, score, c, norm):
    full = k.shape[0]
    live = lax.broadcasted_iota(jnp.int32, (1, full), 1) < lengths[pl.program_id(0)]
    first = lax.broadcasted_iota(jnp.int32, (1, 2 * head), 1) < head
    scale = head ** -0.5
    for r in range(0, full, block):
        rows = pl.ds(r, block)
        queries = q[rows, :] * jnp.asarray(scale, BF16)
        parts, norms = [], []
        for h in range(2):
            mine = jnp.where(first == (h == 0), queries, jnp.zeros_like(queries))
            scores = dot_t(mine, k[...]) + prior[0, h, rows, :].astype(F32)
            score[0, h, rows, :] = scores.astype(BF16)
            masked = jnp.where(live, scores, NEG)
            top = jnp.max(masked, axis=-1, keepdims=True)
            terms = jnp.exp(masked - top)
            total = jnp.sum(terms, axis=-1, keepdims=True)
            probs = (terms * (1.0 / total)).astype(BF16)
            parts.append(dot(probs, v[...]))
            norms.append(top + jnp.log(total))
        c[rows, :] = jnp.where(first, parts[0], parts[1]).astype(BF16)
        norm[0, 0, rows, :] = jnp.where(first, norms[0], norms[1])


def attend(lengths, q, k, v, prior):
    seqs, heads, full, _ = prior.shape
    pair = q.shape[1] // heads * 2
    rows = pl.BlockSpec((full, pair), lambda s, h, n: (s, h))
    big = pl.BlockSpec((1, 2, full, full), lambda s, h, n: (s, h, 0, 0))
    norm = pl.BlockSpec((1, 1, full, pair), lambda s, h, n: (s, h, 0, 0))
    return pl.pallas_call(
        functools.partial(attend_kernel, 256, pair // 2),
        grid_spec=pltpu.PrefetchScalarGridSpec(
            num_scalar_prefetch=1, grid=(seqs, heads // 2),
            in_specs=[rows, rows, rows, big], out_specs=(big, rows, norm)),
        out_shape=(jax.ShapeDtypeStruct(prior.shape, BF16), jax.ShapeDtypeStruct(q.shape, BF16),
                   jax.ShapeDtypeStruct((seqs, heads // 2, full, pair), F32)),
        compiler_params=pltpu.CompilerParams(vmem_limit_bytes=LIMIT),
        name="attend",
    )(lengths, q, k, v, prior)


def attend_back_kernel(block, head, lengths, q, k, v, dc, prior, norm, given, grad, dq, dk, dv):
    full = k.shape[0]
    live = lax.broadcasted_iota(jnp.int32, (1, full), 1) < lengths[pl.program_id(0)]
    first = lax.broadcasted_iota(jnp.int32, (1, 2 * head), 1) < head
    scale = head ** -0.5
    q_t, dc_t = q[...].T, dc[...].T
    dk_t, dv_t = [0.0, 0.0], [0.0, 0.0]
    for r in range(0, full, block):
        rows = pl.ds(r, block)
        queries, cots = q[rows, :] * jnp.asarray(scale, BF16), dc[rows, :]
        parts = []
        for h in range(2):
            mine = first == (h == 0)
            scores = dot_t(jnp.where(mine, queries, jnp.zeros_like(queries)), k[...])
            scores = scores + prior[0, h, rows, :].astype(F32)
            probs = jnp.exp(jnp.where(live, scores, NEG) - norm[0, 0, rows, h * head:h * head + 1])
            dp = dot_t(jnp.where(mine, cots, jnp.zeros_like(cots)), v[...])
            delta = jnp.sum(probs * dp, axis=-1, keepdims=True)
            ds = (probs * (dp - delta) + given[0, h, rows, :].astype(F32)).astype(BF16)
            grad[0, h, rows, :] = ds
            parts.append(dot(ds, k[...]))
            lanes = slice(h * head, (h + 1) * head)
            dk_t[h] = dk_t[h] + dot(q_t[lanes, r:r + block], ds)
            dv_t[h] = dv_t[h] + dot(dc_t[lanes, r:r + block], probs.astype(BF16))
        dq[rows, :] = (jnp.where(first, parts[0], parts[1]) * scale).astype(BF16)
    dk[...] = (jnp.concatenate(dk_t, axis=0) * scale).T.astype(BF16)
    dv[...] = jnp.concatenate(dv_t, axis=0).T.astype(BF16)


def attend_back(lengths, q, k, v, dc, prior, norm, given):
    seqs, heads, full, _ = prior.shape
    pair = q.shape[1] // heads * 2
    rows = pl.BlockSpec((full, pair), lambda s, h, n: (s, h))
    big = pl.BlockSpec((1, 2, full, full), lambda s, h, n: (s, h, 0, 0))
    norms = pl.BlockSpec((1, 1, full, pair), lambda s, h, n: (s, h, 0, 0))
    flat = jax.ShapeDtypeStruct(q.shape, BF16)
    return pl.pallas_call(
        functools.partial(attend_back_kernel, 256, pair // 2),
        grid_spec=pltpu.PrefetchScalarGridSpec(
            num_scalar_prefetch=1, grid=(seqs, heads // 2),
            in_specs=[rows, rows, rows, rows, big, norms, big], out_specs=(big, rows, rows, rows)),
        out_shape=(jax.ShapeDtypeStruct(prior.shape, BF16), flat, flat, flat),
        compiler_params=pltpu.CompilerParams(vmem_limit_bytes=LIMIT),
        cost_estimate=pl.CostEstimate(flops=40 * full * full * seqs * heads * pair // 2, transcendentals=prior.size,
                                      bytes_accessed=6 * prior.size),
        name="attend_back",
    )(lengths, q, k, v, dc, prior, norm, given)


def fold(value):
    return jnp.sum(value.reshape(value.shape[0] // 8, 8, value.shape[1]), axis=0)


def norm_stats(z):
    mean = jnp.mean(z, axis=-1, keepdims=True)
    centred = z - mean
    r = lax.rsqrt(jnp.mean(centred * centred, axis=-1, keepdims=True) + EPS)
    return centred * r, r


def norm_back(cot, gain, unit, r):
    e = cot * gain
    return r * (e - jnp.mean(e, axis=-1, keepdims=True) - unit * jnp.mean(e * unit, axis=-1, keepdims=True))


def middle_kernel(seqs, part, firsts, c, x, wo, wi, wf, b_output, gain1, shift1, b_outer, gain2, shift2, b_inner, gout,
                  out, dz1, dc, g_wo, keep, give_x, give_y, small, g_bi,
                  unit1, r1, dz2, hn, act, slope, df, du, da, give, got, own, sums, bsum, bi, sems):
    me = lax.axis_index("head")
    other = 1 - me
    width = x.shape[2]
    hidden = wi.shape[1]
    tile = 512
    sub = 64
    meet(other)
    b_output, gain1, shift1, b_outer, gain2, shift2 = map(as_row, (b_output, gain1, shift1, b_outer, gain2, shift2))
    sums[...] = jnp.zeros_like(sums)
    bsum[...] = jnp.zeros_like(bsum)
    bi[...] = as_row(b_inner)

    def rows_of(s, p):
        return pl.ds(pl.multiple_of((2 * s + p) * part, part), part)

    def at(start, size):
        return pl.ds(pl.multiple_of(start, size), size)

    def attn_part(s, _):
        give[s] = dot(c[rows_of(s, other), :], wo[...]).astype(BF16)
        return 0
    for s in range(seqs):
        attn_part(s, 0)
        to_partner(give.at[s], got.at[0, s], sems, s, other).start()

    def attn_own(s, _):
        own[s] = dot(c[rows_of(s, me), :], wo[...]).astype(BF16)
        return 0
    lax.fori_loop(0, seqs, attn_own, 0)
    for s in range(seqs):
        to_partner(give.at[s], got.at[0, s], sems, s, other).wait()

        def first_norm(i, _):
            rows = at(i * sub, sub)
            z = x[s, rows, :].astype(F32) + (own[s, rows, :].astype(F32) + got[0, s, rows, :].astype(F32)) + b_output
            unit, r = norm_stats(z)
            unit1[s, rows, :] = unit
            r1[s, rows, :] = jnp.broadcast_to(r, (sub, 128))
            hn[at((2 * s + me) * part + i * sub, sub), :] = (unit * gain1 + shift1).astype(BF16)
            return 0
        lax.fori_loop(0, part // sub, first_norm, 0)
        block = hn.at[rows_of(s, me)]
        to_partner(block, block, sems, seqs + s, other).start()

    order = [(0, me)] + [(s, other) for s in range(seqs)] + [(s, me) for s in range(1, seqs)]

    def inner(s, p):
        rows = rows_of(s, p)

        def columns(j, _):
            cols = at(j * tile, tile)
            u = dot(hn[rows, :], wi[:, cols]) + bi[:, cols]
            cdf = 0.5 * (1.0 + lax.erf(u * 0.7071067811865476))
            act[rows, cols] = (u * cdf).astype(BF16)
            slope[rows, cols] = cdf + u * (jnp.exp(-0.5 * u * u) * 0.3989422804014327)
            return 0
        lax.fori_loop(0, hidden // tile, columns, 0)

    def outer(s, p, place):
        rows = rows_of(s, p)

        def columns(j, _):
            cols = at(j * tile, tile)
            place[s, :, cols] = dot(act[rows, :], wf[:, cols]).astype(BF16)
            return 0
        lax.fori_loop(0, width // tile, columns, 0)

    for n, (s, p) in enumerate(order):
        if n == 1:
            for q in range(seqs):
                block = hn.at[rows_of(q, me)]
                to_partner(block, block, sems, seqs + q, other).wait()
        inner(s, p)
        if p is other:
            outer(s, p, give.at[pl.ds(seqs, seqs)])
            to_partner(give.at[seqs + s], got.at[1, s], sems, 2 * seqs + s, other).start()
        else:
            outer(s, p, own)

    for s in range(seqs):
        to_partner(give.at[seqs + s], got.at[1, s], sems, 2 * seqs + s, other).wait()

        def second_norm(i, _):
            rows = at(i * sub, sub)
            h = unit1[s, rows, :] * gain1 + shift1
            z = (own[s, rows, :].astype(F32) + got[1, s, rows, :].astype(F32)) + b_outer + h
            unit, r = norm_stats(z)
            out[s, rows, :] = (unit * gain2 + shift2).astype(BF16)
            g = gout[s, rows, :].astype(F32)
            d = norm_back(g, gain2, unit, r)
            dz2[s, rows, :] = d
            df[at((2 * s + me) * part + i * sub, sub), :] = d.astype(BF16)
            sums[3] += fold(d)
            sums[4] += fold(g * unit)
            sums[5] += fold(g)
            return 0
        lax.fori_loop(0, part // sub, second_norm, 0)
        block = df.at[rows_of(s, me)]
        to_partner(block, block, sems, 3 * seqs + s, other).start()

    def inner_back(s, p):
        rows = rows_of(s, p)

        def columns(j, _):
            cols = at(j * tile, tile)
            dg = dot_t(df[rows, :], wf[cols, :]).astype(BF16).astype(F32)
            low = (dg * slope[rows, cols]).astype(BF16)
            du[rows, cols] = low
            bsum[:, cols] += fold(low.astype(F32))
            return 0
        lax.fori_loop(0, hidden // tile, columns, 0)

    def outer_back(s, p, place):
        rows = rows_of(s, p)

        def columns(j, _):
            cols = at(j * tile, tile)
            place[s, :, cols] = dot_t(du[rows, :], wi[cols, :]).astype(BF16)
            return 0
        lax.fori_loop(0, width // tile, columns, 0)

    for n, (s, p) in enumerate(order):
        if n == 1:
            for q in range(seqs):
                block = df.at[rows_of(q, me)]
                to_partner(block, block, sems, 3 * seqs + q, other).wait()
        inner_back(s, p)
        if p is other:
            outer_back(s, p, give.at[pl.ds(2 * seqs, seqs)])
            to_partner(give.at[2 * seqs + s], got.at[2, s], sems, 4 * seqs + s, other).start()
        else:
            outer_back(s, p, own)

    for s in range(seqs):
        to_partner(give.at[2 * seqs + s], got.at[2, s], sems, 4 * seqs + s, other).wait()

        def first_back(i, _):
            rows = at(i * sub, sub)
            cot = dz2[s, rows, :] + (own[s, rows, :].astype(F32) + got[2, s, rows, :].astype(F32))
            unit = unit1[s, rows, :]
            d = norm_back(cot, gain1, unit, r1[s, rows, 0:1])
            dz1[s, rows, :] = d
            da[at((2 * s + me) * part + i * sub, sub), :] = d.astype(BF16)
            sums[0] += fold(d)
            sums[1] += fold(cot * unit)
            sums[2] += fold(cot)
            return 0
        lax.fori_loop(0, part // sub, first_back, 0)
        block = da.at[rows_of(s, me)]
        to_partner(block, block, sems, 5 * seqs + s, other).start()

    mine = lax.axis_index("batch")
    gives = (give_x, give_y)
    half = keep.shape[1]
    per = hidden // width

    def put(value, kept, axis, given):
        bit = (mine // (1 << firsts[axis])) % 2

        @pl.when(bit == 0)
        def _():
            keep[kept] = value[:half].astype(BF16)
            gives[axis][given] = value[half:].astype(BF16)

        @pl.when(bit == 1)
        def _():
            keep[kept] = value[half:].astype(BF16)
            gives[axis][given] = value[:half].astype(BF16)

    def grads_of(axis, start, count):
        def grad_outer(i, _):
            at_act = at((start + i) * 2 * half, 2 * half)
            put(t_dot(act[:, at_act], df[...]), early + start + i, axis, count + i)
            return 0

        def grad_inner(i, _):
            at_hn, at_du = at((start + i) // per * 2 * half, 2 * half), at((start + i) % per * width, width)
            put(t_dot(hn[:, at_hn], du[:, at_du]), start + i, axis, i)
            return 0

        lax.fori_loop(0, count, grad_inner, 0)
        lax.fori_loop(0, count, grad_outer, 0)

    early = keep.shape[0] // 2
    begin = 0
    for axis in range(2):
        grads_of(axis, begin, gives[axis].shape[0] // 2)
        begin += gives[axis].shape[0] // 2

    for s in range(seqs):
        block = da.at[rows_of(s, me)]
        to_partner(block, block, sems, 5 * seqs + s, other).wait()
    dc[...] = dot_t(da[...], wo[...]).astype(BF16)
    g_wo[...] = t_dot(c[...], da[...]).astype(BF16)
    small[...] = jnp.sum(sums[...], axis=1)
    g_bi[...] = jnp.sum(bsum[...], axis=0, keepdims=True)


def middle(c, x, wo, wi, wf, vectors, gout, firsts, counts, rows):
    seqs, part, width = x.shape
    total, cols = c.shape
    hidden = wi.shape[1]
    sds = jax.ShapeDtypeStruct
    halves = [sds((2 * count, rows // 2, width), BF16) for count in (sum(counts), *counts)]
    return pl.pallas_call(
        functools.partial(middle_kernel, seqs, part, firsts),
        out_shape=(sds(x.shape, BF16), sds(x.shape, F32), sds(c.shape, BF16), sds(wo.shape, BF16),
                   *halves, sds((6, width), F32), sds((1, hidden), F32)),
        in_specs=vmem(6 + len(vectors)), out_specs=tuple(vmem(9)),
        scratch_shapes=[
            pltpu.VMEM(x.shape, F32), pltpu.VMEM((seqs, part, 128), F32), pltpu.VMEM(x.shape, F32),
            pltpu.VMEM((total, width), BF16), pltpu.VMEM((total, hidden), BF16), pltpu.VMEM((total, hidden), F32),
            pltpu.VMEM((total, width), BF16), pltpu.VMEM((total, hidden), BF16), pltpu.VMEM((total, width), BF16),
            pltpu.VMEM((3 * seqs, part, width), BF16), pltpu.VMEM((3, seqs, part, width), BF16),
            pltpu.VMEM(x.shape, BF16), pltpu.VMEM((6, 8, width), F32), pltpu.VMEM((8, hidden), F32),
            pltpu.VMEM((1, hidden), F32),
            pltpu.SemaphoreType.DMA((2, 6 * seqs)),
        ],
        compiler_params=pltpu.CompilerParams(collective_id=2, has_side_effects=True, vmem_limit_bytes=LIMIT),
        cost_estimate=pl.CostEstimate(flops=14 * total * width * hidden, transcendentals=total * hidden,
                                      bytes_accessed=30 << 20),
        name="middle",
    )(c, x, wo, wi, wf, *vectors, gout)


def project_back_kernel(seqs, part, rows, dq, dk, dv, wq, wk, wv, dz1,
                        gin, g_q, g_k, g_v, g_b, give, got, sems):
    me = lax.axis_index("head")
    other = 1 - me
    meet(other)

    def total_of(s, p):
        at = pl.ds(pl.multiple_of((2 * s + p) * part, part), part)
        return dot_t(dq[at, :], wq[...]) + dot_t(dk[at, :], wk[...]) + dot_t(dv[at, :], wv[...])

    for s in range(seqs):
        give[s] = total_of(s, other).astype(BF16)
        to_partner(give.at[s], got.at[s], sems, s, other).start()
    g_q[...] = t_dot(rows[...], dq[...]).astype(BF16)
    g_k[...] = t_dot(rows[...], dk[...]).astype(BF16)
    g_v[...] = t_dot(rows[...], dv[...]).astype(BF16)
    g_b[0:1, :] = jnp.sum(fold(dq[...].astype(F32)), axis=0, keepdims=True)
    g_b[1:2, :] = jnp.sum(fold(dv[...].astype(F32)), axis=0, keepdims=True)
    for s in range(seqs):
        own = total_of(s, me).astype(BF16)
        to_partner(give.at[s], got.at[s], sems, s, other).wait()
        gin[s] = (dz1[s] + (own.astype(F32) + got[s].astype(F32))).astype(BF16)


def project_back(rows, dq, dk, dv, wq, wk, wv, dz1):
    seqs, part, width = dz1.shape
    sds = jax.ShapeDtypeStruct
    grad = sds(wq.shape, BF16)
    return pl.pallas_call(
        functools.partial(project_back_kernel, seqs, part),
        out_shape=(sds(dz1.shape, BF16), grad, grad, grad, sds((2, wq.shape[1]), F32)),
        in_specs=vmem(8), out_specs=tuple(vmem(5)),
        scratch_shapes=[pltpu.VMEM(dz1.shape, BF16), pltpu.VMEM(dz1.shape, BF16), pltpu.SemaphoreType.DMA((2, seqs))],
        compiler_params=pltpu.CompilerParams(collective_id=3, has_side_effects=True, vmem_limit_bytes=LIMIT),
        cost_estimate=pl.CostEstimate(flops=12 * rows.size * wq.shape[1], transcendentals=0, bytes_accessed=16 << 20),
        name="project_back",
    )(rows, dq, dk, dv, wq, wk, wv, dz1)
LINE = 16
ROWS = 256
LATE_COLORS = (0, 1, 2, 3, 0, 1, 2, 3)
PRECEDENCE = (29, 13, 18, 0, 6, 13, 11, 17, 6, 9, 1, 15, 15, 6, 22, 21, 13, 2, 9, 12, 8, 7, 35, 19)
LANDS = ("gather", "out", "back_in", "back_mid", "back_out")


def grid_bits(n):
    bits = n.bit_length() - 1
    side = bits // 3
    return (0, side, 2 * side), bits


def chunk_plan(n, color, rows):
    (bx, by, bz), bits = grid_bits(n)
    order = (by, bx) if color % 2 else (bx, by)
    line = n == LINE
    plan, length = [], rows
    if line and color >= 2:
        plan = [("far_in", bz, 3 * rows // 4), ("far_mid", bz, rows // 2), ("far_out", bz, rows // 4)]
        length = rows // 4
    if not line:
        order = (*order, bz)
    for b in order:
        length //= 2
        plan.append(("scatter", b, length))
    if line and color < 2:
        plan += [(kind, bz, length) for kind in ("in", "mid", "out")]
    plan += [("double", b, length) for b in range(bits) if not line and b not in order]
    for b in reversed(order):
        plan.append(("gather", b, length))
        length *= 2
    if line and color >= 2:
        plan += [("back_in", bz, rows // 4), ("back_mid", bz, rows // 2), ("back_out", bz, 3 * rows // 4)]
    return plan


def event_order(n, plans, rows):
    first, _ = grid_bits(n)
    lag = 0.16

    def path(kind, b):
        place = kind.split("_")[-1]
        if place in ("in", "mid", "out"):
            return ("in", "mid", "out").index(place) + 2
        return (b >= first[1]) + (b >= first[2])

    work = [[(path(kind, b), size / rows) for kind, b, size in plan] for plan in plans]
    free, ready, step, events = [0.0] * 5, [0.0] * len(plans), [0] * len(plans), []
    for _ in range(sum(map(len, work))):
        start, _, c = min((max(ready[c], free[row[step[c]][0]]), -PRECEDENCE[c % len(PRECEDENCE)], c)
                          for c, row in enumerate(work) if step[c] < len(row))
        link, span = work[c][step[c]]
        free[link] = start + span
        ready[c] = free[link] + lag
        events.append((start, c, step[c]))
        step[c] += 1
    events += [(r, c, len(work[c])) for c, r in enumerate(ready)]
    return [(c, s) for _, c, s in sorted(events)]


def flip(index, bit):
    return index + (1 - 2 * ((index // (1 << bit)) % 2)) * (1 << bit)


def chunk_pieces(shapes, rows, width):
    chunks = []
    for i, (height, cols) in enumerate(shapes):
        per = max(1, width // cols)
        for r in range(0, height, rows * per):
            for col in range(0, cols, width):
                span = min(cols, width)
                chunks.append([(i, r + j * rows, col, span, j * span) for j in range(per)])
    return chunks


def only(cond, body):
    if cond is None:
        body()
    else:
        pl.when(cond)(body)


def reduce_kernel(n, plans, rows, loads, saves, count, results, *refs):
    grads, (small, g_bi, g_b) = refs[:count], refs[count:count + 3]
    refs = refs[count + 3:]
    sums, tiny_out = refs[:results], refs[results]
    work, got, full, hold, tiny_got, load_sem, save_sem, send_sem, recv_sem, tiny_sem = refs[results + 1:]
    nc = len(plans)
    me, head = lax.axis_index("batch"), lax.axis_index("head")
    first, bits = grid_bits(n)
    bit_of = [(me // (1 << b)) % 2 for b in range(bits)]
    z = me // (1 << first[2])
    side = z // 2
    end = z % 3 == 0
    middle = z % 3 != 0
    mirror = me + (3 - 2 * z) * (1 << first[2])

    spans = []
    for plan in plans:
        off, length, at, row = 0, rows, 0, []
        quarter = rows // 4
        for kind, b, size in plan:
            where = None if kind in LANDS else at
            at += 0 if kind in LANDS else size
            if kind == "scatter":
                row.append((off + bit_of[b] * size, off + (1 - bit_of[b]) * size, size, where))
                off = row[-1][0]
            elif kind == "gather":
                row.append((off, off, size, where))
                off = off - bit_of[b] * size
            elif kind in ("far_in", "back_out"):
                row.append(((1 - side) * quarter, (1 - side) * quarter, size, where))
            elif kind == "far_mid":
                row.append((side * 2 * quarter, (1 - side) * 2 * quarter, size, where))
            elif kind == "back_mid":
                row.append((side * 2 * quarter, side * 2 * quarter, size, where))
            elif kind in ("far_out", "back_in"):
                row.append((side * 3 * quarter, side * 3 * quarter, size, where))
                off = z * quarter
            else:
                row.append((off, off, size, where))
        spans.append(row)

    def roles(kind):
        place = kind.split("_")[-1]
        return {"in": (end, middle), "mid": (middle, middle), "out": (middle, end)}.get(place, (None, None))

    def moves(c, out):
        if out:
            for k, (i, r, col, span, at) in enumerate(saves[c]):
                outside = sums[i].at[pl.ds(r, rows), pl.ds(col, span)]
                yield pltpu.make_async_copy(full.at[c, :, pl.ds(at, span)], outside, save_sem.at[c, k])
        elif loads[c] is None:
            for k, (i, r, col, span, at) in enumerate(saves[c]):
                outside = grads[i + count - results].at[pl.ds(r, rows), pl.ds(col, span)]
                yield pltpu.make_async_copy(outside, work.at[c, :, pl.ds(at, span)], load_sem.at[c, k])
        else:
            kept, kept_at, given, given_at = loads[c]
            keep, _, length, at = spans[c][0]
            inside = work.at[c, pl.ds(pl.multiple_of(keep, 16), length)]
            yield pltpu.make_async_copy(grads[kept].at[kept_at], inside, load_sem.at[c, 0])
            yield pltpu.make_async_copy(grads[given].at[given_at], got.at[c, pl.ds(at, length)], load_sem.at[c, 1])

    for c in range(nc):
        for move in moves(c, False):
            move.start()
    hold[...] = jnp.zeros_like(hold)
    hold[0:6, :] = small[...]
    width, row = hold.shape[1], 8
    for j in range(g_bi.shape[1] // width):
        hold[row:row + 1, :] = g_bi[:, j * width:(j + 1) * width]
        row += 1
    cols = g_b.shape[1]
    for j in range(2):
        hold[row + j * cols // width:row + j * cols // width + 1, pl.ds(j * cols % width, cols)] = g_b[j:j + 1, :]
    barrier = pltpu.get_barrier_semaphore()
    friends = [flip(me, b) for b in range(bits)] + ([mirror] if n == LINE else [])
    for friend in friends:
        pl.semaphore_signal(barrier, inc=1, device_id={"batch": friend}, device_id_type=MESH)
    pl.semaphore_signal(barrier, inc=1, device_id={"head": 1 - head}, device_id_type=MESH)
    pl.semaphore_wait(barrier, len(friends) + 1)

    def copy_of(c, s):
        kind, b, _ = plans[c][s]
        _, start, length, at = spans[c][s]
        place = (c, pl.ds(pl.multiple_of(start, 16), length))
        src = full.at[place] if kind in LANDS else work.at[place]
        dst = full.at[place] if kind in LANDS else got.at[c, pl.ds(at, length)]
        return pltpu.make_async_remote_copy(
            src_ref=src, dst_ref=dst, send_sem=send_sem.at[c, s], recv_sem=recv_sem.at[c, s],
            device_id={"batch": mirror if kind.endswith("mid") else flip(me, b)}, device_id_type=MESH)

    def finish(c, s):
        kind = plans[c][s][0]
        keep, _, length, at = spans[c][s]
        sender, receiver = roles(kind)
        if s == 0 and loads[c] is not None:
            for move in moves(c, False):
                move.wait()
        else:
            only(sender, lambda: copy_of(c, s).wait_send())

        def take():
            if s > 0 or loads[c] is None:
                copy_of(c, s).wait_recv()
            if kind in LANDS:
                return
            target = full if plans[c][s + 1][0] in LANDS else work

            def add(i, _):
                here = pl.ds(pl.multiple_of(keep + i * 16, 16), 16)
                there = pl.ds(pl.multiple_of(at + i * 16, 16), 16)
                target[c, here, :] = (work[c, here, :].astype(F32) + got[c, there, :].astype(F32)).astype(BF16)
                return 0
            lax.fori_loop(0, length // 16, add, 0)
        only(receiver, take)

    def tiny_copy(k):
        rest = hold.at[pl.ds(0, 8)] if k == 0 else hold
        there = tiny_got.at[k, pl.ds(0, 8)] if k == 0 else tiny_got.at[k]
        target = {"head": 1 - head} if k == 0 else {"batch": flip(me, k - 1)}
        return pltpu.make_async_remote_copy(
            src_ref=rest, dst_ref=there, send_sem=tiny_sem.at[0, k], recv_sem=tiny_sem.at[1, k],
            device_id=target, device_id_type=MESH)

    def tiny_finish(k):
        tiny_copy(k).wait()
        if k == 0:
            hold[0:8, :] += tiny_got[0, 0:8, :]
        else:
            hold[...] += tiny_got[k]

    done = [load is not None for load in loads]
    events = [(c, s + done[c]) for c, s in event_order(n, [p[d:] for p, d in zip(plans, done)], rows)]
    gap = len(events) // (bits + 2)
    for e, (c, s) in enumerate(events):
        if s == 0:
            for move in moves(c, False):
                move.wait()
        else:
            finish(c, s - 1)
        if s == len(plans[c]):
            for move in moves(c, True):
                move.start()
        else:
            only(roles(plans[c][s][0])[0], lambda: copy_of(c, s).start())
        if e % gap == 0 and e // gap <= bits:
            k = e // gap
            if k > 0:
                tiny_finish(k - 1)
            tiny_copy(k).start()
    tiny_finish(bits)
    tiny_out[...] = hold[...]
    for c in range(nc):
        for move in moves(c, True):
            move.wait()


def reduce_gradients(early, late, shapes, tiny, n):
    width = tiny[0].shape[1]
    tiny_shape = (16, width)
    saves = chunk_pieces(shapes, ROWS, width)
    count = early[0].shape[0] // 2
    slots, plans, loads = [0, 0], [], []
    for which in range(2):
        for c in range(count):
            color = c * 2 // count
            loads.append((0, which * count + c, 1 + color, slots[color]))
            slots[color] += 1
            plans.append(chunk_plan(n, color, ROWS))
    for c in range(len(saves) - 2 * count):
        plans.append(chunk_plan(n, LATE_COLORS[c % len(LATE_COLORS)], ROWS))
        loads.append(None)
    nc = len(saves)
    stages = max(len(plan) for plan in plans)
    _, bits = grid_bits(n)
    got_rows = max(sum(size for kind, _, size in plan if kind not in LANDS) for plan in plans)
    grads = (*early, *late)
    hbm = lambda k: [pl.BlockSpec(memory_space=pl.ANY)] * k
    done = pl.pallas_call(
        functools.partial(reduce_kernel, n, plans, ROWS, loads, saves, len(grads), len(shapes)),
        out_shape=(*(jax.ShapeDtypeStruct(shape, BF16) for shape in shapes), jax.ShapeDtypeStruct(tiny_shape, F32)),
        in_specs=hbm(len(grads)) + vmem(3), out_specs=tuple(hbm(len(shapes)) + vmem(1)),
        scratch_shapes=[
            pltpu.VMEM((nc, ROWS, width), BF16), pltpu.VMEM((nc, got_rows, width), BF16),
            pltpu.VMEM((nc, ROWS, width), BF16), pltpu.VMEM(tiny_shape, F32),
            pltpu.VMEM((bits + 1,) + tiny_shape, F32),
            pltpu.SemaphoreType.DMA((nc, 2)), pltpu.SemaphoreType.DMA((nc, 2)),
            pltpu.SemaphoreType.DMA((nc, stages)), pltpu.SemaphoreType.DMA((nc, stages)),
            pltpu.SemaphoreType.DMA((2, bits + 1)),
        ],
        compiler_params=pltpu.CompilerParams(collective_id=0, has_side_effects=True, vmem_limit_bytes=LIMIT),
        name="reduce_gradients",
    )(*grads, *tiny)
    return done[:-1], done[-1]


def results_kernel(count, plain, *refs):
    ins, tiny, outs = refs[:count + plain], refs[count + plain], refs[count + plain + 1:]
    for src, dst in zip(ins, outs):
        dst[...] = src[...].astype(dst.dtype)

    @pl.when(pl.program_id(0) == 0)
    def _():
        row = 0
        for place, dst in zip((0, 1, 2, 3, 4, 5, 8), outs[count + plain:]):
            width = tiny.shape[1]
            for j in range(dst.shape[0] // width):
                dst[pl.ds(j * width, width)] = tiny[place + j, :]
                row = place + j + 1
        for j, dst in enumerate(outs[count + plain + 7:]):
            at = j * dst.shape[0]
            dst[...] = tiny[row + at // tiny.shape[1], pl.ds(at % tiny.shape[1], dst.shape[0])]


def results(grads, rows, tiny, hidden, cols, steps=8):
    flat = [r.reshape(-1, r.shape[-1]) for r in rows]
    blocks = [pl.BlockSpec((a.shape[0] // steps, a.shape[1]), lambda i: (i, 0)) for a in (*grads, *flat)]
    vectors = [tiny.shape[1]] * 6 + [hidden, cols, cols]
    done = pl.pallas_call(
        functools.partial(results_kernel, len(grads), len(flat)),
        grid=(steps,),
        in_specs=blocks + [pl.BlockSpec(tiny.shape, lambda i: (0, 0))],
        out_specs=tuple(blocks + [pl.BlockSpec((v,), lambda i: (0,)) for v in vectors]),
        out_shape=tuple([jax.ShapeDtypeStruct(g.shape, F32) for g in grads]
                        + [jax.ShapeDtypeStruct(f.shape, f.dtype) for f in flat]
                        + [jax.ShapeDtypeStruct((v,), F32) for v in vectors]),
        compiler_params=pltpu.CompilerParams(vmem_limit_bytes=LIMIT),
        name="results",
    )(*grads, *flat, tiny)
    grads, flat, vectors = done[:len(grads)], done[len(grads):-len(vectors)], done[-len(vectors):]
    return grads, [f.reshape(r.shape) for f, r in zip(flat, rows)], vectors


def on_device(n_batch, inputs, prior_scores, lengths, w_query, w_key, w_value, b_query, b_value, w_output, b_output,
              gain_attn, shift_attn, w_inner, b_inner, w_outer, b_outer, gain_ffn, shift_ffn, grad_out, grad_scores):
    width = inputs.shape[2]
    vectors = (b_output, gain_attn, shift_attn, b_outer, gain_ffn, shift_ffn, b_inner)
    rows, q, k, v = project_rows(inputs, w_query, w_key, w_value, b_query, b_value)
    new_scores, context, norm = attend(lengths, q, k, v, prior_scores)
    firsts = grid_bits(n_batch)[0][:2]
    chunks = w_inner.size // (ROWS * width)
    counts = [chunks // 2] * 2
    outputs, dz1, dc, g_wo, keep, *gives, small, g_bi = middle(
        context, inputs, w_output, w_inner, w_outer, vectors, grad_out, firsts, counts, ROWS)
    taken = [lax.ppermute(give, "batch", [(i, flip(i, first)) for i in range(n_batch)])
             for give, first in zip(gives, firsts)]
    grad_prior, dq, dk, dv = attend_back(lengths, q, k, v, dc, prior_scores, norm, grad_scores)
    grad_inputs, g_wq, g_wk, g_wv, g_b = project_back(rows, dq, dk, dv, w_query, w_key, w_value, dz1)
    late = (g_wo, g_wq, g_wk, g_wv)
    shapes = [w_inner.shape, w_outer.shape] + [g.shape for g in late]
    grads, tiny = reduce_gradients((keep, *taken), late, shapes, (small, g_bi, g_b), n_batch)
    hidden, cols = g_bi.shape[1], g_b.shape[1]
    grads, (outputs, grad_inputs), vectors = results(grads, (outputs, grad_inputs), tiny, hidden, cols)
    g_wi, g_wf, g_wo, g_wq, g_wk, g_wv = grads
    g_bo, g_g1, g_s1, g_bf, g_g2, g_s2, g_bi, g_bq, g_bv = vectors
    return (outputs, new_scores, grad_inputs, grad_prior, g_wq, g_wk, g_wv, g_bq, g_bv, g_wo,
            g_bo, g_g1, g_s1, g_wi, g_bi, g_wf, g_bf, g_g2, g_s2)


def solution(mesh):
    seq, scores, whole = P("batch", "head", None), P("batch", "head", None, None), P()
    down, across, vector = P("head", None), P(None, "head"), P("head")
    in_specs = (seq, scores, P("batch"), across, across, across, vector, vector, down, whole, whole, whole,
                across, vector, down, whole, whole, whole, seq, scores)
    out_specs = (seq, scores, seq, scores, across, across, across, vector, vector, down, whole, whole, whole,
                 across, vector, down, whole, whole, whole)
    layer = functools.partial(on_device, mesh.shape["batch"])
    return jax.shard_map(layer, mesh=mesh, in_specs=in_specs, out_specs=out_specs, check_vma=False)
```

```python
import functools
import jax, jax.numpy as jnp
from jax import lax
from jax.experimental import pallas as pl
from jax.experimental.pallas import tpu as pltpu
from jax.sharding import PartitionSpec as P

MESH = pl.DeviceIdType.MESH
F32, BF16 = jnp.float32, jnp.bfloat16
EPS = 1e-12
NEG = -1e30
LIMIT = 64 * 1000 * 1000


def dot(a, b):
    return jnp.dot(a, b, preferred_element_type=F32)


def dot_t(a, b):
    return lax.dot_general(a, b, (((1,), (1,)), ((), ())), preferred_element_type=F32)


def t_dot(a, b):
    return lax.dot_general(a, b, (((0,), (0,)), ((), ())), preferred_element_type=F32)


def meet(partner):
    barrier = pltpu.get_barrier_semaphore()
    pl.semaphore_signal(barrier, inc=1, device_id={"head": partner}, device_id_type=MESH)
    pl.semaphore_wait(barrier, 1)


def to_partner(src, dst, sems, i, partner):
    return pltpu.make_async_remote_copy(
        src_ref=src, dst_ref=dst, send_sem=sems.at[0, i], recv_sem=sems.at[1, i],
        device_id={"head": partner}, device_id_type=MESH)


def vmem(count):
    return [pl.BlockSpec(memory_space=pltpu.VMEM)] * count


def as_row(vector):
    return vector[...].astype(F32).reshape(1, vector.shape[0])


def project_kernel(seqs, part, x, wq, wk, wv, b_query, b_value, rows, q, k, v, got, sems):
    me = lax.axis_index("head")
    other = 1 - me
    meet(other)
    for s in range(seqs):
        to_partner(x.at[s], got.at[s], sems, s, other).start()

    bias_q, bias_v = as_row(b_query), as_row(b_value)

    def emit(block, s, p):
        at = pl.ds(pl.multiple_of((2 * s + p) * part, part), part)
        rows[at, :] = block
        q[at, :] = (dot(block, wq[...]) + bias_q).astype(BF16)
        k[at, :] = dot(block, wk[...]).astype(BF16)
        v[at, :] = (dot(block, wv[...]) + bias_v).astype(BF16)

    def own(s, _):
        emit(x[s], s, me)
        return 0

    lax.fori_loop(0, seqs, own, 0)
    for s in range(seqs):
        to_partner(x.at[s], got.at[s], sems, s, other).wait()

    def theirs(s, _):
        emit(got[s], s, other)
        return 0

    lax.fori_loop(0, seqs, theirs, 0)


def project_rows(x, wq, wk, wv, b_query, b_value):
    seqs, part, width = x.shape
    total, cols = 2 * seqs * part, wq.shape[1]
    out = jax.ShapeDtypeStruct((total, cols), BF16)
    return pl.pallas_call(
        functools.partial(project_kernel, seqs, part),
        out_shape=(jax.ShapeDtypeStruct((total, width), BF16), out, out, out),
        in_specs=vmem(6), out_specs=tuple(vmem(4)),
        scratch_shapes=[pltpu.VMEM(x.shape, BF16), pltpu.SemaphoreType.DMA((2, seqs))],
        compiler_params=pltpu.CompilerParams(collective_id=1, has_side_effects=True, vmem_limit_bytes=LIMIT),
        name="project_rows",
    )(x, wq, wk, wv, b_query, b_value)


def attend_kernel(block, head, lengths, q, k, v, prior, score, c, norm):
    full = k.shape[0]
    live = lax.broadcasted_iota(jnp.int32, (1, full), 1) < lengths[pl.program_id(0)]
    first = lax.broadcasted_iota(jnp.int32, (1, 2 * head), 1) < head
    scale = head ** -0.5
    for r in range(0, full, block):
        rows = pl.ds(r, block)
        queries = q[rows, :] * jnp.asarray(scale, BF16)
        parts, norms = [], []
        for h in range(2):
            mine = jnp.where(first == (h == 0), queries, jnp.zeros_like(queries))
            scores = dot_t(mine, k[...]) + prior[0, h, rows, :].astype(F32)
            score[0, h, rows, :] = scores.astype(BF16)
            masked = jnp.where(live, scores, NEG)
            top = jnp.max(masked, axis=-1, keepdims=True)
            terms = jnp.exp(masked - top)
            total = jnp.sum(terms, axis=-1, keepdims=True)
            probs = (terms * (1.0 / total)).astype(BF16)
            parts.append(dot(probs, v[...]))
            norms.append(top + jnp.log(total))
        c[rows, :] = jnp.where(first, parts[0], parts[1]).astype(BF16)
        norm[0, 0, rows, :] = jnp.where(first, norms[0], norms[1])


def attend(lengths, q, k, v, prior):
    seqs, heads, full, _ = prior.shape
    pair = q.shape[1] // heads * 2
    rows = pl.BlockSpec((full, pair), lambda s, h, n: (s, h))
    big = pl.BlockSpec((1, 2, full, full), lambda s, h, n: (s, h, 0, 0))
    norm = pl.BlockSpec((1, 1, full, pair), lambda s, h, n: (s, h, 0, 0))
    return pl.pallas_call(
        functools.partial(attend_kernel, 256, pair // 2),
        grid_spec=pltpu.PrefetchScalarGridSpec(
            num_scalar_prefetch=1, grid=(seqs, heads // 2),
            in_specs=[rows, rows, rows, big], out_specs=(big, rows, norm)),
        out_shape=(jax.ShapeDtypeStruct(prior.shape, BF16), jax.ShapeDtypeStruct(q.shape, BF16),
                   jax.ShapeDtypeStruct((seqs, heads // 2, full, pair), F32)),
        compiler_params=pltpu.CompilerParams(vmem_limit_bytes=LIMIT),
        name="attend",
    )(lengths, q, k, v, prior)


def attend_back_kernel(block, head, lengths, q, k, v, dc, prior, norm, given, grad, dq, dk, dv):
    full = k.shape[0]
    live = lax.broadcasted_iota(jnp.int32, (1, full), 1) < lengths[pl.program_id(0)]
    first = lax.broadcasted_iota(jnp.int32, (1, 2 * head), 1) < head
    scale = head ** -0.5
    q_t, dc_t = q[...].T, dc[...].T
    dk_t, dv_t = [0.0, 0.0], [0.0, 0.0]
    for r in range(0, full, block):
        rows = pl.ds(r, block)
        queries, cots = q[rows, :] * jnp.asarray(scale, BF16), dc[rows, :]
        parts = []
        for h in range(2):
            mine = first == (h == 0)
            scores = dot_t(jnp.where(mine, queries, jnp.zeros_like(queries)), k[...])
            scores = scores + prior[0, h, rows, :].astype(F32)
            probs = jnp.exp(jnp.where(live, scores, NEG) - norm[0, 0, rows, h * head:h * head + 1])
            dp = dot_t(jnp.where(mine, cots, jnp.zeros_like(cots)), v[...])
            delta = jnp.sum(probs * dp, axis=-1, keepdims=True)
            ds = (probs * (dp - delta) + given[0, h, rows, :].astype(F32)).astype(BF16)
            grad[0, h, rows, :] = ds
            parts.append(dot(ds, k[...]))
            lanes = slice(h * head, (h + 1) * head)
            dk_t[h] = dk_t[h] + dot(q_t[lanes, r:r + block], ds)
            dv_t[h] = dv_t[h] + dot(dc_t[lanes, r:r + block], probs.astype(BF16))
        dq[rows, :] = (jnp.where(first, parts[0], parts[1]) * scale).astype(BF16)
    dk[...] = (jnp.concatenate(dk_t, axis=0) * scale).T.astype(BF16)
    dv[...] = jnp.concatenate(dv_t, axis=0).T.astype(BF16)


def attend_back(lengths, q, k, v, dc, prior, norm, given):
    seqs, heads, full, _ = prior.shape
    pair = q.shape[1] // heads * 2
    rows = pl.BlockSpec((full, pair), lambda s, h, n: (s, h))
    big = pl.BlockSpec((1, 2, full, full), lambda s, h, n: (s, h, 0, 0))
    norms = pl.BlockSpec((1, 1, full, pair), lambda s, h, n: (s, h, 0, 0))
    flat = jax.ShapeDtypeStruct(q.shape, BF16)
    return pl.pallas_call(
        functools.partial(attend_back_kernel, 256, pair // 2),
        grid_spec=pltpu.PrefetchScalarGridSpec(
            num_scalar_prefetch=1, grid=(seqs, heads // 2),
            in_specs=[rows, rows, rows, rows, big, norms, big], out_specs=(big, rows, rows, rows)),
        out_shape=(jax.ShapeDtypeStruct(prior.shape, BF16), flat, flat, flat),
        compiler_params=pltpu.CompilerParams(vmem_limit_bytes=LIMIT),
        cost_estimate=pl.CostEstimate(flops=40 * full * full * seqs * heads * pair // 2, transcendentals=prior.size,
                                      bytes_accessed=6 * prior.size),
        name="attend_back",
    )(lengths, q, k, v, dc, prior, norm, given)


def fold(value):
    return jnp.sum(value.reshape(value.shape[0] // 8, 8, value.shape[1]), axis=0)


def norm_stats(z):
    mean = jnp.mean(z, axis=-1, keepdims=True)
    centred = z - mean
    r = lax.rsqrt(jnp.mean(centred * centred, axis=-1, keepdims=True) + EPS)
    return centred * r, r


def norm_back(cot, gain, unit, r):
    e = cot * gain
    return r * (e - jnp.mean(e, axis=-1, keepdims=True) - unit * jnp.mean(e * unit, axis=-1, keepdims=True))


def middle_kernel(seqs, part, firsts, c, x, wo, wi, wf, b_output, gain1, shift1, b_outer, gain2, shift2, b_inner, gout,
                  out, dz1, dc, keep, give_x, give_y, taken, small, g_bi,
                  unit1, r1, dz2, hn, act, slope, df, du, da, give, got, own, sums, bsum, bi, give_f, sems, far_sems):
    me = lax.axis_index("head")
    other = 1 - me
    width = x.shape[2]
    hidden = wi.shape[1]
    tile = 512
    sub = 64
    barrier = pltpu.get_barrier_semaphore()
    pl.semaphore_signal(barrier, inc=1, device_id={"head": other}, device_id_type=MESH)
    for first in firsts:
        pl.semaphore_signal(barrier, inc=1, device_id={"batch": flip(lax.axis_index("batch"), first)},
                            device_id_type=MESH)
    pl.semaphore_wait(barrier, 3)
    b_output, gain1, shift1, b_outer, gain2, shift2 = map(as_row, (b_output, gain1, shift1, b_outer, gain2, shift2))
    sums[...] = jnp.zeros_like(sums)
    bsum[...] = jnp.zeros_like(bsum)
    bi[...] = as_row(b_inner)

    def rows_of(s, p):
        return pl.ds(pl.multiple_of((2 * s + p) * part, part), part)

    def at(start, size):
        return pl.ds(pl.multiple_of(start, size), size)

    def attn_part(s, _):
        give[s] = dot(c[rows_of(s, other), :], wo[...]).astype(BF16)
        return 0
    for s in range(seqs):
        attn_part(s, 0)
        to_partner(give.at[s], got.at[0, s], sems, s, other).start()

    def attn_own(s, _):
        own[s] = dot(c[rows_of(s, me), :], wo[...]).astype(BF16)
        return 0
    lax.fori_loop(0, seqs, attn_own, 0)
    for s in range(seqs):
        to_partner(give.at[s], got.at[0, s], sems, s, other).wait()

        def first_norm(i, _):
            rows = at(i * sub, sub)
            z = x[s, rows, :].astype(F32) + (own[s, rows, :].astype(F32) + got[0, s, rows, :].astype(F32)) + b_output
            unit, r = norm_stats(z)
            unit1[s, rows, :] = unit
            r1[s, rows, :] = jnp.broadcast_to(r, (sub, 128))
            hn[at((2 * s + me) * part + i * sub, sub), :] = (unit * gain1 + shift1).astype(BF16)
            return 0
        lax.fori_loop(0, part // sub, first_norm, 0)
        block = hn.at[rows_of(s, me)]
        to_partner(block, block, sems, seqs + s, other).start()

    order = [(0, me)] + [(s, other) for s in range(seqs)] + [(s, me) for s in range(1, seqs)]

    def inner(s, p):
        rows = rows_of(s, p)

        def columns(j, _):
            cols = at(j * tile, tile)
            u = dot(hn[rows, :], wi[:, cols]) + bi[:, cols]
            cdf = 0.5 * (1.0 + lax.erf(u * 0.7071067811865476))
            act[rows, cols] = (u * cdf).astype(BF16)
            slope[rows, cols] = cdf + u * (jnp.exp(-0.5 * u * u) * 0.3989422804014327)
            return 0
        lax.fori_loop(0, hidden // tile, columns, 0)

    def outer(s, p, place):
        rows = rows_of(s, p)

        def columns(j, _):
            cols = at(j * tile, tile)
            place[s, :, cols] = dot(act[rows, :], wf[:, cols]).astype(BF16)
            return 0
        lax.fori_loop(0, width // tile, columns, 0)

    for n, (s, p) in enumerate(order):
        if n == 1:
            for q in range(seqs):
                block = hn.at[rows_of(q, me)]
                to_partner(block, block, sems, seqs + q, other).wait()
        inner(s, p)
        if p is other:
            outer(s, p, give.at[pl.ds(seqs, seqs)])
            to_partner(give.at[seqs + s], got.at[1, s], sems, 2 * seqs + s, other).start()
        else:
            outer(s, p, own)

    for s in range(seqs):
        to_partner(give.at[seqs + s], got.at[1, s], sems, 2 * seqs + s, other).wait()

        def second_norm(i, _):
            rows = at(i * sub, sub)
            h = unit1[s, rows, :] * gain1 + shift1
            z = (own[s, rows, :].astype(F32) + got[1, s, rows, :].astype(F32)) + b_outer + h
            unit, r = norm_stats(z)
            out[s, rows, :] = (unit * gain2 + shift2).astype(BF16)
            g = gout[s, rows, :].astype(F32)
            d = norm_back(g, gain2, unit, r)
            dz2[s, rows, :] = d
            df[at((2 * s + me) * part + i * sub, sub), :] = d.astype(BF16)
            sums[3] += fold(d)
            sums[4] += fold(g * unit)
            sums[5] += fold(g)
            return 0
        lax.fori_loop(0, part // sub, second_norm, 0)
        block = df.at[rows_of(s, me)]
        to_partner(block, block, sems, 3 * seqs + s, other).start()

    mine = lax.axis_index("batch")
    gives = (give_x, give_y)
    half = keep.shape[1]
    per = hidden // width
    side = give_f.shape[0] // 2
    edge = give_x.shape[0] - side

    def put(value, kept, axis, given, given_at):
        bit = (mine // (1 << firsts[axis])) % 2

        @pl.when(bit == 0)
        def _():
            keep[kept] = value[:half].astype(BF16)
            given[given_at] = value[half:].astype(BF16)

        @pl.when(bit == 1)
        def _():
            keep[kept] = value[half:].astype(BF16)
            given[given_at] = value[:half].astype(BF16)

    def far_copy(i, axis):
        return pltpu.make_async_remote_copy(
            src_ref=give_f.at[i], dst_ref=taken.at[i], send_sem=far_sems.at[0, i], recv_sem=far_sems.at[1, i],
            device_id={"batch": flip(mine, firsts[axis])}, device_id_type=MESH)

    def grads_outer():
        for axis in range(2):
            def give_outer(i, _, axis=axis):
                chunk = axis * side + i
                put(t_dot(act[:, at(chunk * 2 * half, 2 * half)], df[...]), 2 * side + chunk, axis, give_f, chunk)
                far_copy(chunk, axis).start()
                return 0
            lax.fori_loop(0, side, give_outer, 0)

    def inner_back(s, p):
        rows = rows_of(s, p)

        def columns(j, _):
            cols = at(j * tile, tile)
            dg = dot_t(df[rows, :], wf[cols, :]).astype(BF16).astype(F32)
            low = (dg * slope[rows, cols]).astype(BF16)
            du[rows, cols] = low
            bsum[:, cols] += fold(low.astype(F32))
            return 0
        lax.fori_loop(0, hidden // tile, columns, 0)

    def outer_back(s, p, place):
        rows = rows_of(s, p)

        def columns(j, _):
            cols = at(j * tile, tile)
            place[s, :, cols] = dot_t(du[rows, :], wi[cols, :]).astype(BF16)
            return 0
        lax.fori_loop(0, width // tile, columns, 0)

    for n, (s, p) in enumerate(order):
        if n == 1:
            for q in range(seqs):
                block = df.at[rows_of(q, me)]
                to_partner(block, block, sems, 3 * seqs + q, other).wait()
            grads_outer()
        inner_back(s, p)
        if p is other:
            outer_back(s, p, give.at[pl.ds(2 * seqs, seqs)])
            to_partner(give.at[2 * seqs + s], got.at[2, s], sems, 4 * seqs + s, other).start()
        else:
            outer_back(s, p, own)

    for s in range(seqs):
        to_partner(give.at[2 * seqs + s], got.at[2, s], sems, 4 * seqs + s, other).wait()

        def first_back(i, _):
            rows = at(i * sub, sub)
            cot = dz2[s, rows, :] + (own[s, rows, :].astype(F32) + got[2, s, rows, :].astype(F32))
            unit = unit1[s, rows, :]
            d = norm_back(cot, gain1, unit, r1[s, rows, 0:1])
            dz1[s, rows, :] = d
            da[at((2 * s + me) * part + i * sub, sub), :] = d.astype(BF16)
            sums[0] += fold(d)
            sums[1] += fold(cot * unit)
            sums[2] += fold(cot)
            return 0
        lax.fori_loop(0, part // sub, first_back, 0)
        block = da.at[rows_of(s, me)]
        to_partner(block, block, sems, 5 * seqs + s, other).start()

    for axis in range(2):
        def give_inner(i, _, axis=axis):
            at_hn, at_du = at((axis * side + i) // per * 2 * half, 2 * half), at((axis * side + i) % per * width, width)
            put(t_dot(hn[:, at_hn], du[:, at_du]), axis * side + i, axis, gives[axis], i)
            return 0
        lax.fori_loop(0, side, give_inner, 0)

    for s in range(seqs):
        block = da.at[rows_of(s, me)]
        to_partner(block, block, sems, 5 * seqs + s, other).wait()
    dc[...] = dot_t(da[...], wo[...]).astype(BF16)
    for axis in range(2):
        def give_output(i, _, axis=axis):
            cols = at((axis * edge + i) * 2 * half, 2 * half)
            put(t_dot(c[:, cols], da[...]), 4 * side + axis * edge + i, axis, gives[axis], side + i)
            return 0
        lax.fori_loop(0, edge, give_output, 0)
    small[...] = jnp.sum(sums[...], axis=1)
    g_bi[...] = jnp.sum(bsum[...], axis=0, keepdims=True)
    for axis in range(2):
        def far_done(i, _, axis=axis):
            far_copy(axis * side + i, axis).wait()
            return 0
        lax.fori_loop(0, side, far_done, 0)


def middle(c, x, wo, wi, wf, vectors, gout, firsts, rows):
    seqs, part, width = x.shape
    total, cols = c.shape
    hidden = wi.shape[1]
    sds = jax.ShapeDtypeStruct
    side, edge = hidden // rows // 2, cols // rows // 2
    halves = [sds((count, rows // 2, width), BF16)
              for count in (4 * side + 2 * edge, side + edge, side + edge, 2 * side)]
    return pl.pallas_call(
        functools.partial(middle_kernel, seqs, part, firsts),
        out_shape=(sds(x.shape, BF16), sds(x.shape, F32), sds(c.shape, BF16),
                   *halves, sds((6, width), F32), sds((1, hidden), F32)),
        in_specs=vmem(6 + len(vectors)), out_specs=(*vmem(6), pl.BlockSpec(memory_space=pl.ANY), *vmem(2)),
        scratch_shapes=[
            pltpu.VMEM(x.shape, F32), pltpu.VMEM((seqs, part, 128), F32), pltpu.VMEM(x.shape, F32),
            pltpu.VMEM((total, width), BF16), pltpu.VMEM((total, hidden), BF16), pltpu.VMEM((total, hidden), F32),
            pltpu.VMEM((total, width), BF16), pltpu.VMEM((total, hidden), BF16), pltpu.VMEM((total, width), BF16),
            pltpu.VMEM((3 * seqs, part, width), BF16), pltpu.VMEM((3, seqs, part, width), BF16),
            pltpu.VMEM(x.shape, BF16), pltpu.VMEM((6, 8, width), F32), pltpu.VMEM((8, hidden), F32),
            pltpu.VMEM((1, hidden), F32),
            pltpu.VMEM((2 * side, rows // 2, width), BF16),
            pltpu.SemaphoreType.DMA((2, 6 * seqs)), pltpu.SemaphoreType.DMA((2, 2 * side)),
        ],
        compiler_params=pltpu.CompilerParams(collective_id=2, has_side_effects=True, vmem_limit_bytes=LIMIT),
        cost_estimate=pl.CostEstimate(flops=14 * total * width * hidden, transcendentals=total * hidden,
                                      bytes_accessed=30 << 20),
        name="middle",
    )(c, x, wo, wi, wf, *vectors, gout)


def project_back_kernel(seqs, part, rows, dq, dk, dv, wq, wk, wv, dz1,
                        gin, g_q, g_k, g_v, g_b, give, got, sems):
    me = lax.axis_index("head")
    other = 1 - me
    meet(other)

    def total_of(s, p):
        at = pl.ds(pl.multiple_of((2 * s + p) * part, part), part)
        return dot_t(dq[at, :], wq[...]) + dot_t(dk[at, :], wk[...]) + dot_t(dv[at, :], wv[...])

    for s in range(seqs):
        give[s] = total_of(s, other).astype(BF16)
        to_partner(give.at[s], got.at[s], sems, s, other).start()
    g_q[...] = t_dot(rows[...], dq[...]).astype(BF16)
    g_k[...] = t_dot(rows[...], dk[...]).astype(BF16)
    g_v[...] = t_dot(rows[...], dv[...]).astype(BF16)
    g_b[0:1, :] = jnp.sum(fold(dq[...].astype(F32)), axis=0, keepdims=True)
    g_b[1:2, :] = jnp.sum(fold(dv[...].astype(F32)), axis=0, keepdims=True)
    for s in range(seqs):
        own = total_of(s, me).astype(BF16)
        to_partner(give.at[s], got.at[s], sems, s, other).wait()
        gin[s] = (dz1[s] + (own.astype(F32) + got[s].astype(F32))).astype(BF16)


def project_back(rows, dq, dk, dv, wq, wk, wv, dz1):
    seqs, part, width = dz1.shape
    sds = jax.ShapeDtypeStruct
    grad = sds(wq.shape, BF16)
    return pl.pallas_call(
        functools.partial(project_back_kernel, seqs, part),
        out_shape=(sds(dz1.shape, BF16), grad, grad, grad, sds((2, wq.shape[1]), F32)),
        in_specs=vmem(8), out_specs=tuple(vmem(5)),
        scratch_shapes=[pltpu.VMEM(dz1.shape, BF16), pltpu.VMEM(dz1.shape, BF16), pltpu.SemaphoreType.DMA((2, seqs))],
        compiler_params=pltpu.CompilerParams(collective_id=3, has_side_effects=True, vmem_limit_bytes=LIMIT),
        cost_estimate=pl.CostEstimate(flops=12 * rows.size * wq.shape[1], transcendentals=0, bytes_accessed=16 << 20),
        name="project_back",
    )(rows, dq, dk, dv, wq, wk, wv, dz1)
LINE = 16
ROWS = 256
LATE_COLORS = (0, 1, 2, 3, 2, 3)
PRECEDENCE = (4, 18, 28, 24, 6, 31, 14, 24, 33, 31, 35, 17, 18, 35, 27, 25, 9, 35, 23, 15, 35, 21, 35, 19)
LANDS = ("gather", "out", "back_in", "back_mid", "back_out")


def grid_bits(n):
    bits = n.bit_length() - 1
    side = bits // 3
    return (0, side, 2 * side), bits


def chunk_plan(n, color, rows):
    (bx, by, bz), bits = grid_bits(n)
    order = (by, bx) if color % 2 else (bx, by)
    line = n == LINE
    plan, length = [], rows
    if line and color >= 2:
        plan = [("far_in", bz, 3 * rows // 4), ("far_mid", bz, rows // 2), ("far_out", bz, rows // 4)]
        length = rows // 4
    if not line:
        order = (*order, bz)
    for b in order:
        length //= 2
        plan.append(("scatter", b, length))
    if line and color < 2:
        plan += [(kind, bz, length) for kind in ("in", "mid", "out")]
    plan += [("double", b, length) for b in range(bits) if not line and b not in order]
    for b in reversed(order):
        plan.append(("gather", b, length))
        length *= 2
    if line and color >= 2:
        plan += [("back_in", bz, rows // 4), ("back_mid", bz, rows // 2), ("back_out", bz, 3 * rows // 4)]
    return plan


def event_order(n, plans, rows):
    first, _ = grid_bits(n)
    lag = 0.16

    def path(kind, b):
        place = kind.split("_")[-1]
        if place in ("in", "mid", "out"):
            return ("in", "mid", "out").index(place) + 2
        return (b >= first[1]) + (b >= first[2])

    work = [[(path(kind, b), size / rows) for kind, b, size in plan] for plan in plans]
    free, ready, step, events = [0.0] * 5, [0.0] * len(plans), [0] * len(plans), []
    for _ in range(sum(map(len, work))):
        start, _, c = min((max(ready[c], free[row[step[c]][0]]), -PRECEDENCE[c % len(PRECEDENCE)], c)
                          for c, row in enumerate(work) if step[c] < len(row))
        link, span = work[c][step[c]]
        free[link] = start + span
        ready[c] = free[link] + lag
        events.append((start, c, step[c]))
        step[c] += 1
    events += [(r, c, len(work[c])) for c, r in enumerate(ready)]
    return [(c, s) for _, c, s in sorted(events)]


def flip(index, bit):
    return index + (1 - 2 * ((index // (1 << bit)) % 2)) * (1 << bit)


def chunk_pieces(shapes, rows, width):
    chunks = []
    for i, (height, cols) in enumerate(shapes):
        per = max(1, width // cols)
        for r in range(0, height, rows * per):
            for col in range(0, cols, width):
                span = min(cols, width)
                chunks.append([(i, r + j * rows, col, span, j * span) for j in range(per)])
    return chunks


def only(cond, body):
    if cond is None:
        body()
    else:
        pl.when(cond)(body)


def reduce_kernel(n, plans, rows, loads, saves, count, results, *refs):
    grads, (small, g_bi, g_b) = refs[:count], refs[count:count + 3]
    refs = refs[count + 3:]
    sums, tiny_out = refs[:results], refs[results]
    work, got, full, hold, tiny_got, load_sem, save_sem, send_sem, recv_sem, tiny_sem = refs[results + 1:]
    nc = len(plans)
    me, head = lax.axis_index("batch"), lax.axis_index("head")
    first, bits = grid_bits(n)
    bit_of = [(me // (1 << b)) % 2 for b in range(bits)]
    z = me // (1 << first[2])
    side = z // 2
    end = z % 3 == 0
    middle = z % 3 != 0
    mirror = me + (3 - 2 * z) * (1 << first[2])

    spans = []
    for plan in plans:
        off, length, at, row = 0, rows, 0, []
        quarter = rows // 4
        for kind, b, size in plan:
            where = None if kind in LANDS else at
            at += 0 if kind in LANDS else size
            if kind == "scatter":
                row.append((off + bit_of[b] * size, off + (1 - bit_of[b]) * size, size, where))
                off = row[-1][0]
            elif kind == "gather":
                row.append((off, off, size, where))
                off = off - bit_of[b] * size
            elif kind in ("far_in", "back_out"):
                row.append(((1 - side) * quarter, (1 - side) * quarter, size, where))
            elif kind == "far_mid":
                row.append((side * 2 * quarter, (1 - side) * 2 * quarter, size, where))
            elif kind == "back_mid":
                row.append((side * 2 * quarter, side * 2 * quarter, size, where))
            elif kind in ("far_out", "back_in"):
                row.append((side * 3 * quarter, side * 3 * quarter, size, where))
                off = z * quarter
            else:
                row.append((off, off, size, where))
        spans.append(row)

    def roles(kind):
        place = kind.split("_")[-1]
        return {"in": (end, middle), "mid": (middle, middle), "out": (middle, end)}.get(place, (None, None))

    def moves(c, out):
        if out:
            for k, (i, r, col, span, at) in enumerate(saves[c]):
                outside = sums[i].at[pl.ds(r, rows), pl.ds(col, span)]
                yield pltpu.make_async_copy(full.at[c, :, pl.ds(at, span)], outside, save_sem.at[c, k])
        elif loads[c] is None:
            for k, (i, r, col, span, at) in enumerate(saves[c]):
                outside = grads[i + count - results].at[pl.ds(r, rows), pl.ds(col, span)]
                yield pltpu.make_async_copy(outside, work.at[c, :, pl.ds(at, span)], load_sem.at[c, k])
        else:
            kept, kept_at, given, given_at = loads[c]
            keep, _, length, at = spans[c][0]
            inside = work.at[c, pl.ds(pl.multiple_of(keep, 16), length)]
            yield pltpu.make_async_copy(grads[kept].at[kept_at], inside, load_sem.at[c, 0])
            yield pltpu.make_async_copy(grads[given].at[given_at], got.at[c, pl.ds(at, length)], load_sem.at[c, 1])

    for c in range(nc):
        for move in moves(c, False):
            move.start()
    hold[...] = jnp.zeros_like(hold)
    hold[0:6, :] = small[...]
    width, row = hold.shape[1], 8
    for j in range(g_bi.shape[1] // width):
        hold[row:row + 1, :] = g_bi[:, j * width:(j + 1) * width]
        row += 1
    cols = g_b.shape[1]
    for j in range(2):
        hold[row + j * cols // width:row + j * cols // width + 1, pl.ds(j * cols % width, cols)] = g_b[j:j + 1, :]
    barrier = pltpu.get_barrier_semaphore()
    friends = [flip(me, b) for b in range(bits)] + ([mirror] if n == LINE else [])
    for friend in friends:
        pl.semaphore_signal(barrier, inc=1, device_id={"batch": friend}, device_id_type=MESH)
    pl.semaphore_signal(barrier, inc=1, device_id={"head": 1 - head}, device_id_type=MESH)
    pl.semaphore_wait(barrier, len(friends) + 1)

    def copy_of(c, s):
        kind, b, _ = plans[c][s]
        _, start, length, at = spans[c][s]
        place = (c, pl.ds(pl.multiple_of(start, 16), length))
        src = full.at[place] if kind in LANDS else work.at[place]
        dst = full.at[place] if kind in LANDS else got.at[c, pl.ds(at, length)]
        return pltpu.make_async_remote_copy(
            src_ref=src, dst_ref=dst, send_sem=send_sem.at[c, s], recv_sem=recv_sem.at[c, s],
            device_id={"batch": mirror if kind.endswith("mid") else flip(me, b)}, device_id_type=MESH)

    def finish(c, s):
        kind = plans[c][s][0]
        keep, _, length, at = spans[c][s]
        sender, receiver = roles(kind)
        if s == 0 and loads[c] is not None:
            for move in moves(c, False):
                move.wait()
        else:
            only(sender, lambda: copy_of(c, s).wait_send())

        def take():
            if s > 0 or loads[c] is None:
                copy_of(c, s).wait_recv()
            if kind in LANDS:
                return
            target = full if plans[c][s + 1][0] in LANDS else work

            def add(i, _):
                here = pl.ds(pl.multiple_of(keep + i * 16, 16), 16)
                there = pl.ds(pl.multiple_of(at + i * 16, 16), 16)
                target[c, here, :] = (work[c, here, :].astype(F32) + got[c, there, :].astype(F32)).astype(BF16)
                return 0
            lax.fori_loop(0, length // 16, add, 0)
        only(receiver, take)

    def tiny_copy(k):
        rest = hold.at[pl.ds(0, 8)] if k == 0 else hold
        there = tiny_got.at[k, pl.ds(0, 8)] if k == 0 else tiny_got.at[k]
        target = {"head": 1 - head} if k == 0 else {"batch": flip(me, k - 1)}
        return pltpu.make_async_remote_copy(
            src_ref=rest, dst_ref=there, send_sem=tiny_sem.at[0, k], recv_sem=tiny_sem.at[1, k],
            device_id=target, device_id_type=MESH)

    def tiny_finish(k):
        tiny_copy(k).wait()
        if k == 0:
            hold[0:8, :] += tiny_got[0, 0:8, :]
        else:
            hold[...] += tiny_got[k]

    done = [load is not None for load in loads]
    events = [(c, s + done[c]) for c, s in event_order(n, [p[d:] for p, d in zip(plans, done)], rows)]
    gap = len(events) // (bits + 2)
    for e, (c, s) in enumerate(events):
        if s == 0:
            for move in moves(c, False):
                move.wait()
        else:
            finish(c, s - 1)
        if s == len(plans[c]):
            for move in moves(c, True):
                move.start()
        else:
            only(roles(plans[c][s][0])[0], lambda: copy_of(c, s).start())
        if e % gap == 0 and e // gap <= bits:
            k = e // gap
            if k > 0:
                tiny_finish(k - 1)
            tiny_copy(k).start()
    tiny_finish(bits)
    tiny_out[...] = hold[...]
    for c in range(nc):
        for move in moves(c, True):
            move.wait()


def reduce_gradients(early, late, shapes, tiny, n):
    width = tiny[0].shape[1]
    tiny_shape = (16, width)
    saves = chunk_pieces(shapes, ROWS, width)
    outer = early[3].shape[0]
    edge = early[0].shape[0] - 2 * outer
    slots, plans, loads = [0, 0], [], []
    for which, count in enumerate((outer, outer, edge)):
        for c in range(count):
            color = c * 2 // count
            kept = which * outer + c
            loads.append((0, kept, 3, c) if which == 1 else (0, kept, 1 + color, slots[color]))
            slots[color] += which != 1
            plans.append(chunk_plan(n, color, ROWS))
    for c in range(len(saves) - len(plans)):
        plans.append(chunk_plan(n, LATE_COLORS[c % len(LATE_COLORS)], ROWS))
        loads.append(None)
    nc = len(saves)
    stages = max(len(plan) for plan in plans)
    _, bits = grid_bits(n)
    got_rows = max(sum(size for kind, _, size in plan if kind not in LANDS) for plan in plans)
    grads = (*early, *late)
    hbm = lambda k: [pl.BlockSpec(memory_space=pl.ANY)] * k
    done = pl.pallas_call(
        functools.partial(reduce_kernel, n, plans, ROWS, loads, saves, len(grads), len(shapes)),
        out_shape=(*(jax.ShapeDtypeStruct(shape, BF16) for shape in shapes), jax.ShapeDtypeStruct(tiny_shape, F32)),
        in_specs=hbm(len(grads)) + vmem(3), out_specs=tuple(hbm(len(shapes)) + vmem(1)),
        scratch_shapes=[
            pltpu.VMEM((nc, ROWS, width), BF16), pltpu.VMEM((nc, got_rows, width), BF16),
            pltpu.VMEM((nc, ROWS, width), BF16), pltpu.VMEM(tiny_shape, F32),
            pltpu.VMEM((bits + 1,) + tiny_shape, F32),
            pltpu.SemaphoreType.DMA((nc, 2)), pltpu.SemaphoreType.DMA((nc, 2)),
            pltpu.SemaphoreType.DMA((nc, stages)), pltpu.SemaphoreType.DMA((nc, stages)),
            pltpu.SemaphoreType.DMA((2, bits + 1)),
        ],
        compiler_params=pltpu.CompilerParams(collective_id=0, has_side_effects=True, vmem_limit_bytes=LIMIT),
        name="reduce_gradients",
    )(*grads, *tiny)
    return done[:-1], done[-1]


def results_kernel(count, plain, *refs):
    ins, tiny, outs = refs[:count + plain], refs[count + plain], refs[count + plain + 1:]
    for src, dst in zip(ins, outs):
        dst[...] = src[...].astype(dst.dtype)

    @pl.when(pl.program_id(0) == 0)
    def _():
        row = 0
        for place, dst in zip((0, 1, 2, 3, 4, 5, 8), outs[count + plain:]):
            width = tiny.shape[1]
            for j in range(dst.shape[0] // width):
                dst[pl.ds(j * width, width)] = tiny[place + j, :]
                row = place + j + 1
        for j, dst in enumerate(outs[count + plain + 7:]):
            at = j * dst.shape[0]
            dst[...] = tiny[row + at // tiny.shape[1], pl.ds(at % tiny.shape[1], dst.shape[0])]


def results(grads, rows, tiny, hidden, cols, steps=8):
    flat = [r.reshape(-1, r.shape[-1]) for r in rows]
    blocks = [pl.BlockSpec((a.shape[0] // steps, a.shape[1]), lambda i: (i, 0)) for a in (*grads, *flat)]
    vectors = [tiny.shape[1]] * 6 + [hidden, cols, cols]
    done = pl.pallas_call(
        functools.partial(results_kernel, len(grads), len(flat)),
        grid=(steps,),
        in_specs=blocks + [pl.BlockSpec(tiny.shape, lambda i: (0, 0))],
        out_specs=tuple(blocks + [pl.BlockSpec((v,), lambda i: (0,)) for v in vectors]),
        out_shape=tuple([jax.ShapeDtypeStruct(g.shape, F32) for g in grads]
                        + [jax.ShapeDtypeStruct(f.shape, f.dtype) for f in flat]
                        + [jax.ShapeDtypeStruct((v,), F32) for v in vectors]),
        compiler_params=pltpu.CompilerParams(vmem_limit_bytes=LIMIT),
        name="results",
    )(*grads, *flat, tiny)
    grads, flat, vectors = done[:len(grads)], done[len(grads):-len(vectors)], done[-len(vectors):]
    return grads, [f.reshape(r.shape) for f, r in zip(flat, rows)], vectors


def on_device(n_batch, inputs, prior_scores, lengths, w_query, w_key, w_value, b_query, b_value, w_output, b_output,
              gain_attn, shift_attn, w_inner, b_inner, w_outer, b_outer, gain_ffn, shift_ffn, grad_out, grad_scores):
    width = inputs.shape[2]
    vectors = (b_output, gain_attn, shift_attn, b_outer, gain_ffn, shift_ffn, b_inner)
    rows, q, k, v = project_rows(inputs, w_query, w_key, w_value, b_query, b_value)
    new_scores, context, norm = attend(lengths, q, k, v, prior_scores)
    firsts = grid_bits(n_batch)[0][:2]
    outputs, dz1, dc, keep, *gives, far, small, g_bi = middle(
        context, inputs, w_output, w_inner, w_outer, vectors, grad_out, firsts, ROWS)
    taken = [lax.ppermute(give, "batch", [(i, flip(i, first)) for i in range(n_batch)])
             for give, first in zip(gives, firsts)]
    grad_prior, dq, dk, dv = attend_back(lengths, q, k, v, dc, prior_scores, norm, grad_scores)
    grad_inputs, g_wq, g_wk, g_wv, g_b = project_back(rows, dq, dk, dv, w_query, w_key, w_value, dz1)
    late = (g_wq, g_wk, g_wv)
    shapes = [w_inner.shape, w_outer.shape, w_output.shape] + [g.shape for g in late]
    grads, tiny = reduce_gradients((keep, *taken, far), late, shapes, (small, g_bi, g_b), n_batch)
    hidden, cols = g_bi.shape[1], g_b.shape[1]
    grads, (outputs, grad_inputs), vectors = results(grads, (outputs, grad_inputs), tiny, hidden, cols)
    g_wi, g_wf, g_wo, g_wq, g_wk, g_wv = grads
    g_bo, g_g1, g_s1, g_bf, g_g2, g_s2, g_bi, g_bq, g_bv = vectors
    return (outputs, new_scores, grad_inputs, grad_prior, g_wq, g_wk, g_wv, g_bq, g_bv, g_wo,
            g_bo, g_g1, g_s1, g_wi, g_bi, g_wf, g_bf, g_g2, g_s2)


def solution(mesh):
    seq, scores, whole = P("batch", "head", None), P("batch", "head", None, None), P()
    down, across, vector = P("head", None), P(None, "head"), P("head")
    in_specs = (seq, scores, P("batch"), across, across, across, vector, vector, down, whole, whole, whole,
                across, vector, down, whole, whole, whole, seq, scores)
    out_specs = (seq, scores, seq, scores, across, across, across, vector, vector, down, whole, whole, whole,
                 across, vector, down, whole, whole, whole)
    layer = functools.partial(on_device, mesh.shape["batch"])
    return jax.shard_map(layer, mesh=mesh, in_specs=in_specs, out_specs=out_specs, check_vma=False)
```

```python
import functools
import jax, jax.numpy as jnp
from jax import lax
from jax.experimental import pallas as pl
from jax.experimental.pallas import tpu as pltpu
from jax.sharding import PartitionSpec as P

MESH = pl.DeviceIdType.MESH
F32, BF16 = jnp.float32, jnp.bfloat16
EPS = 1e-12
NEG = -1e30
LIMIT = 64 * 1000 * 1000


def dot(a, b):
    return jnp.dot(a, b, preferred_element_type=F32)


def dot_t(a, b):
    return lax.dot_general(a, b, (((1,), (1,)), ((), ())), preferred_element_type=F32)


def t_dot(a, b):
    return lax.dot_general(a, b, (((0,), (0,)), ((), ())), preferred_element_type=F32)


def meet(partner):
    barrier = pltpu.get_barrier_semaphore()
    pl.semaphore_signal(barrier, inc=1, device_id={"head": partner}, device_id_type=MESH)
    pl.semaphore_wait(barrier, 1)


def to_partner(src, dst, sems, i, partner):
    return pltpu.make_async_remote_copy(
        src_ref=src, dst_ref=dst, send_sem=sems.at[0, i], recv_sem=sems.at[1, i],
        device_id={"head": partner}, device_id_type=MESH)


def vmem(count):
    return [pl.BlockSpec(memory_space=pltpu.VMEM)] * count


def as_row(vector):
    return vector[...].astype(F32).reshape(1, vector.shape[0])


def project_kernel(seqs, part, x, wq, wk, wv, b_query, b_value, rows, q, k, v, got, sems):
    me = lax.axis_index("head")
    other = 1 - me
    meet(other)
    for s in range(seqs):
        to_partner(x.at[s], got.at[s], sems, s, other).start()

    bias_q, bias_v = as_row(b_query), as_row(b_value)

    def emit(block, s, p):
        at = pl.ds(pl.multiple_of((2 * s + p) * part, part), part)
        rows[at, :] = block
        q[at, :] = (dot(block, wq[...]) + bias_q).astype(BF16)
        k[at, :] = dot(block, wk[...]).astype(BF16)
        v[at, :] = (dot(block, wv[...]) + bias_v).astype(BF16)

    def own(s, _):
        emit(x[s], s, me)
        return 0

    lax.fori_loop(0, seqs, own, 0)
    for s in range(seqs):
        to_partner(x.at[s], got.at[s], sems, s, other).wait()

    def theirs(s, _):
        emit(got[s], s, other)
        return 0

    lax.fori_loop(0, seqs, theirs, 0)


def project_rows(x, wq, wk, wv, b_query, b_value):
    seqs, part, width = x.shape
    total, cols = 2 * seqs * part, wq.shape[1]
    out = jax.ShapeDtypeStruct((total, cols), BF16)
    return pl.pallas_call(
        functools.partial(project_kernel, seqs, part),
        out_shape=(jax.ShapeDtypeStruct((total, width), BF16), out, out, out),
        in_specs=vmem(6), out_specs=tuple(vmem(4)),
        scratch_shapes=[pltpu.VMEM(x.shape, BF16), pltpu.SemaphoreType.DMA((2, seqs))],
        compiler_params=pltpu.CompilerParams(collective_id=1, has_side_effects=True, vmem_limit_bytes=LIMIT),
        name="project_rows",
    )(x, wq, wk, wv, b_query, b_value)


def attend_kernel(block, head, lengths, q, k, v, prior, score, c, norm):
    full = k.shape[0]
    live = lax.broadcasted_iota(jnp.int32, (1, full), 1) < lengths[pl.program_id(0)]
    first = lax.broadcasted_iota(jnp.int32, (1, 2 * head), 1) < head
    scale = head ** -0.5
    for r in range(0, full, block):
        rows = pl.ds(r, block)
        queries = q[rows, :] * jnp.asarray(scale, BF16)
        parts, norms = [], []
        for h in range(2):
            mine = jnp.where(first == (h == 0), queries, jnp.zeros_like(queries))
            scores = dot_t(mine, k[...]) + prior[0, h, rows, :].astype(F32)
            score[0, h, rows, :] = scores.astype(BF16)
            masked = jnp.where(live, scores, NEG)
            top = jnp.max(masked, axis=-1, keepdims=True)
            terms = jnp.exp(masked - top)
            total = jnp.sum(terms, axis=-1, keepdims=True)
            probs = (terms * (1.0 / total)).astype(BF16)
            parts.append(dot(probs, v[...]))
            norms.append(top + jnp.log(total))
        c[rows, :] = jnp.where(first, parts[0], parts[1]).astype(BF16)
        norm[0, 0, rows, :] = jnp.where(first, norms[0], norms[1])


def attend(lengths, q, k, v, prior):
    seqs, heads, full, _ = prior.shape
    pair = q.shape[1] // heads * 2
    rows = pl.BlockSpec((full, pair), lambda s, h, n: (s, h))
    big = pl.BlockSpec((1, 2, full, full), lambda s, h, n: (s, h, 0, 0))
    norm = pl.BlockSpec((1, 1, full, pair), lambda s, h, n: (s, h, 0, 0))
    return pl.pallas_call(
        functools.partial(attend_kernel, 256, pair // 2),
        grid_spec=pltpu.PrefetchScalarGridSpec(
            num_scalar_prefetch=1, grid=(seqs, heads // 2),
            in_specs=[rows, rows, rows, big], out_specs=(big, rows, norm)),
        out_shape=(jax.ShapeDtypeStruct(prior.shape, BF16), jax.ShapeDtypeStruct(q.shape, BF16),
                   jax.ShapeDtypeStruct((seqs, heads // 2, full, pair), F32)),
        compiler_params=pltpu.CompilerParams(vmem_limit_bytes=LIMIT),
        name="attend",
    )(lengths, q, k, v, prior)


def attend_back_kernel(block, head, lengths, q, k, v, dc, prior, norm, given, grad, dq, dk, dv):
    full = k.shape[0]
    live = lax.broadcasted_iota(jnp.int32, (1, full), 1) < lengths[pl.program_id(0)]
    first = lax.broadcasted_iota(jnp.int32, (1, 2 * head), 1) < head
    scale = head ** -0.5
    q_t, dc_t = q[...].T, dc[...].T
    dk_t, dv_t = [0.0, 0.0], [0.0, 0.0]
    for r in range(0, full, block):
        rows = pl.ds(r, block)
        queries, cots = q[rows, :] * jnp.asarray(scale, BF16), dc[rows, :]
        parts = []
        for h in range(2):
            mine = first == (h == 0)
            scores = dot_t(jnp.where(mine, queries, jnp.zeros_like(queries)), k[...])
            scores = scores + prior[0, h, rows, :].astype(F32)
            probs = jnp.exp(jnp.where(live, scores, NEG) - norm[0, 0, rows, h * head:h * head + 1])
            dp = dot_t(jnp.where(mine, cots, jnp.zeros_like(cots)), v[...])
            delta = jnp.sum(probs * dp, axis=-1, keepdims=True)
            ds = (probs * (dp - delta) + given[0, h, rows, :].astype(F32)).astype(BF16)
            grad[0, h, rows, :] = ds
            parts.append(dot(ds, k[...]))
            lanes = slice(h * head, (h + 1) * head)
            dk_t[h] = dk_t[h] + dot(q_t[lanes, r:r + block], ds)
            dv_t[h] = dv_t[h] + dot(dc_t[lanes, r:r + block], probs.astype(BF16))
        dq[rows, :] = (jnp.where(first, parts[0], parts[1]) * scale).astype(BF16)
    dk[...] = (jnp.concatenate(dk_t, axis=0) * scale).T.astype(BF16)
    dv[...] = jnp.concatenate(dv_t, axis=0).T.astype(BF16)


def attend_back(lengths, q, k, v, dc, prior, norm, given):
    seqs, heads, full, _ = prior.shape
    pair = q.shape[1] // heads * 2
    rows = pl.BlockSpec((full, pair), lambda s, h, n: (s, h))
    big = pl.BlockSpec((1, 2, full, full), lambda s, h, n: (s, h, 0, 0))
    norms = pl.BlockSpec((1, 1, full, pair), lambda s, h, n: (s, h, 0, 0))
    flat = jax.ShapeDtypeStruct(q.shape, BF16)
    return pl.pallas_call(
        functools.partial(attend_back_kernel, 256, pair // 2),
        grid_spec=pltpu.PrefetchScalarGridSpec(
            num_scalar_prefetch=1, grid=(seqs, heads // 2),
            in_specs=[rows, rows, rows, rows, big, norms, big], out_specs=(big, rows, rows, rows)),
        out_shape=(jax.ShapeDtypeStruct(prior.shape, BF16), flat, flat, flat),
        compiler_params=pltpu.CompilerParams(vmem_limit_bytes=LIMIT),
        cost_estimate=pl.CostEstimate(flops=40 * full * full * seqs * heads * pair // 2, transcendentals=prior.size,
                                      bytes_accessed=6 * prior.size),
        name="attend_back",
    )(lengths, q, k, v, dc, prior, norm, given)


def fold(value):
    return jnp.sum(value.reshape(value.shape[0] // 8, 8, value.shape[1]), axis=0)


def norm_stats(z):
    mean = jnp.mean(z, axis=-1, keepdims=True)
    centred = z - mean
    r = lax.rsqrt(jnp.mean(centred * centred, axis=-1, keepdims=True) + EPS)
    return centred * r, r


def norm_back(cot, gain, unit, r):
    e = cot * gain
    return r * (e - jnp.mean(e, axis=-1, keepdims=True) - unit * jnp.mean(e * unit, axis=-1, keepdims=True))


def middle_kernel(seqs, part, firsts, c, x, wo, wi, wf, b_output, gain1, shift1, b_outer, gain2, shift2, b_inner, gout,
                  out, dz1, dc, keep, give_x, give_y, quarter, small, g_bi,
                  unit1, r1, hn, act, slope, df, du, da, give, got, own, sums, bsum, bi, keep_f, give_f, taken, sems, far_sems):
    me = lax.axis_index("head")
    other = 1 - me
    width = x.shape[2]
    hidden = wi.shape[1]
    tile = 512
    sub = 64
    barrier = pltpu.get_barrier_semaphore()
    pl.semaphore_signal(barrier, inc=1, device_id={"head": other}, device_id_type=MESH)
    for first in firsts:
        pl.semaphore_signal(barrier, inc=1, device_id={"batch": flip(lax.axis_index("batch"), first)},
                            device_id_type=MESH)
    pl.semaphore_wait(barrier, 3)
    b_output, gain1, shift1, b_outer, gain2, shift2 = map(as_row, (b_output, gain1, shift1, b_outer, gain2, shift2))
    sums[...] = jnp.zeros_like(sums)
    bsum[...] = jnp.zeros_like(bsum)
    bi[...] = as_row(b_inner)

    def rows_of(s, p):
        return pl.ds(pl.multiple_of((2 * s + p) * part, part), part)

    def at(start, size):
        return pl.ds(pl.multiple_of(start, size), size)

    def attn_part(s, _):
        give[s] = dot(c[rows_of(s, other), :], wo[...]).astype(BF16)
        return 0
    for s in range(seqs):
        attn_part(s, 0)
        to_partner(give.at[s], got.at[0, s], sems, s, other).start()

    def attn_own(s, _):
        own[s] = dot(c[rows_of(s, me), :], wo[...]).astype(BF16)
        return 0
    lax.fori_loop(0, seqs, attn_own, 0)
    for s in range(seqs):
        to_partner(give.at[s], got.at[0, s], sems, s, other).wait()

        def first_norm(i, _):
            rows = at(i * sub, sub)
            z = x[s, rows, :].astype(F32) + (own[s, rows, :].astype(F32) + got[0, s, rows, :].astype(F32)) + b_output
            unit, r = norm_stats(z)
            unit1[s, rows, :] = unit
            r1[s, rows, :] = jnp.broadcast_to(r, (sub, 128))
            hn[at((2 * s + me) * part + i * sub, sub), :] = (unit * gain1 + shift1).astype(BF16)
            return 0
        lax.fori_loop(0, part // sub, first_norm, 0)
        block = hn.at[rows_of(s, me)]
        to_partner(block, block, sems, seqs + s, other).start()

    order = [(0, me)] + [(s, other) for s in range(seqs)] + [(s, me) for s in range(1, seqs)]

    def inner(s, p):
        rows = rows_of(s, p)

        def columns(j, _):
            cols = at(j * tile, tile)
            u = dot(hn[rows, :], wi[:, cols]) + bi[:, cols]
            cdf = 0.5 * (1.0 + lax.erf(u * 0.7071067811865476))
            act[rows, cols] = (u * cdf).astype(BF16)
            slope[rows, cols] = cdf + u * (jnp.exp(-0.5 * u * u) * 0.3989422804014327)
            return 0
        lax.fori_loop(0, hidden // tile, columns, 0)

    def outer(s, p, place):
        rows = rows_of(s, p)

        def columns(j, _):
            cols = at(j * tile, tile)
            place[s, :, cols] = dot(act[rows, :], wf[:, cols]).astype(BF16)
            return 0
        lax.fori_loop(0, width // tile, columns, 0)

    for n, (s, p) in enumerate(order):
        if n == 1:
            for q in range(seqs):
                block = hn.at[rows_of(q, me)]
                to_partner(block, block, sems, seqs + q, other).wait()
        inner(s, p)
        if p is other:
            outer(s, p, give.at[pl.ds(seqs, seqs)])
            to_partner(give.at[seqs + s], got.at[1, s], sems, 2 * seqs + s, other).start()
        else:
            outer(s, p, own)

    for s in range(seqs):
        to_partner(give.at[seqs + s], got.at[1, s], sems, 2 * seqs + s, other).wait()

        def second_norm(i, _):
            rows = at(i * sub, sub)
            h = unit1[s, rows, :] * gain1 + shift1
            z = (own[s, rows, :].astype(F32) + got[1, s, rows, :].astype(F32)) + b_outer + h
            unit, r = norm_stats(z)
            out[s, rows, :] = (unit * gain2 + shift2).astype(BF16)
            g = gout[s, rows, :].astype(F32)
            d = norm_back(g, gain2, unit, r)
            dz1[s, rows, :] = d
            df[at((2 * s + me) * part + i * sub, sub), :] = d.astype(BF16)
            sums[3] += fold(d)
            sums[4] += fold(g * unit)
            sums[5] += fold(g)
            return 0
        lax.fori_loop(0, part // sub, second_norm, 0)
        block = df.at[rows_of(s, me)]
        to_partner(block, block, sems, 3 * seqs + s, other).start()

    mine = lax.axis_index("batch")
    gives = (give_x, give_y)
    half = keep.shape[1]
    per = hidden // width
    side = give_f.shape[0] // 2
    edge = give_x.shape[0] - side - side // 2

    def put(value, kept, axis, given):
        bit = (mine // (1 << firsts[axis])) % 2
        size = value.shape[0] // 2

        @pl.when(bit == 0)
        def _():
            kept[...] = value[:size].astype(BF16)
            given[...] = value[size:].astype(BF16)

        @pl.when(bit == 1)
        def _():
            kept[...] = value[size:].astype(BF16)
            given[...] = value[:size].astype(BF16)

    def far_copy(i, axis):
        return pltpu.make_async_remote_copy(
            src_ref=give_f.at[i], dst_ref=taken.at[i], send_sem=far_sems.at[0, i], recv_sem=far_sems.at[1, i],
            device_id={"batch": flip(mine, firsts[axis])}, device_id_type=MESH)

    def grads_outer():
        def give_outer(i, _):
            for axis in range(2):
                chunk = axis * side + i
                put(t_dot(act[:, at(chunk * 2 * half, 2 * half)], df[...]), keep_f.at[chunk], axis, give_f.at[chunk])
                far_copy(chunk, axis).start()
            return 0
        lax.fori_loop(0, side, give_outer, 0)

    def inner_back(s, p):
        rows = rows_of(s, p)

        def columns(j, _):
            cols = at(j * tile, tile)
            dg = dot_t(df[rows, :], wf[cols, :]).astype(BF16).astype(F32)
            low = (dg * slope[rows, cols]).astype(BF16)
            du[rows, cols] = low
            bsum[:, cols] += fold(low.astype(F32))
            return 0
        lax.fori_loop(0, hidden // tile, columns, 0)

    def outer_back(s, p, place):
        rows = rows_of(s, p)

        def columns(j, _):
            cols = at(j * tile, tile)
            place[s, :, cols] = dot_t(du[rows, :], wi[cols, :]).astype(BF16)
            return 0
        lax.fori_loop(0, width // tile, columns, 0)

    for n, (s, p) in enumerate(order):
        if n == 1:
            for q in range(seqs):
                block = df.at[rows_of(q, me)]
                to_partner(block, block, sems, 3 * seqs + q, other).wait()
            grads_outer()
        inner_back(s, p)
        if p is other:
            outer_back(s, p, give.at[pl.ds(2 * seqs, seqs)])
            to_partner(give.at[2 * seqs + s], got.at[2, s], sems, 4 * seqs + s, other).start()
        else:
            outer_back(s, p, own)

    for s in range(seqs):
        to_partner(give.at[2 * seqs + s], got.at[2, s], sems, 4 * seqs + s, other).wait()

        def first_back(i, _):
            rows = at(i * sub, sub)
            cot = dz1[s, rows, :] + (own[s, rows, :].astype(F32) + got[2, s, rows, :].astype(F32))
            unit = unit1[s, rows, :]
            d = norm_back(cot, gain1, unit, r1[s, rows, 0:1])
            dz1[s, rows, :] = d
            da[at((2 * s + me) * part + i * sub, sub), :] = d.astype(BF16)
            sums[0] += fold(d)
            sums[1] += fold(cot * unit)
            sums[2] += fold(cot)
            return 0
        lax.fori_loop(0, part // sub, first_back, 0)
        block = da.at[rows_of(s, me)]
        to_partner(block, block, sems, 5 * seqs + s, other).start()

    for axis in range(2):
        def give_inner(i, _, axis=axis):
            at_hn, at_du = at((axis * side + i) // per * 2 * half, 2 * half), at((axis * side + i) % per * width, width)
            put(t_dot(hn[:, at_hn], du[:, at_du]), keep.at[axis * side + i], axis, gives[axis].at[i])
            return 0
        lax.fori_loop(0, side, give_inner, 0)

    for s in range(seqs):
        block = da.at[rows_of(s, me)]
        to_partner(block, block, sems, 5 * seqs + s, other).wait()
    dc[...] = dot_t(da[...], wo[...]).astype(BF16)
    for axis in range(2):
        def give_output(i, _, axis=axis):
            cols = at((axis * edge + i) * 2 * half, 2 * half)
            put(t_dot(c[:, cols], da[...]), keep.at[2 * side + axis * edge + i], axis, gives[axis].at[side + i])
            return 0
        lax.fori_loop(0, edge, give_output, 0)
    small[...] = jnp.sum(sums[...], axis=1)
    g_bi[...] = jnp.sum(bsum[...], axis=0, keepdims=True)
    for axis in range(2):
        def far_done(i, _, axis=axis):
            chunk = axis * side + i
            far_copy(chunk, axis).wait()
            place = gives[1 - axis].at[side + edge + i // 2, at(i % 2 * (half // 2), half // 2)]
            put(keep_f[chunk].astype(F32) + taken[chunk].astype(F32), quarter.at[chunk], 1 - axis, place)
            return 0
        lax.fori_loop(0, side, far_done, 0)


def middle(c, x, wo, wi, wf, vectors, gout, firsts, rows):
    seqs, part, width = x.shape
    total, cols = c.shape
    hidden = wi.shape[1]
    sds = jax.ShapeDtypeStruct
    side, edge = hidden // rows // 2, cols // rows // 2
    halves = [sds((count, rows // 2, width), BF16)
              for count in (2 * side + 2 * edge, side + edge + side // 2, side + edge + side // 2)]
    halves.append(sds((2 * side, rows // 4, width), BF16))
    return pl.pallas_call(
        functools.partial(middle_kernel, seqs, part, firsts),
        out_shape=(sds(x.shape, BF16), sds(x.shape, F32), sds(c.shape, BF16),
                   *halves, sds((6, width), F32), sds((1, hidden), F32)),
        in_specs=vmem(6 + len(vectors)), out_specs=tuple(vmem(9)),
        scratch_shapes=[
            pltpu.VMEM(x.shape, F32), pltpu.VMEM((seqs, part, 128), F32),
            pltpu.VMEM((total, width), BF16), pltpu.VMEM((total, hidden), BF16), pltpu.VMEM((total, hidden), F32),
            pltpu.VMEM((total, width), BF16), pltpu.VMEM((total, hidden), BF16), pltpu.VMEM((total, width), BF16),
            pltpu.VMEM((3 * seqs, part, width), BF16), pltpu.VMEM((3, seqs, part, width), BF16),
            pltpu.VMEM(x.shape, BF16), pltpu.VMEM((6, 8, width), F32), pltpu.VMEM((8, hidden), F32),
            pltpu.VMEM((1, hidden), F32),
            *[pltpu.VMEM((2 * side, rows // 2, width), BF16)] * 3,
            pltpu.SemaphoreType.DMA((2, 6 * seqs)), pltpu.SemaphoreType.DMA((2, 2 * side)),
        ],
        compiler_params=pltpu.CompilerParams(collective_id=2, has_side_effects=True, vmem_limit_bytes=66 * 1000 * 1000),
        cost_estimate=pl.CostEstimate(flops=14 * total * width * hidden, transcendentals=total * hidden,
                                      bytes_accessed=30 << 20),
        name="middle",
    )(c, x, wo, wi, wf, *vectors, gout)


def project_back_kernel(seqs, part, rows, dq, dk, dv, wq, wk, wv, dz1,
                        gin, g_q, g_k, g_v, g_b, give, got, sems):
    me = lax.axis_index("head")
    other = 1 - me
    meet(other)

    def total_of(s, p):
        at = pl.ds(pl.multiple_of((2 * s + p) * part, part), part)
        return dot_t(dq[at, :], wq[...]) + dot_t(dk[at, :], wk[...]) + dot_t(dv[at, :], wv[...])

    for s in range(seqs):
        give[s] = total_of(s, other).astype(BF16)
        to_partner(give.at[s], got.at[s], sems, s, other).start()
    g_q[...] = t_dot(rows[...], dq[...]).astype(BF16)
    g_k[...] = t_dot(rows[...], dk[...]).astype(BF16)
    g_v[...] = t_dot(rows[...], dv[...]).astype(BF16)
    g_b[0:1, :] = jnp.sum(fold(dq[...].astype(F32)), axis=0, keepdims=True)
    g_b[1:2, :] = jnp.sum(fold(dv[...].astype(F32)), axis=0, keepdims=True)
    for s in range(seqs):
        own = total_of(s, me).astype(BF16)
        to_partner(give.at[s], got.at[s], sems, s, other).wait()
        gin[s] = (dz1[s] + (own.astype(F32) + got[s].astype(F32))).astype(BF16)


def project_back(rows, dq, dk, dv, wq, wk, wv, dz1):
    seqs, part, width = dz1.shape
    sds = jax.ShapeDtypeStruct
    grad = sds(wq.shape, BF16)
    return pl.pallas_call(
        functools.partial(project_back_kernel, seqs, part),
        out_shape=(sds(dz1.shape, BF16), grad, grad, grad, sds((2, wq.shape[1]), F32)),
        in_specs=vmem(8), out_specs=tuple(vmem(5)),
        scratch_shapes=[pltpu.VMEM(dz1.shape, BF16), pltpu.VMEM(dz1.shape, BF16), pltpu.SemaphoreType.DMA((2, seqs))],
        compiler_params=pltpu.CompilerParams(collective_id=3, has_side_effects=True, vmem_limit_bytes=LIMIT),
        cost_estimate=pl.CostEstimate(flops=12 * rows.size * wq.shape[1], transcendentals=0, bytes_accessed=16 << 20),
        name="project_back",
    )(rows, dq, dk, dv, wq, wk, wv, dz1)
LINE = 16
ROWS = 256
LATE_COLORS = (2, 3, 0, 1, 2, 0)
LAG = 0.16
PRECEDENCE = (22, 6, 15, 2, 35, 0, 7, 26, 35, 20, 25, 7, 20, 21, 9, 24, 29, 3, 10, 29, 34, 14, 14, 6)
LANDS = ("gather", "out", "back_in", "back_mid", "back_out")


def grid_bits(n):
    bits = n.bit_length() - 1
    side = bits // 3
    return (0, side, 2 * side), bits


def chunk_plan(n, color, rows):
    (bx, by, bz), bits = grid_bits(n)
    order = (by, bx) if color % 2 else (bx, by)
    line = n == LINE
    plan, length = [], rows
    if line and color >= 2:
        plan = [("far_in", bz, 3 * rows // 4), ("far_mid", bz, rows // 2), ("far_out", bz, rows // 4)]
        length = rows // 4
    if not line:
        order = (*order, bz)
    for b in order:
        length //= 2
        plan.append(("scatter", b, length))
    if line and color < 2:
        plan += [(kind, bz, length) for kind in ("in", "mid", "out")]
    plan += [("double", b, length) for b in range(bits) if not line and b not in order]
    for b in reversed(order):
        plan.append(("gather", b, length))
        length *= 2
    if line and color >= 2:
        plan += [("back_in", bz, rows // 4), ("back_mid", bz, rows // 2), ("back_out", bz, 3 * rows // 4)]
    return plan


def event_order(n, plans, rows):
    first, _ = grid_bits(n)

    def path(kind, b):
        place = kind.split("_")[-1]
        if place in ("in", "mid", "out"):
            return ("in", "mid", "out").index(place) + 2
        return (b >= first[1]) + (b >= first[2])

    work = [[(path(kind, b), size / rows) for kind, b, size in plan] for plan in plans]
    free, ready, step, events = [0.0] * 5, [0.0] * len(plans), [0] * len(plans), []
    for _ in range(sum(map(len, work))):
        start, _, c = min((max(ready[c], free[row[step[c]][0]]), -PRECEDENCE[c % len(PRECEDENCE)], c)
                          for c, row in enumerate(work) if step[c] < len(row))
        link, span = work[c][step[c]]
        free[link] = start + span
        ready[c] = free[link] + LAG
        events.append((start, c, step[c]))
        step[c] += 1
    events += [(r, c, len(work[c])) for c, r in enumerate(ready)]
    return [(c, s) for _, c, s in sorted(events)]


def flip(index, bit):
    return index + (1 - 2 * ((index // (1 << bit)) % 2)) * (1 << bit)


def chunk_pieces(shapes, rows, width):
    chunks = []
    for i, (height, cols) in enumerate(shapes):
        per = max(1, width // cols)
        for r in range(0, height, rows * per):
            for col in range(0, cols, width):
                span = min(cols, width)
                chunks.append([(i, r + j * rows, col, span, j * span) for j in range(per)])
    return chunks


def only(cond, body):
    if cond is None:
        body()
    else:
        pl.when(cond)(body)


def reduce_kernel(n, plans, rows, loads, saves, count, results, *refs):
    grads, (small, g_bi, g_b) = refs[:count], refs[count:count + 3]
    refs = refs[count + 3:]
    sums, tiny_out = refs[:results], refs[results]
    work, got, full, hold, tiny_got, load_sem, save_sem, send_sem, recv_sem, tiny_sem = refs[results + 1:]
    nc = len(plans)
    me, head = lax.axis_index("batch"), lax.axis_index("head")
    first, bits = grid_bits(n)
    done = [0 if load is None else load[0] for load in loads]
    bit_of = [(me // (1 << b)) % 2 for b in range(bits)]
    z = me // (1 << first[2])
    side = z // 2
    end = z % 3 == 0
    middle = z % 3 != 0
    mirror = me + (3 - 2 * z) * (1 << first[2])

    spans = []
    for plan in plans:
        off, length, at, row = 0, rows, 0, []
        quarter = rows // 4
        for kind, b, size in plan:
            where = None if kind in LANDS else at
            at += 0 if kind in LANDS else size
            if kind == "scatter":
                row.append((off + bit_of[b] * size, off + (1 - bit_of[b]) * size, size, where))
                off = row[-1][0]
            elif kind == "gather":
                row.append((off, off, size, where))
                off = off - bit_of[b] * size
            elif kind in ("far_in", "back_out"):
                row.append(((1 - side) * quarter, (1 - side) * quarter, size, where))
            elif kind == "far_mid":
                row.append((side * 2 * quarter, (1 - side) * 2 * quarter, size, where))
            elif kind == "back_mid":
                row.append((side * 2 * quarter, side * 2 * quarter, size, where))
            elif kind in ("far_out", "back_in"):
                row.append((side * 3 * quarter, side * 3 * quarter, size, where))
                off = z * quarter
            else:
                row.append((off, off, size, where))
        spans.append(row)

    def roles(kind):
        place = kind.split("_")[-1]
        return {"in": (end, middle), "mid": (middle, middle), "out": (middle, end)}.get(place, (None, None))

    def moves(c, out):
        if out:
            for k, (i, r, col, span, at) in enumerate(saves[c]):
                outside = sums[i].at[pl.ds(r, rows), pl.ds(col, span)]
                yield pltpu.make_async_copy(full.at[c, :, pl.ds(at, span)], outside, save_sem.at[c, k])
        elif loads[c] is None:
            for k, (i, r, col, span, at) in enumerate(saves[c]):
                outside = grads[i + count - results].at[pl.ds(r, rows), pl.ds(col, span)]
                yield pltpu.make_async_copy(outside, work.at[c, :, pl.ds(at, span)], load_sem.at[c, k])
        else:
            _, kept, kept_at, given, given_at, given_row = loads[c]
            keep, _, length, at = spans[c][done[c] - 1]
            inside = work.at[c, pl.ds(pl.multiple_of(keep, 16), length)]
            yield pltpu.make_async_copy(grads[kept].at[kept_at], inside, load_sem.at[c, 0])
            outside = grads[given].at[given_at, pl.ds(given_row, length)]
            yield pltpu.make_async_copy(outside, got.at[c, pl.ds(at, length)], load_sem.at[c, 1])

    events = [(c, s + done[c]) for c, s in event_order(n, [p[d:] for p, d in zip(plans, done)], rows)]
    for c, s in events:
        if s == done[c]:
            for move in moves(c, False):
                move.start()
    hold[...] = jnp.zeros_like(hold)
    hold[0:6, :] = small[...]
    width, row = hold.shape[1], 8
    for j in range(g_bi.shape[1] // width):
        hold[row:row + 1, :] = g_bi[:, j * width:(j + 1) * width]
        row += 1
    cols = g_b.shape[1]
    for j in range(2):
        hold[row + j * cols // width:row + j * cols // width + 1, pl.ds(j * cols % width, cols)] = g_b[j:j + 1, :]
    barrier = pltpu.get_barrier_semaphore()
    friends = [flip(me, b) for b in range(bits)] + ([mirror] if n == LINE else [])
    for friend in friends:
        pl.semaphore_signal(barrier, inc=1, device_id={"batch": friend}, device_id_type=MESH)
    pl.semaphore_signal(barrier, inc=1, device_id={"head": 1 - head}, device_id_type=MESH)
    pl.semaphore_wait(barrier, len(friends) + 1)

    def copy_of(c, s):
        kind, b, _ = plans[c][s]
        _, start, length, at = spans[c][s]
        place = (c, pl.ds(pl.multiple_of(start, 16), length))
        src = full.at[place] if kind in LANDS else work.at[place]
        dst = full.at[place] if kind in LANDS else got.at[c, pl.ds(at, length)]
        return pltpu.make_async_remote_copy(
            src_ref=src, dst_ref=dst, send_sem=send_sem.at[c, s], recv_sem=recv_sem.at[c, s],
            device_id={"batch": mirror if kind.endswith("mid") else flip(me, b)}, device_id_type=MESH)

    def finish(c, s):
        kind = plans[c][s][0]
        keep, _, length, at = spans[c][s]
        sender, receiver = roles(kind)
        if s == done[c] - 1:
            for move in moves(c, False):
                move.wait()
        else:
            only(sender, lambda: copy_of(c, s).wait_send())

        def take():
            if s != done[c] - 1:
                copy_of(c, s).wait_recv()
            if kind in LANDS:
                return
            target = full if plans[c][s + 1][0] in LANDS else work

            def add(i, _):
                here = pl.ds(pl.multiple_of(keep + i * 16, 16), 16)
                there = pl.ds(pl.multiple_of(at + i * 16, 16), 16)
                target[c, here, :] = (work[c, here, :].astype(F32) + got[c, there, :].astype(F32)).astype(BF16)
                return 0
            lax.fori_loop(0, length // 16, add, 0)
        only(receiver, take)

    def tiny_copy(k):
        rest = hold.at[pl.ds(0, 8)] if k == 0 else hold
        there = tiny_got.at[k, pl.ds(0, 8)] if k == 0 else tiny_got.at[k]
        target = {"head": 1 - head} if k == 0 else {"batch": flip(me, k - 1)}
        return pltpu.make_async_remote_copy(
            src_ref=rest, dst_ref=there, send_sem=tiny_sem.at[0, k], recv_sem=tiny_sem.at[1, k],
            device_id=target, device_id_type=MESH)

    def tiny_finish(k):
        tiny_copy(k).wait()
        if k == 0:
            hold[0:8, :] += tiny_got[0, 0:8, :]
        else:
            hold[...] += tiny_got[k]

    gap = len(events) // (bits + 2)
    for e, (c, s) in enumerate(events):
        if s == 0:
            for move in moves(c, False):
                move.wait()
        else:
            finish(c, s - 1)
        if s == len(plans[c]):
            for move in moves(c, True):
                move.start()
        else:
            only(roles(plans[c][s][0])[0], lambda: copy_of(c, s).start())
        if e % gap == 0 and e // gap <= bits:
            k = e // gap
            if k > 0:
                tiny_finish(k - 1)
            tiny_copy(k).start()
    tiny_finish(bits)
    tiny_out[...] = hold[...]
    for c in range(nc):
        for move in moves(c, True):
            move.wait()


def reduce_gradients(early, late, shapes, tiny, n):
    width = tiny[0].shape[1]
    tiny_shape = (16, width)
    saves = chunk_pieces(shapes, ROWS, width)
    outer = early[3].shape[0]
    edge = early[0].shape[0] - outer
    side = (outer + edge) // 2
    plans, loads = [], []
    for which, count in enumerate((outer, outer, edge)):
        for c in range(count):
            color, slot = c * 2 // count, c % (count // 2)
            if which == 1:
                loads.append((2, 3, c, 2 - color, side + slot // 2, slot % 2 * (ROWS // 4)))
            else:
                base = outer if which == 2 else 0
                loads.append((1, 0, base + c, 1 + color, base // 2 + slot, 0))
            plans.append(chunk_plan(n, color, ROWS))
    for c in range(len(saves) - len(plans)):
        plans.append(chunk_plan(n, LATE_COLORS[c % len(LATE_COLORS)], ROWS))
        loads.append(None)
    nc = len(saves)
    stages = max(len(plan) for plan in plans)
    _, bits = grid_bits(n)
    got_rows = max(sum(size for kind, _, size in plan if kind not in LANDS) for plan in plans)
    grads = (*early, *late)
    hbm = lambda k: [pl.BlockSpec(memory_space=pl.ANY)] * k
    done = pl.pallas_call(
        functools.partial(reduce_kernel, n, plans, ROWS, loads, saves, len(grads), len(shapes)),
        out_shape=(*(jax.ShapeDtypeStruct(shape, BF16) for shape in shapes), jax.ShapeDtypeStruct(tiny_shape, F32)),
        in_specs=hbm(len(grads)) + vmem(3), out_specs=tuple(hbm(len(shapes)) + vmem(1)),
        scratch_shapes=[
            pltpu.VMEM((nc, ROWS, width), BF16), pltpu.VMEM((nc, got_rows, width), BF16),
            pltpu.VMEM((nc, ROWS, width), BF16), pltpu.VMEM(tiny_shape, F32),
            pltpu.VMEM((bits + 1,) + tiny_shape, F32),
            pltpu.SemaphoreType.DMA((nc, 2)), pltpu.SemaphoreType.DMA((nc, 2)),
            pltpu.SemaphoreType.DMA((nc, stages)), pltpu.SemaphoreType.DMA((nc, stages)),
            pltpu.SemaphoreType.DMA((2, bits + 1)),
        ],
        compiler_params=pltpu.CompilerParams(collective_id=0, has_side_effects=True, vmem_limit_bytes=LIMIT),
        name="reduce_gradients",
    )(*grads, *tiny)
    return done[:-1], done[-1]


def results_kernel(count, plain, *refs):
    ins, tiny, outs = refs[:count + plain], refs[count + plain], refs[count + plain + 1:]
    for src, dst in zip(ins, outs):
        dst[...] = src[...].astype(dst.dtype)

    @pl.when(pl.program_id(0) == 0)
    def _():
        row = 0
        for place, dst in zip((0, 1, 2, 3, 4, 5, 8), outs[count + plain:]):
            width = tiny.shape[1]
            for j in range(dst.shape[0] // width):
                dst[pl.ds(j * width, width)] = tiny[place + j, :]
                row = place + j + 1
        for j, dst in enumerate(outs[count + plain + 7:]):
            at = j * dst.shape[0]
            dst[...] = tiny[row + at // tiny.shape[1], pl.ds(at % tiny.shape[1], dst.shape[0])]


def results(grads, rows, tiny, hidden, cols, steps=8):
    flat = [r.reshape(-1, r.shape[-1]) for r in rows]
    blocks = [pl.BlockSpec((a.shape[0] // steps, a.shape[1]), lambda i: (i, 0)) for a in (*grads, *flat)]
    vectors = [tiny.shape[1]] * 6 + [hidden, cols, cols]
    done = pl.pallas_call(
        functools.partial(results_kernel, len(grads), len(flat)),
        grid=(steps,),
        in_specs=blocks + [pl.BlockSpec(tiny.shape, lambda i: (0, 0))],
        out_specs=tuple(blocks + [pl.BlockSpec((v,), lambda i: (0,)) for v in vectors]),
        out_shape=tuple([jax.ShapeDtypeStruct(g.shape, F32) for g in grads]
                        + [jax.ShapeDtypeStruct(f.shape, f.dtype) for f in flat]
                        + [jax.ShapeDtypeStruct((v,), F32) for v in vectors]),
        compiler_params=pltpu.CompilerParams(vmem_limit_bytes=LIMIT),
        name="results",
    )(*grads, *flat, tiny)
    grads, flat, vectors = done[:len(grads)], done[len(grads):-len(vectors)], done[-len(vectors):]
    return grads, [f.reshape(r.shape) for f, r in zip(flat, rows)], vectors


def on_device(n_batch, inputs, prior_scores, lengths, w_query, w_key, w_value, b_query, b_value, w_output, b_output,
              gain_attn, shift_attn, w_inner, b_inner, w_outer, b_outer, gain_ffn, shift_ffn, grad_out, grad_scores):
    width = inputs.shape[2]
    vectors = (b_output, gain_attn, shift_attn, b_outer, gain_ffn, shift_ffn, b_inner)
    rows, q, k, v = project_rows(inputs, w_query, w_key, w_value, b_query, b_value)
    new_scores, context, norm = attend(lengths, q, k, v, prior_scores)
    firsts = grid_bits(n_batch)[0][:2]
    outputs, dz1, dc, keep, *gives, quarter, small, g_bi = middle(
        context, inputs, w_output, w_inner, w_outer, vectors, grad_out, firsts, ROWS)
    taken = [lax.ppermute(give, "batch", [(i, flip(i, first)) for i in range(n_batch)])
             for give, first in zip(gives, firsts)]
    grad_prior, dq, dk, dv = attend_back(lengths, q, k, v, dc, prior_scores, norm, grad_scores)
    grad_inputs, g_wq, g_wk, g_wv, g_b = project_back(rows, dq, dk, dv, w_query, w_key, w_value, dz1)
    late = (g_wq, g_wk, g_wv)
    shapes = [w_inner.shape, w_outer.shape, w_output.shape] + [g.shape for g in late]
    grads, tiny = reduce_gradients((keep, *taken, quarter), late, shapes, (small, g_bi, g_b), n_batch)
    hidden, cols = g_bi.shape[1], g_b.shape[1]
    grads, (outputs, grad_inputs), vectors = results(grads, (outputs, grad_inputs), tiny, hidden, cols)
    g_wi, g_wf, g_wo, g_wq, g_wk, g_wv = grads
    g_bo, g_g1, g_s1, g_bf, g_g2, g_s2, g_bi, g_bq, g_bv = vectors
    return (outputs, new_scores, grad_inputs, grad_prior, g_wq, g_wk, g_wv, g_bq, g_bv, g_wo,
            g_bo, g_g1, g_s1, g_wi, g_bi, g_wf, g_bf, g_g2, g_s2)


def solution(mesh):
    seq, scores, whole = P("batch", "head", None), P("batch", "head", None, None), P()
    down, across, vector = P("head", None), P(None, "head"), P("head")
    in_specs = (seq, scores, P("batch"), across, across, across, vector, vector, down, whole, whole, whole,
                across, vector, down, whole, whole, whole, seq, scores)
    out_specs = (seq, scores, seq, scores, across, across, across, vector, vector, down, whole, whole, whole,
                 across, vector, down, whole, whole, whole)
    layer = functools.partial(on_device, mesh.shape["batch"])
    return jax.shard_map(layer, mesh=mesh, in_specs=in_specs, out_specs=out_specs, check_vma=False)
```

```python
import functools
import jax, jax.numpy as jnp
from jax import lax
from jax.experimental import pallas as pl
from jax.experimental.pallas import tpu as pltpu
from jax.sharding import PartitionSpec as P

MESH = pl.DeviceIdType.MESH
F32, BF16 = jnp.float32, jnp.bfloat16
EPS = 1e-12
NEG = -1e30
LIMIT = 64 * 1000 * 1000


def dot(a, b):
    return jnp.dot(a, b, preferred_element_type=F32)


def dot_t(a, b):
    return lax.dot_general(a, b, (((1,), (1,)), ((), ())), preferred_element_type=F32)


def t_dot(a, b):
    return lax.dot_general(a, b, (((0,), (0,)), ((), ())), preferred_element_type=F32)


def meet(partner):
    barrier = pltpu.get_barrier_semaphore()
    pl.semaphore_signal(barrier, inc=1, device_id={"head": partner}, device_id_type=MESH)
    pl.semaphore_wait(barrier, 1)


def to_partner(src, dst, sems, i, partner):
    return pltpu.make_async_remote_copy(
        src_ref=src, dst_ref=dst, send_sem=sems.at[0, i], recv_sem=sems.at[1, i],
        device_id={"head": partner}, device_id_type=MESH)


def vmem(count):
    return [pl.BlockSpec(memory_space=pltpu.VMEM)] * count


def hbm(count):
    return [pl.BlockSpec(memory_space=pl.ANY)] * count


def as_row(vector):
    return vector[...].astype(F32).reshape(1, vector.shape[0])


def project_kernel(seqs, part, x, wq, wk, wv, b_query, b_value, rows, q, k, v, got, sems):
    me = lax.axis_index("head")
    other = 1 - me
    meet(other)
    for s in range(seqs):
        to_partner(x.at[s], got.at[s], sems, s, other).start()

    bias_q, bias_v = as_row(b_query), as_row(b_value)

    def emit(block, s, p):
        at = pl.ds(pl.multiple_of((2 * s + p) * part, part), part)
        rows[at, :] = block
        q[at, :] = (dot(block, wq[...]) + bias_q).astype(BF16)
        k[at, :] = dot(block, wk[...]).astype(BF16)
        v[at, :] = (dot(block, wv[...]) + bias_v).astype(BF16)

    def own(s, _):
        emit(x[s], s, me)
        return 0

    lax.fori_loop(0, seqs, own, 0)
    for s in range(seqs):
        to_partner(x.at[s], got.at[s], sems, s, other).wait()

    def theirs(s, _):
        emit(got[s], s, other)
        return 0

    lax.fori_loop(0, seqs, theirs, 0)


def project_rows(x, wq, wk, wv, b_query, b_value):
    seqs, part, width = x.shape
    total, cols = 2 * seqs * part, wq.shape[1]
    out = jax.ShapeDtypeStruct((total, cols), BF16)
    return pl.pallas_call(
        functools.partial(project_kernel, seqs, part),
        out_shape=(jax.ShapeDtypeStruct((total, width), BF16), out, out, out),
        in_specs=vmem(6), out_specs=tuple(vmem(4)),
        scratch_shapes=[pltpu.VMEM(x.shape, BF16), pltpu.SemaphoreType.DMA((2, seqs))],
        compiler_params=pltpu.CompilerParams(collective_id=1, has_side_effects=True, vmem_limit_bytes=LIMIT),
        name="project_rows",
    )(x, wq, wk, wv, b_query, b_value)


def attend_kernel(block, head, lengths, q, k, v, prior, score, c, norm):
    full = k.shape[0]
    live = lax.broadcasted_iota(jnp.int32, (1, full), 1) < lengths[pl.program_id(0)]
    first = lax.broadcasted_iota(jnp.int32, (1, 2 * head), 1) < head
    scale = head ** -0.5
    for r in range(0, full, block):
        rows = pl.ds(r, block)
        queries = q[rows, :] * jnp.asarray(scale, BF16)
        parts, norms = [], []
        for h in range(2):
            mine = jnp.where(first == (h == 0), queries, jnp.zeros_like(queries))
            scores = dot_t(mine, k[...]) + prior[0, h, rows, :].astype(F32)
            score[0, h, rows, :] = scores.astype(BF16)
            masked = jnp.where(live, scores, NEG)
            top = jnp.max(masked, axis=-1, keepdims=True)
            terms = jnp.exp(masked - top)
            total = jnp.sum(terms, axis=-1, keepdims=True)
            parts.append(dot(terms.astype(BF16), v[...]) * (1.0 / total))
            norms.append(top + jnp.log(total))
        c[rows, :] = jnp.where(first, parts[0], parts[1]).astype(BF16)
        norm[0, 0, rows, :] = jnp.where(first, norms[0], norms[1])


def attend(lengths, q, k, v, prior):
    seqs, heads, full, _ = prior.shape
    pair = q.shape[1] // heads * 2
    rows = pl.BlockSpec((full, pair), lambda s, h, n: (s, h))
    big = pl.BlockSpec((1, 2, full, full), lambda s, h, n: (s, h, 0, 0))
    norm = pl.BlockSpec((1, 1, full, pair), lambda s, h, n: (s, h, 0, 0))
    return pl.pallas_call(
        functools.partial(attend_kernel, full, pair // 2),
        grid_spec=pltpu.PrefetchScalarGridSpec(
            num_scalar_prefetch=1, grid=(seqs, heads // 2),
            in_specs=[rows, rows, rows, big], out_specs=(big, rows, norm)),
        out_shape=(jax.ShapeDtypeStruct(prior.shape, BF16), jax.ShapeDtypeStruct(q.shape, BF16),
                   jax.ShapeDtypeStruct((seqs, heads // 2, full, pair), F32)),
        compiler_params=pltpu.CompilerParams(vmem_limit_bytes=LIMIT),
        name="attend",
    )(lengths, q, k, v, prior)


def attend_back_kernel(block, head, lengths, q, k, v, dc, prior, norm, given, grad, dq, dk, dv):
    full = k.shape[0]
    live = lax.broadcasted_iota(jnp.int32, (1, full), 1) < lengths[pl.program_id(0)]
    first = lax.broadcasted_iota(jnp.int32, (1, 2 * head), 1) < head
    scale = head ** -0.5
    q_t, dc_t = q[...].T, dc[...].T
    dk_t, dv_t = [0.0, 0.0], [0.0, 0.0]
    for r in range(0, full, block):
        rows = pl.ds(r, block)
        queries, cots = q[rows, :] * jnp.asarray(scale, BF16), dc[rows, :]
        parts = []
        for h in range(2):
            mine = first == (h == 0)
            scores = dot_t(jnp.where(mine, queries, jnp.zeros_like(queries)), k[...])
            scores = scores + prior[0, h, rows, :].astype(F32)
            probs = jnp.exp(jnp.where(live, scores, NEG) - norm[0, 0, rows, h * head:h * head + 1])
            dp = dot_t(jnp.where(mine, cots, jnp.zeros_like(cots)), v[...])
            delta = jnp.sum(probs * dp, axis=-1, keepdims=True)
            ds = (probs * (dp - delta) + given[0, h, rows, :].astype(F32)).astype(BF16)
            grad[0, h, rows, :] = ds
            parts.append(dot(ds, k[...]))
            lanes = slice(h * head, (h + 1) * head)
            dk_t[h] = dk_t[h] + dot(q_t[lanes, r:r + block], ds)
            dv_t[h] = dv_t[h] + dot(dc_t[lanes, r:r + block], probs.astype(BF16))
        dq[rows, :] = (jnp.where(first, parts[0], parts[1]) * scale).astype(BF16)
    dk[...] = (jnp.concatenate(dk_t, axis=0) * scale).T.astype(BF16)
    dv[...] = jnp.concatenate(dv_t, axis=0).T.astype(BF16)


def attend_back(lengths, q, k, v, dc, prior, norm, given):
    seqs, heads, full, _ = prior.shape
    pair = q.shape[1] // heads * 2
    rows = pl.BlockSpec((full, pair), lambda s, h, n: (s, h))
    big = pl.BlockSpec((1, 2, full, full), lambda s, h, n: (s, h, 0, 0))
    norms = pl.BlockSpec((1, 1, full, pair), lambda s, h, n: (s, h, 0, 0))
    flat = jax.ShapeDtypeStruct(q.shape, BF16)
    return pl.pallas_call(
        functools.partial(attend_back_kernel, full, pair // 2),
        grid_spec=pltpu.PrefetchScalarGridSpec(
            num_scalar_prefetch=1, grid=(seqs, heads // 2),
            in_specs=[rows, rows, rows, rows, big, norms, big], out_specs=(big, rows, rows, rows)),
        out_shape=(jax.ShapeDtypeStruct(prior.shape, BF16), flat, flat, flat),
        compiler_params=pltpu.CompilerParams(vmem_limit_bytes=LIMIT),
        cost_estimate=pl.CostEstimate(flops=40 * full * full * seqs * heads * pair // 2, transcendentals=prior.size,
                                      bytes_accessed=6 * prior.size),
        name="attend_back",
    )(lengths, q, k, v, dc, prior, norm, given)


def fold(value):
    return jnp.sum(value.reshape(value.shape[0] // 8, 8, value.shape[1]), axis=0)


def norm_stats(z):
    mean = jnp.mean(z, axis=-1, keepdims=True)
    centred = z - mean
    r = lax.rsqrt(jnp.mean(centred * centred, axis=-1, keepdims=True) + EPS)
    return centred * r, r


def norm_back(cot, gain, unit, r):
    e = cot * gain
    return r * (e - jnp.mean(e, axis=-1, keepdims=True) - unit * jnp.mean(e * unit, axis=-1, keepdims=True))


def middle_kernel(seqs, part, firsts, c, x, wo, wi_far, wf_far, b_output, gain1, shift1, b_outer, gain2, shift2, b_inner, gout_far,
                  out_far, dz1_far, dc, keep, give_x, give_y, quarter, small, g_bi,
                  unit1, r1, hn, act, slope, df, du, da, give, got, own, sums, bsum, bi, keep_f, give_f, taken, wi, wf, gout, out, dz1, sems, far_sems, own_sems):
    me = lax.axis_index("head")
    other = 1 - me
    width = x.shape[2]
    hidden = wi.shape[1]
    tile = 512
    sub = 64
    fetch_wi, fetch_wf, fetch_gout, store_out, store_dz1 = [
        pltpu.make_async_copy(src, dst, own_sems.at[i]) for i, (src, dst) in enumerate(
            ((wi_far, wi), (wf_far, wf), (gout_far, gout), (out, out_far), (dz1, dz1_far)))]
    fetch_wi.start()
    fetch_wf.start()
    fetch_gout.start()
    barrier = pltpu.get_barrier_semaphore()
    pl.semaphore_signal(barrier, inc=1, device_id={"head": other}, device_id_type=MESH)
    for first in firsts:
        pl.semaphore_signal(barrier, inc=1, device_id={"batch": flip(lax.axis_index("batch"), first)},
                            device_id_type=MESH)
    pl.semaphore_wait(barrier, 3)
    b_output, gain1, shift1, b_outer, gain2, shift2 = map(as_row, (b_output, gain1, shift1, b_outer, gain2, shift2))
    sums[...] = jnp.zeros_like(sums)
    bsum[...] = jnp.zeros_like(bsum)
    bi[...] = as_row(b_inner)

    def rows_of(s, p):
        return pl.ds(pl.multiple_of((2 * s + p) * part, part), part)

    def at(start, size):
        return pl.ds(pl.multiple_of(start, size), size)

    def attn_part(s, _):
        give[s] = dot(c[rows_of(s, other), :], wo[...]).astype(BF16)
        return 0
    for s in range(seqs):
        attn_part(s, 0)
        to_partner(give.at[s], got.at[0, s], sems, s, other).start()

    def attn_own(s, _):
        own[s] = dot(c[rows_of(s, me), :], wo[...]).astype(BF16)
        return 0
    lax.fori_loop(0, seqs, attn_own, 0)
    for s in range(seqs):
        to_partner(give.at[s], got.at[0, s], sems, s, other).wait()

        def first_norm(i, _):
            rows = at(i * sub, sub)
            z = x[s, rows, :].astype(F32) + (own[s, rows, :].astype(F32) + got[0, s, rows, :].astype(F32)) + b_output
            unit, r = norm_stats(z)
            unit1[s, rows, :] = unit
            r1[s, rows, :] = jnp.broadcast_to(r, (sub, 128))
            hn[at((2 * s + me) * part + i * sub, sub), :] = (unit * gain1 + shift1).astype(BF16)
            return 0
        lax.fori_loop(0, part // sub, first_norm, 0)
        block = hn.at[rows_of(s, me)]
        to_partner(block, block, sems, seqs + s, other).start()

    order = [(0, me)] + [(s, other) for s in range(seqs)] + [(s, me) for s in range(1, seqs)]

    def inner(s, p):
        rows = rows_of(s, p)

        def columns(j, _):
            cols = at(j * tile, tile)
            u = dot(hn[rows, :], wi[:, cols]) + bi[:, cols]
            cdf = 0.5 * (1.0 + lax.erf(u * 0.7071067811865476))
            act[rows, cols] = (u * cdf).astype(BF16)
            slope[rows, cols] = cdf + u * (jnp.exp(-0.5 * u * u) * 0.3989422804014327)
            return 0
        lax.fori_loop(0, hidden // tile, columns, 0)

    def outer(s, p, place):
        rows = rows_of(s, p)

        def columns(j, _):
            cols = at(j * tile, tile)
            place[s, :, cols] = dot(act[rows, :], wf[:, cols]).astype(BF16)
            return 0
        lax.fori_loop(0, width // tile, columns, 0)

    for n, (s, p) in enumerate(order):
        if n == 1:
            for q in range(seqs):
                block = hn.at[rows_of(q, me)]
                to_partner(block, block, sems, seqs + q, other).wait()
        if n == 0:
            fetch_wi.wait()
        inner(s, p)
        if n == 0:
            fetch_wf.wait()
        if p is other:
            outer(s, p, give.at[pl.ds(seqs, seqs)])
            to_partner(give.at[seqs + s], got.at[1, s], sems, 2 * seqs + s, other).start()
        else:
            outer(s, p, own)

    fetch_gout.wait()
    for s in range(seqs):
        to_partner(give.at[seqs + s], got.at[1, s], sems, 2 * seqs + s, other).wait()

        def second_norm(i, _):
            rows = at(i * sub, sub)
            h = unit1[s, rows, :] * gain1 + shift1
            z = (own[s, rows, :].astype(F32) + got[1, s, rows, :].astype(F32)) + b_outer + h
            unit, r = norm_stats(z)
            out[s, rows, :] = (unit * gain2 + shift2).astype(BF16)
            g = gout[s, rows, :].astype(F32)
            d = norm_back(g, gain2, unit, r)
            dz1[s, rows, :] = d
            df[at((2 * s + me) * part + i * sub, sub), :] = d.astype(BF16)
            sums[3] += fold(d)
            sums[4] += fold(g * unit)
            sums[5] += fold(g)
            return 0
        lax.fori_loop(0, part // sub, second_norm, 0)
        block = df.at[rows_of(s, me)]
        to_partner(block, block, sems, 3 * seqs + s, other).start()

    store_out.start()

    mine = lax.axis_index("batch")
    gives = (give_x, give_y)
    half = keep.shape[1]
    per = hidden // width
    side = give_f.shape[0] // 2
    edge = give_x.shape[0] - side - side // 2

    def put(value, kept, axis, given):
        bit = (mine // (1 << firsts[axis])) % 2
        size = value.shape[0] // 2

        @pl.when(bit == 0)
        def _():
            kept[...] = value[:size].astype(BF16)
            given[...] = value[size:].astype(BF16)

        @pl.when(bit == 1)
        def _():
            kept[...] = value[size:].astype(BF16)
            given[...] = value[:size].astype(BF16)

    def far_copy(i, axis):
        return pltpu.make_async_remote_copy(
            src_ref=give_f.at[i], dst_ref=taken.at[i], send_sem=far_sems.at[0, i], recv_sem=far_sems.at[1, i],
            device_id={"batch": flip(mine, firsts[axis])}, device_id_type=MESH)

    def grads_outer():
        def give_outer(i, _):
            for axis in range(2):
                chunk = axis * side + i
                put(t_dot(act[:, at(chunk * 2 * half, 2 * half)], df[...]), keep_f.at[chunk], axis, give_f.at[chunk])
                far_copy(chunk, axis).start()
            return 0
        lax.fori_loop(0, side, give_outer, 0)

    def inner_back(s, p):
        rows = rows_of(s, p)

        def columns(j, _):
            cols = at(j * tile, tile)
            dg = dot_t(df[rows, :], wf[cols, :]).astype(BF16).astype(F32)
            low = (dg * slope[rows, cols]).astype(BF16)
            du[rows, cols] = low
            bsum[:, cols] += fold(low.astype(F32))
            return 0
        lax.fori_loop(0, hidden // tile, columns, 0)

    def outer_back(s, p, place):
        rows = rows_of(s, p)

        def columns(j, _):
            cols = at(j * tile, tile)
            place[s, :, cols] = dot_t(du[rows, :], wi[cols, :]).astype(BF16)
            return 0
        lax.fori_loop(0, width // tile, columns, 0)

    for n, (s, p) in enumerate(order):
        if n == 1:
            for q in range(seqs):
                block = df.at[rows_of(q, me)]
                to_partner(block, block, sems, 3 * seqs + q, other).wait()
            grads_outer()
        inner_back(s, p)
        if p is other:
            outer_back(s, p, give.at[pl.ds(2 * seqs, seqs)])
            to_partner(give.at[2 * seqs + s], got.at[2, s], sems, 4 * seqs + s, other).start()
        else:
            outer_back(s, p, own)

    for s in range(seqs):
        to_partner(give.at[2 * seqs + s], got.at[2, s], sems, 4 * seqs + s, other).wait()

        def first_back(i, _):
            rows = at(i * sub, sub)
            cot = dz1[s, rows, :] + (own[s, rows, :].astype(F32) + got[2, s, rows, :].astype(F32))
            unit = unit1[s, rows, :]
            d = norm_back(cot, gain1, unit, r1[s, rows, 0:1])
            dz1[s, rows, :] = d
            da[at((2 * s + me) * part + i * sub, sub), :] = d.astype(BF16)
            sums[0] += fold(d)
            sums[1] += fold(cot * unit)
            sums[2] += fold(cot)
            return 0
        lax.fori_loop(0, part // sub, first_back, 0)
        block = da.at[rows_of(s, me)]
        to_partner(block, block, sems, 5 * seqs + s, other).start()

    store_dz1.start()
    for axis in range(2):
        def give_inner(i, _, axis=axis):
            at_hn, at_du = at((axis * side + i) // per * 2 * half, 2 * half), at((axis * side + i) % per * width, width)
            put(t_dot(hn[:, at_hn], du[:, at_du]), keep.at[axis * side + i], axis, gives[axis].at[i])
            return 0
        lax.fori_loop(0, side, give_inner, 0)

    for s in range(seqs):
        block = da.at[rows_of(s, me)]
        to_partner(block, block, sems, 5 * seqs + s, other).wait()
    dc[...] = dot_t(da[...], wo[...]).astype(BF16)
    for axis in range(2):
        def give_output(i, _, axis=axis):
            cols = at((axis * edge + i) * 2 * half, 2 * half)
            put(t_dot(c[:, cols], da[...]), keep.at[2 * side + axis * edge + i], axis, gives[axis].at[side + i])
            return 0
        lax.fori_loop(0, edge, give_output, 0)
    small[...] = jnp.sum(sums[...], axis=1)
    g_bi[...] = jnp.sum(bsum[...], axis=0, keepdims=True)
    for axis in range(2):
        def far_done(i, _, axis=axis):
            chunk = axis * side + i
            far_copy(chunk, axis).wait()
            place = gives[1 - axis].at[side + edge + i // 2, at(i % 2 * (half // 2), half // 2)]
            put(keep_f[chunk].astype(F32) + taken[chunk].astype(F32), quarter.at[chunk], 1 - axis, place)
            return 0
        lax.fori_loop(0, side, far_done, 0)
    store_out.wait()
    store_dz1.wait()


def middle(c, x, wo, wi, wf, vectors, gout, firsts, rows):
    seqs, part, width = x.shape
    total, cols = c.shape
    hidden = wi.shape[1]
    sds = jax.ShapeDtypeStruct
    side, edge = hidden // rows // 2, cols // rows // 2
    halves = [sds((count, rows // 2, width), BF16)
              for count in (2 * side + 2 * edge, side + edge + side // 2, side + edge + side // 2)]
    halves.append(sds((2 * side, rows // 4, width), BF16))
    return pl.pallas_call(
        functools.partial(middle_kernel, seqs, part, firsts),
        out_shape=(sds(x.shape, BF16), sds(x.shape, F32), sds(c.shape, BF16),
                   *halves, sds((6, width), F32), sds((1, hidden), F32)),
        in_specs=vmem(3) + hbm(2) + vmem(len(vectors)) + hbm(1), out_specs=tuple(hbm(2) + vmem(7)),
        scratch_shapes=[
            pltpu.VMEM(x.shape, F32), pltpu.VMEM((seqs, part, 128), F32),
            pltpu.VMEM((total, width), BF16), pltpu.VMEM((total, hidden), BF16), pltpu.VMEM((total, hidden), F32),
            pltpu.VMEM((total, width), BF16), pltpu.VMEM((total, hidden), BF16), pltpu.VMEM((total, width), BF16),
            pltpu.VMEM((3 * seqs, part, width), BF16), pltpu.VMEM((3, seqs, part, width), BF16),
            pltpu.VMEM(x.shape, BF16), pltpu.VMEM((6, 8, width), F32), pltpu.VMEM((8, hidden), F32),
            pltpu.VMEM((1, hidden), F32),
            *[pltpu.VMEM((2 * side, rows // 2, width), BF16)] * 3,
            pltpu.VMEM(wi.shape, BF16), pltpu.VMEM(wf.shape, BF16), pltpu.VMEM(x.shape, BF16),
            pltpu.VMEM(x.shape, BF16), pltpu.VMEM(x.shape, F32),
            pltpu.SemaphoreType.DMA((2, 6 * seqs)), pltpu.SemaphoreType.DMA((2, 2 * side)), pltpu.SemaphoreType.DMA((5,)),
        ],
        compiler_params=pltpu.CompilerParams(collective_id=2, has_side_effects=True, vmem_limit_bytes=66 * 1000 * 1000),
        cost_estimate=pl.CostEstimate(flops=14 * total * width * hidden, transcendentals=total * hidden,
                                      bytes_accessed=30 << 20),
        name="middle",
    )(c, x, wo, wi, wf, *vectors, gout)


def project_back_kernel(seqs, part, rows, dq, dk, dv, wq, wk, wv, dz1,
                        gin, g_q, g_k, g_v, g_b, give, got, sems):
    me = lax.axis_index("head")
    other = 1 - me
    meet(other)

    def total_of(s, p):
        at = pl.ds(pl.multiple_of((2 * s + p) * part, part), part)
        return dot_t(dq[at, :], wq[...]) + dot_t(dk[at, :], wk[...]) + dot_t(dv[at, :], wv[...])

    for s in range(seqs):
        give[s] = total_of(s, other).astype(BF16)
        to_partner(give.at[s], got.at[s], sems, s, other).start()
    g_q[...] = t_dot(rows[...], dq[...]).astype(BF16)
    g_k[...] = t_dot(rows[...], dk[...]).astype(BF16)
    g_v[...] = t_dot(rows[...], dv[...]).astype(BF16)
    g_b[0:1, :] = jnp.sum(fold(dq[...].astype(F32)), axis=0, keepdims=True)
    g_b[1:2, :] = jnp.sum(fold(dv[...].astype(F32)), axis=0, keepdims=True)
    for s in range(seqs):
        own = total_of(s, me).astype(BF16)
        to_partner(give.at[s], got.at[s], sems, s, other).wait()
        gin[s] = (dz1[s] + (own.astype(F32) + got[s].astype(F32))).astype(BF16)


def project_back(rows, dq, dk, dv, wq, wk, wv, dz1):
    seqs, part, width = dz1.shape
    sds = jax.ShapeDtypeStruct
    grad = sds(wq.shape, BF16)
    return pl.pallas_call(
        functools.partial(project_back_kernel, seqs, part),
        out_shape=(sds(dz1.shape, BF16), grad, grad, grad, sds((2, wq.shape[1]), F32)),
        in_specs=vmem(8), out_specs=tuple(vmem(5)),
        scratch_shapes=[pltpu.VMEM(dz1.shape, BF16), pltpu.VMEM(dz1.shape, BF16), pltpu.SemaphoreType.DMA((2, seqs))],
        compiler_params=pltpu.CompilerParams(collective_id=3, has_side_effects=True, vmem_limit_bytes=LIMIT),
        cost_estimate=pl.CostEstimate(flops=12 * rows.size * wq.shape[1], transcendentals=0, bytes_accessed=16 << 20),
        name="project_back",
    )(rows, dq, dk, dv, wq, wk, wv, dz1)
LINE = 16
ROWS = 256
LATE_COLORS = (2, 3, 0, 1, 2, 0)
LAG = 0.16
PRECEDENCE = (22, 6, 15, 2, 35, 0, 7, 26, 35, 20, 25, 7, 20, 21, 9, 24, 29, 3, 10, 29, 34, 14, 14, 6)
LANDS = ("gather", "out", "back_in", "back_mid", "back_out")


def grid_bits(n):
    bits = n.bit_length() - 1
    side = bits // 3
    return (0, side, 2 * side), bits


def chunk_plan(n, color, rows):
    (bx, by, bz), bits = grid_bits(n)
    order = (by, bx) if color % 2 else (bx, by)
    line = n == LINE
    plan, length = [], rows
    if line and color >= 2:
        plan = [("far_in", bz, 3 * rows // 4), ("far_mid", bz, rows // 2), ("far_out", bz, rows // 4)]
        length = rows // 4
    if not line:
        order = (*order, bz)
    for b in order:
        length //= 2
        plan.append(("scatter", b, length))
    if line and color < 2:
        plan += [(kind, bz, length) for kind in ("in", "mid", "out")]
    plan += [("double", b, length) for b in range(bits) if not line and b not in order]
    for b in reversed(order):
        plan.append(("gather", b, length))
        length *= 2
    if line and color >= 2:
        plan += [("back_in", bz, rows // 4), ("back_mid", bz, rows // 2), ("back_out", bz, 3 * rows // 4)]
    return plan


def event_order(n, plans, rows):
    first, _ = grid_bits(n)

    def path(kind, b):
        place = kind.split("_")[-1]
        if place in ("in", "mid", "out"):
            return ("in", "mid", "out").index(place) + 2
        return (b >= first[1]) + (b >= first[2])

    work = [[(path(kind, b), size / rows) for kind, b, size in plan] for plan in plans]
    free, ready, step, events = [0.0] * 5, [0.0] * len(plans), [0] * len(plans), []
    for _ in range(sum(map(len, work))):
        start, _, c = min((max(ready[c], free[row[step[c]][0]]), -PRECEDENCE[c % len(PRECEDENCE)], c)
                          for c, row in enumerate(work) if step[c] < len(row))
        link, span = work[c][step[c]]
        free[link] = start + span
        ready[c] = free[link] + LAG
        events.append((start, c, step[c]))
        step[c] += 1
    events += [(r, c, len(work[c])) for c, r in enumerate(ready)]
    return [(c, s) for _, c, s in sorted(events)]


def flip(index, bit):
    return index + (1 - 2 * ((index // (1 << bit)) % 2)) * (1 << bit)


def chunk_pieces(shapes, rows, width):
    chunks = []
    for i, (height, cols) in enumerate(shapes):
        per = max(1, width // cols)
        for r in range(0, height, rows * per):
            for col in range(0, cols, width):
                span = min(cols, width)
                chunks.append([(i, r + j * rows, col, span, j * span) for j in range(per)])
    return chunks


def only(cond, body):
    if cond is None:
        body()
    else:
        pl.when(cond)(body)


def reduce_kernel(n, plans, rows, loads, saves, count, results, *refs):
    grads, (small, g_bi, g_b) = refs[:count], refs[count:count + 3]
    refs = refs[count + 3:]
    sums, tiny_out = refs[:results], refs[results]
    work, got, full, hold, tiny_got, load_sem, save_sem, send_sem, recv_sem, tiny_sem = refs[results + 1:]
    nc = len(plans)
    me, head = lax.axis_index("batch"), lax.axis_index("head")
    first, bits = grid_bits(n)
    done = [0 if load is None else load[0] for load in loads]
    bit_of = [(me // (1 << b)) % 2 for b in range(bits)]
    z = me // (1 << first[2])
    side = z // 2
    end = z % 3 == 0
    middle = z % 3 != 0
    mirror = me + (3 - 2 * z) * (1 << first[2])

    spans = []
    for plan in plans:
        off, length, at, row = 0, rows, 0, []
        quarter = rows // 4
        for kind, b, size in plan:
            where = None if kind in LANDS else at
            at += 0 if kind in LANDS else size
            if kind == "scatter":
                row.append((off + bit_of[b] * size, off + (1 - bit_of[b]) * size, size, where))
                off = row[-1][0]
            elif kind == "gather":
                row.append((off, off, size, where))
                off = off - bit_of[b] * size
            elif kind in ("far_in", "back_out"):
                row.append(((1 - side) * quarter, (1 - side) * quarter, size, where))
            elif kind == "far_mid":
                row.append((side * 2 * quarter, (1 - side) * 2 * quarter, size, where))
            elif kind == "back_mid":
                row.append((side * 2 * quarter, side * 2 * quarter, size, where))
            elif kind in ("far_out", "back_in"):
                row.append((side * 3 * quarter, side * 3 * quarter, size, where))
                off = z * quarter
            else:
                row.append((off, off, size, where))
        spans.append(row)

    def roles(kind):
        place = kind.split("_")[-1]
        return {"in": (end, middle), "mid": (middle, middle), "out": (middle, end)}.get(place, (None, None))

    def moves(c, out):
        if out:
            for k, (i, r, col, span, at) in enumerate(saves[c]):
                outside = sums[i].at[pl.ds(r, rows), pl.ds(col, span)]
                yield pltpu.make_async_copy(full.at[c, :, pl.ds(at, span)], outside, save_sem.at[c, k])
        elif loads[c] is None:
            for k, (i, r, col, span, at) in enumerate(saves[c]):
                outside = grads[i + count - results].at[pl.ds(r, rows), pl.ds(col, span)]
                yield pltpu.make_async_copy(outside, work.at[c, :, pl.ds(at, span)], load_sem.at[c, k])
        else:
            _, kept, kept_at, given, given_at, given_row = loads[c]
            keep, _, length, at = spans[c][done[c] - 1]
            inside = work.at[c, pl.ds(pl.multiple_of(keep, 16), length)]
            yield pltpu.make_async_copy(grads[kept].at[kept_at], inside, load_sem.at[c, 0])
            outside = grads[given].at[given_at, pl.ds(given_row, length)]
            yield pltpu.make_async_copy(outside, got.at[c, pl.ds(at, length)], load_sem.at[c, 1])

    events = [(c, s + done[c]) for c, s in event_order(n, [p[d:] for p, d in zip(plans, done)], rows)]
    for c, s in events:
        if s == done[c]:
            for move in moves(c, False):
                move.start()
    hold[...] = jnp.zeros_like(hold)
    hold[0:6, :] = small[...]
    width, row = hold.shape[1], 8
    for j in range(g_bi.shape[1] // width):
        hold[row:row + 1, :] = g_bi[:, j * width:(j + 1) * width]
        row += 1
    cols = g_b.shape[1]
    for j in range(2):
        hold[row + j * cols // width:row + j * cols // width + 1, pl.ds(j * cols % width, cols)] = g_b[j:j + 1, :]
    barrier = pltpu.get_barrier_semaphore()
    friends = [flip(me, b) for b in range(bits)] + ([mirror] if n == LINE else [])
    for friend in friends:
        pl.semaphore_signal(barrier, inc=1, device_id={"batch": friend}, device_id_type=MESH)
    pl.semaphore_signal(barrier, inc=1, device_id={"head": 1 - head}, device_id_type=MESH)
    pl.semaphore_wait(barrier, len(friends) + 1)

    def copy_of(c, s):
        kind, b, _ = plans[c][s]
        _, start, length, at = spans[c][s]
        place = (c, pl.ds(pl.multiple_of(start, 16), length))
        src = full.at[place] if kind in LANDS else work.at[place]
        dst = full.at[place] if kind in LANDS else got.at[c, pl.ds(at, length)]
        return pltpu.make_async_remote_copy(
            src_ref=src, dst_ref=dst, send_sem=send_sem.at[c, s], recv_sem=recv_sem.at[c, s],
            device_id={"batch": mirror if kind.endswith("mid") else flip(me, b)}, device_id_type=MESH)

    def finish(c, s):
        kind = plans[c][s][0]
        keep, _, length, at = spans[c][s]
        sender, receiver = roles(kind)
        if s == done[c] - 1:
            for move in moves(c, False):
                move.wait()
        else:
            only(sender, lambda: copy_of(c, s).wait_send())

        def take():
            if s != done[c] - 1:
                copy_of(c, s).wait_recv()
            if kind in LANDS:
                return
            target = full if plans[c][s + 1][0] in LANDS else work

            def add(i, _):
                here = pl.ds(pl.multiple_of(keep + i * 16, 16), 16)
                there = pl.ds(pl.multiple_of(at + i * 16, 16), 16)
                target[c, here, :] = (work[c, here, :].astype(F32) + got[c, there, :].astype(F32)).astype(BF16)
                return 0
            lax.fori_loop(0, length // 16, add, 0)
        only(receiver, take)

    def tiny_copy(k):
        rest = hold.at[pl.ds(0, 8)] if k == 0 else hold
        there = tiny_got.at[k, pl.ds(0, 8)] if k == 0 else tiny_got.at[k]
        target = {"head": 1 - head} if k == 0 else {"batch": flip(me, k - 1)}
        return pltpu.make_async_remote_copy(
            src_ref=rest, dst_ref=there, send_sem=tiny_sem.at[0, k], recv_sem=tiny_sem.at[1, k],
            device_id=target, device_id_type=MESH)

    def tiny_finish(k):
        tiny_copy(k).wait()
        if k == 0:
            hold[0:8, :] += tiny_got[0, 0:8, :]
        else:
            hold[...] += tiny_got[k]

    gap = len(events) // (bits + 2)
    for e, (c, s) in enumerate(events):
        if s == 0:
            for move in moves(c, False):
                move.wait()
        else:
            finish(c, s - 1)
        if s == len(plans[c]):
            for move in moves(c, True):
                move.start()
        else:
            only(roles(plans[c][s][0])[0], lambda: copy_of(c, s).start())
        if e % gap == 0 and e // gap <= bits:
            k = e // gap
            if k > 0:
                tiny_finish(k - 1)
            tiny_copy(k).start()
    tiny_finish(bits)
    tiny_out[...] = hold[...]
    for c in range(nc):
        for move in moves(c, True):
            move.wait()


def reduce_gradients(early, late, shapes, tiny, n):
    width = tiny[0].shape[1]
    tiny_shape = (16, width)
    saves = chunk_pieces(shapes, ROWS, width)
    outer = early[3].shape[0]
    edge = early[0].shape[0] - outer
    side = (outer + edge) // 2
    plans, loads = [], []
    for which, count in enumerate((outer, outer, edge)):
        for c in range(count):
            color, slot = c * 2 // count, c % (count // 2)
            if which == 1:
                loads.append((2, 3, c, 2 - color, side + slot // 2, slot % 2 * (ROWS // 4)))
            else:
                base = outer if which == 2 else 0
                loads.append((1, 0, base + c, 1 + color, base // 2 + slot, 0))
            plans.append(chunk_plan(n, color, ROWS))
    for c in range(len(saves) - len(plans)):
        plans.append(chunk_plan(n, LATE_COLORS[c % len(LATE_COLORS)], ROWS))
        loads.append(None)
    nc = len(saves)
    stages = max(len(plan) for plan in plans)
    _, bits = grid_bits(n)
    got_rows = max(sum(size for kind, _, size in plan if kind not in LANDS) for plan in plans)
    grads = (*early, *late)
    done = pl.pallas_call(
        functools.partial(reduce_kernel, n, plans, ROWS, loads, saves, len(grads), len(shapes)),
        out_shape=(*(jax.ShapeDtypeStruct(shape, BF16) for shape in shapes), jax.ShapeDtypeStruct(tiny_shape, F32)),
        in_specs=hbm(len(grads)) + vmem(3), out_specs=tuple(hbm(len(shapes)) + vmem(1)),
        scratch_shapes=[
            pltpu.VMEM((nc, ROWS, width), BF16), pltpu.VMEM((nc, got_rows, width), BF16),
            pltpu.VMEM((nc, ROWS, width), BF16), pltpu.VMEM(tiny_shape, F32),
            pltpu.VMEM((bits + 1,) + tiny_shape, F32),
            pltpu.SemaphoreType.DMA((nc, 2)), pltpu.SemaphoreType.DMA((nc, 2)),
            pltpu.SemaphoreType.DMA((nc, stages)), pltpu.SemaphoreType.DMA((nc, stages)),
            pltpu.SemaphoreType.DMA((2, bits + 1)),
        ],
        compiler_params=pltpu.CompilerParams(collective_id=0, has_side_effects=True, vmem_limit_bytes=LIMIT),
        name="reduce_gradients",
    )(*grads, *tiny)
    return done[:-1], done[-1]


def results_kernel(count, plain, *refs):
    ins, tiny, outs = refs[:count + plain], refs[count + plain], refs[count + plain + 1:]
    for src, dst in zip(ins, outs):
        dst[...] = src[...].astype(dst.dtype)

    @pl.when(pl.program_id(0) == 0)
    def _():
        row = 0
        for place, dst in zip((0, 1, 2, 3, 4, 5, 8), outs[count + plain:]):
            width = tiny.shape[1]
            for j in range(dst.shape[0] // width):
                dst[pl.ds(j * width, width)] = tiny[place + j, :]
                row = place + j + 1
        for j, dst in enumerate(outs[count + plain + 7:]):
            at = j * dst.shape[0]
            dst[...] = tiny[row + at // tiny.shape[1], pl.ds(at % tiny.shape[1], dst.shape[0])]


def results(grads, rows, tiny, hidden, cols, steps=4):
    flat = [r.reshape(-1, r.shape[-1]) for r in rows]
    blocks = [pl.BlockSpec((a.shape[0] // steps, a.shape[1]), lambda i: (i, 0)) for a in (*grads, *flat)]
    vectors = [tiny.shape[1]] * 6 + [hidden, cols, cols]
    done = pl.pallas_call(
        functools.partial(results_kernel, len(grads), len(flat)),
        grid=(steps,),
        in_specs=blocks + [pl.BlockSpec(tiny.shape, lambda i: (0, 0))],
        out_specs=tuple(blocks + [pl.BlockSpec((v,), lambda i: (0,)) for v in vectors]),
        out_shape=tuple([jax.ShapeDtypeStruct(g.shape, F32) for g in grads]
                        + [jax.ShapeDtypeStruct(f.shape, f.dtype) for f in flat]
                        + [jax.ShapeDtypeStruct((v,), F32) for v in vectors]),
        compiler_params=pltpu.CompilerParams(vmem_limit_bytes=LIMIT),
        name="results",
    )(*grads, *flat, tiny)
    grads, flat, vectors = done[:len(grads)], done[len(grads):-len(vectors)], done[-len(vectors):]
    return grads, [f.reshape(r.shape) for f, r in zip(flat, rows)], vectors


def on_device(n_batch, inputs, prior_scores, lengths, w_query, w_key, w_value, b_query, b_value, w_output, b_output,
              gain_attn, shift_attn, w_inner, b_inner, w_outer, b_outer, gain_ffn, shift_ffn, grad_out, grad_scores):
    width = inputs.shape[2]
    vectors = (b_output, gain_attn, shift_attn, b_outer, gain_ffn, shift_ffn, b_inner)
    rows, q, k, v = project_rows(inputs, w_query, w_key, w_value, b_query, b_value)
    new_scores, context, norm = attend(lengths, q, k, v, prior_scores)
    firsts = grid_bits(n_batch)[0][:2]
    outputs, dz1, dc, keep, *gives, quarter, small, g_bi = middle(
        context, inputs, w_output, w_inner, w_outer, vectors, grad_out, firsts, ROWS)
    taken = [lax.ppermute(give, "batch", [(i, flip(i, first)) for i in range(n_batch)])
             for give, first in zip(gives, firsts)]
    grad_prior, dq, dk, dv = attend_back(lengths, q, k, v, dc, prior_scores, norm, grad_scores)
    grad_inputs, g_wq, g_wk, g_wv, g_b = project_back(rows, dq, dk, dv, w_query, w_key, w_value, dz1)
    late = (g_wq, g_wk, g_wv)
    shapes = [w_inner.shape, w_outer.shape, w_output.shape] + [g.shape for g in late]
    grads, tiny = reduce_gradients((keep, *taken, quarter), late, shapes, (small, g_bi, g_b), n_batch)
    hidden, cols = g_bi.shape[1], g_b.shape[1]
    grads, (outputs, grad_inputs), vectors = results(grads, (outputs, grad_inputs), tiny, hidden, cols)
    g_wi, g_wf, g_wo, g_wq, g_wk, g_wv = grads
    g_bo, g_g1, g_s1, g_bf, g_g2, g_s2, g_bi, g_bq, g_bv = vectors
    return (outputs, new_scores, grad_inputs, grad_prior, g_wq, g_wk, g_wv, g_bq, g_bv, g_wo,
            g_bo, g_g1, g_s1, g_wi, g_bi, g_wf, g_bf, g_g2, g_s2)


def solution(mesh):
    seq, scores, whole = P("batch", "head", None), P("batch", "head", None, None), P()
    down, across, vector = P("head", None), P(None, "head"), P("head")
    in_specs = (seq, scores, P("batch"), across, across, across, vector, vector, down, whole, whole, whole,
                across, vector, down, whole, whole, whole, seq, scores)
    out_specs = (seq, scores, seq, scores, across, across, across, vector, vector, down, whole, whole, whole,
                 across, vector, down, whole, whole, whole)
    layer = functools.partial(on_device, mesh.shape["batch"])
    return jax.shard_map(layer, mesh=mesh, in_specs=in_specs, out_specs=out_specs, check_vma=False)
```
